32 devices in a mesh: replica: 8 (over z, x), brick: 4 (over y, core).
Axes of the slice: x: 2, y: 2, z: 4, core: 2. Of those that a mesh axis runs over, the one named last changes fastest.
Arguments:
- atom_locations: float32 [8, 3, 3072], P('replica', None, 'brick'), may hold values from 0 to 128, as said below
- atom_speeds_vector: float32 [8, 3, 3072], P('replica', None, 'brick'), may hold values from -7 to 7
- inertial_amounts: float32 [3072], P('brick'), may hold values from 1 to 4
- electric_loads: float32 [3072], P('brick'), may hold values from -4 to 4
- scatter_strengths: float32 [3072], P('brick'), may hold values from 0.5 to 2
- gaussian_spreads_sigma: float32 [3072], P('brick'), may hold values from 0.7 to 1.4
- atom_present_flags: int32 [3072], P('brick'), may hold values 0 or 1
- observed_volume_values: float32 [40, 128, 128], P('brick'), may hold values from 0 to 2
- voxel_reciprocal_spread: float32 [40, 128, 128], P('brick'), may hold values from 0.5 to 4
- paired_partner_lists: int32 [24, 14], P('brick'), may hold values from 0 to 9
- cell_usage_tally: int32 [24], P('brick'), may hold values from 1 to 14, as said below
- halo_sender_spots: int32 [2, 1024], P(None, 'brick'), may hold values from 0 to 767
- target_warmth_levels: int32 [8], P('replica'), may hold values from 280 to 399
Outputs:
- new_positions: float32 [8, 3, 3072], P('replica', None, 'brick')
- new_velocities: float32 [8, 3, 3072], P('replica', None, 'brick')
- deviation: float32 [40, 128, 128], P('brick', 'replica')
The draws below stay inside these ranges and needn't reach their ends.
Inputs may be any that keep to these rules, and one draw needn't show every extreme that they name: `atom_locations`: atoms in the slots of brick b have x in [b * 10, (b + 1) * 10), y in [0, 128), z in [0, 128). Only the first cell_usage_tally[c] slots of cell c count; some cell uses all 14 slots.
All inputs are finite; a program needn't handle non-finite values. No bound on the sum of `atom_present_flags` on one device may be relied on, other than what follows from the above.
Results may differ from the reference program's by a relative error of at most 0.00062.
Values may be sent and summed in bfloat16 or wider, within the bound.
No kernel may reach another device: no remote copies, remote signals or barrier semaphores. Data moves between devices by JAX's collectives and lax.ppermute only.
A program may use at most 64 MiB of HBM per device.

```python
import math
import jax
import jax.numpy as jnp
from jax import lax

SX = 10
GY = 128
GZ = 128
ATOM_DEV = 768
HALO = 2
CELL = 128
NBR = 14
CELLS = 6
GHOST = 256
BLOCKS = 10
REPLICA_MEMBERS = 8
NX = 40
ATOMS = 3072
N_BRICK = 4


def brick_of(count):
    return (jnp.arange(count, dtype=jnp.int32) // ATOM_DEV).astype(jnp.float32)


def draw_atom_locations(key, part):
    keys = jax.random.split(jax.random.fold_in(key, 11), 1)
    frac = jax.random.uniform(keys[0], (REPLICA_MEMBERS, 3, ATOMS), jnp.float32)
    xpart = (brick_of(ATOMS)[None, :] + frac[:, 0]) * SX
    ypart = frac[:, 1] * GY
    zpart = frac[:, 2] * GZ
    return jnp.stack([xpart, ypart, zpart], axis=1)


def draw_atom_speeds_vector(key, part):
    slabs = ATOMS // ATOM_DEV
    ramp = brick_of(ATOMS) / max(slabs - 1, 1)
    inner = jax.random.fold_in(key, 23)
    base = jnp.clip(jax.random.normal(inner, (REPLICA_MEMBERS, 3, ATOMS), jnp.float32), -4.0, 4.0)
    spread_scale = 1.0 + 0.732 * ramp
    return base * spread_scale[None, None, :]


def draw_cell_usage_tally(key, part):
    keys = jax.random.split(jax.random.fold_in(key, 37), 4)
    slabs = ATOMS // ATOM_DEV
    cells = ATOM_DEV // CELL
    ceiling = jax.random.randint(keys[0], (slabs,), 2, NBR + 1)
    chosen = jax.random.randint(keys[1], (), 0, slabs)
    ceiling = jnp.where(jnp.arange(slabs, dtype=jnp.int32) == chosen, NBR, ceiling)
    counts = jax.random.randint(keys[2], (slabs, cells), ceiling[:, None] // 2 + 1, ceiling[:, None] + 1)
    spot = jax.random.randint(keys[3], (slabs,), 0, cells)
    counts = jnp.where(jnp.arange(cells, dtype=jnp.int32)[None, :] == spot[:, None], ceiling[:, None], counts)
    return counts.reshape(-1).astype(jnp.int32)


def touch_ends(values, own_key, low, top_value):
    extent = values.shape
    spot = [jax.random.randint(jax.random.fold_in(own_key, axis), (), 0, extent[axis]) for axis in range(len(extent))]
    values = values.at[tuple(spot)].set(low)
    longest = extent.index(max(extent))
    spot[longest] = (spot[longest] + 1) % extent[longest]
    return values.at[tuple(spot)].set(top_value)


def shard_levels(stream_key, extent, shards, least, largest):
    loudness, own = 1.0, jax.random.fold_in(stream_key, 6)
    for axis_at, shards_of in shards:
        steps = jnp.exp(jax.random.uniform(jax.random.fold_in(own, axis_at), (shards_of,), jnp.float32, least / len(shards), largest / len(shards)))
        loudness = loudness * jnp.repeat(steps, extent[axis_at] // shards_of).reshape([-1 if axis == axis_at else 1 for axis in range(len(extent))])
    return loudness


def bell_draw(stream_key, extent, scale, most, pieces=(), held_as=jnp.bfloat16):
    loudness = shard_levels(stream_key, extent, pieces, -0.22, 0.18) if pieces else 1.0
    drawn = jax.random.normal(stream_key, extent, jnp.float32) * scale * loudness
    return jnp.minimum(jnp.maximum(drawn, -most), most).astype(held_as)


def setup_inputs(seed: int = 0) -> dict:
    seeds = jax.random.split(jax.random.key(seed), 14)
    atom_locations = draw_atom_locations(jax.random.fold_in(seeds[13], 71), 0)
    atom_speeds_vector = draw_atom_speeds_vector(jax.random.fold_in(seeds[13], 71), 0)
    inertial_amounts = jnp.clip(jnp.exp(math.log(4.0) - 1.3862944 * jax.random.uniform(seeds[2], (ATOMS,), jnp.float32) ** shard_levels(seeds[2], (ATOMS,), ((0, 4),), -0.2, 0.2)), 1.0, 4.0)
    electric_loads = bell_draw(seeds[3], (ATOMS,), 1.0, 4.0, ((0, 4),), jnp.float32)
    scatter_strengths = jnp.clip(jnp.exp(math.log(2.0) - 1.3862944 * jax.random.uniform(seeds[4], (ATOMS,), jnp.float32) ** shard_levels(seeds[4], (ATOMS,), ((0, 4),), -0.2, 0.2)), 0.5, 2.0)
    gaussian_spreads_sigma = jnp.clip(jnp.exp(math.log(1.4) - 0.6931472 * jax.random.uniform(seeds[5], (ATOMS,), jnp.float32) ** shard_levels(seeds[5], (ATOMS,), ((0, 4),), -0.2, 0.2)), 0.7, 1.4)
    atom_present_flags = touch_ends((jax.random.randint(seeds[6], (ATOMS,), 0, 8) < 7).astype(jnp.int32), jax.random.fold_in(seeds[6], 1), 0, 1)
    observed_volume_values = jnp.clip(2.0 * jax.random.uniform(seeds[7], (NX, GY, GZ), jnp.float32) ** shard_levels(seeds[7], (NX, GY, GZ), ((0, 4),), -0.2, 0.2), 0.0, 2.0)
    voxel_reciprocal_spread = jnp.clip(jnp.exp(math.log(4.0) - 2.0794415 * jax.random.uniform(seeds[8], (NX, GY, GZ), jnp.float32) ** shard_levels(seeds[8], (NX, GY, GZ), ((0, 4),), -0.2, 0.2)), 0.5, 4.0)
    paired_partner_lists = touch_ends(jax.random.randint(seeds[9], (N_BRICK * CELLS, NBR), 0, BLOCKS), jax.random.fold_in(seeds[9], 1), 0, BLOCKS - 1).astype(jnp.int32)
    cell_usage_tally = draw_cell_usage_tally(jax.random.fold_in(seeds[13], 71), 0)
    halo_sender_spots = touch_ends(jax.random.randint(seeds[11], (2, N_BRICK * GHOST), 0, ATOM_DEV), jax.random.fold_in(seeds[11], 1), 0, ATOM_DEV - 1).astype(jnp.int32)
    target_warmth_levels = touch_ends(jax.random.randint(seeds[12], (REPLICA_MEMBERS,), 280, 400), jax.random.fold_in(seeds[12], 1), 280, 399).astype(jnp.int32)
    return dict(atom_locations=atom_locations, atom_speeds_vector=atom_speeds_vector, inertial_amounts=inertial_amounts, electric_loads=electric_loads, scatter_strengths=scatter_strengths, gaussian_spreads_sigma=gaussian_spreads_sigma, atom_present_flags=atom_present_flags, observed_volume_values=observed_volume_values, voxel_reciprocal_spread=voxel_reciprocal_spread, paired_partner_lists=paired_partner_lists, cell_usage_tally=cell_usage_tally, halo_sender_spots=halo_sender_spots, target_warmth_levels=target_warmth_levels)


restraint = 0.1
coupling = 5.0
softening = 1.0
timestep = 0.5
boltzmann = 0.015
heat_bath_damping = 0.5

def wrapped(delta, period):
    return delta - period * jnp.floor(delta / period + 0.5)

def factors(grid, coord, inv_var, period):
    delta = wrapped(grid[:, None] - coord[None, :], period)
    value = jnp.exp(-0.5 * delta * delta * inv_var[None, :])
    return (value, delta * inv_var[None, :] * value)

def spread(x_val, y_val, z_fac, amp):

    def one_plane(row):
        left = ((amp * row)[None, :] * y_val).astype(jnp.bfloat16)
        return lax.dot_general(left, z_fac, (((1,), (1,)), ((), ())), preferred_element_type=jnp.float32)
    return lax.map(one_plane, x_val)

def map_forces(grad_ext, x_val, x_der, y_val, y_der, z_pair, amp):
    count = amp.shape[0]

    def one_plane(carry, inputs):
        plane, x_one, x_slope = inputs
        product = jnp.dot(plane, z_pair, preferred_element_type=jnp.float32)
        along = product[:, :count]
        across = product[:, count:]
        first = lax.optimization_barrier(jnp.sum(y_val * along, axis=0))
        second = lax.optimization_barrier(jnp.sum(y_der * along, axis=0))
        third = lax.optimization_barrier(jnp.sum(y_val * across, axis=0))
        return (carry + jnp.stack([x_slope * first, x_one * second, x_one * third]), None)
    total, _ = lax.scan(one_plane, jnp.zeros((3, count), jnp.float32), (grad_ext, x_val, x_der))
    return -amp[None, :] * total

def pair_forces(coords, charge, ghost_low, ghost_high, paired_partner_lists, live, periods, limit):
    own = jnp.concatenate([coords, charge[None, :]], 0).reshape(4, -1, CELL)
    blocks = jnp.concatenate([own, ghost_low.reshape(4, -1, CELL), ghost_high.reshape(4, -1, CELL)], axis=1)
    period = jnp.array([float(p) for p in periods], jnp.float32)[:, None, None, None]

    def slot(index, total):
        partner = jnp.take(blocks, paired_partner_lists[:, index], axis=1)
        delta = wrapped(own[:3, :, :, None] - partner[:3, :, None, :], period)
        dist = lax.optimization_barrier(jnp.sum(delta * delta, axis=0)) + softening
        active = (index < live).astype(jnp.float32)
        scale = coupling * own[3][:, :, None] * partner[3][:, None, :] * active[:, None, None] / (dist * jnp.sqrt(dist))
        return total + lax.optimization_barrier(jnp.sum(scale[None] * delta, axis=3))
    total = lax.fori_loop(0, limit, slot, jnp.zeros((3, own.shape[1], CELL), jnp.float32))
    return total.reshape(3, -1)

def grids(coords, inv_var, brick):
    planes = SX + 2 * HALO
    plane_grid = (brick * SX - HALO + jnp.arange(planes, dtype=jnp.int32)).astype(jnp.float32)
    x_val, x_der = factors(plane_grid, coords[0], inv_var, NX)
    y_val, y_der = factors(jnp.arange(GY, dtype=jnp.int32).astype(jnp.float32), coords[1], inv_var, GY)
    z_val, z_der = factors(jnp.arange(GZ, dtype=jnp.int32).astype(jnp.float32), coords[2], inv_var, GZ)
    z_pair = jnp.concatenate([z_val, z_der], axis=1).astype(jnp.bfloat16)
    return (x_val, x_der, y_val, y_der, z_pair)

def reference(atom_locations, atom_speeds_vector, inertial_amounts, electric_loads, scatter_strengths, gaussian_spreads_sigma, atom_present_flags, observed_volume_values, voxel_reciprocal_spread, paired_partner_lists, cell_usage_tally, halo_sender_spots, target_warmth_levels):
    occupancy = atom_present_flags.astype(jnp.float32)
    amp_b = (occupancy * scatter_strengths).reshape(N_BRICK, ATOM_DEV)
    charge_b = (occupancy * electric_loads).reshape(N_BRICK, ATOM_DEV)
    inv_b = (1.0 / (gaussian_spreads_sigma * gaussian_spreads_sigma)).reshape(N_BRICK, ATOM_DEV)
    bricks = jnp.arange(N_BRICK, dtype=jnp.int32)
    coords_b = atom_locations.reshape(REPLICA_MEMBERS, 3, N_BRICK, ATOM_DEV)

    def spread_one(inputs):
        coords, inv_var, amp, brick = inputs
        x_val, x_der, y_val, y_der, z_pair = grids(coords, inv_var, brick)
        return spread(x_val, y_val, z_pair[:, :ATOM_DEV], amp)

    def spread_member(coords):
        return lax.map(spread_one, (jnp.moveaxis(coords, 1, 0), inv_b, amp_b, bricks))
    partial_value = lax.map(spread_member, coords_b)
    own = partial_value[:, :, HALO:HALO + SX]
    from_lower = jnp.roll(partial_value[:, :, SX + HALO:], 1, axis=1)
    from_upper = jnp.roll(partial_value[:, :, :HALO], -1, axis=1)
    pad_low = jnp.pad(from_lower, ((0, 0), (0, 0), (0, SX - HALO), (0, 0), (0, 0)))
    pad_high = jnp.pad(from_upper, ((0, 0), (0, 0), (SX - HALO, 0), (0, 0), (0, 0)))
    maps = own + pad_low + pad_high
    summed = lax.optimization_barrier(jnp.sum(maps, axis=0)).reshape(NX, GY, GZ)
    deviation = summed / REPLICA_MEMBERS - observed_volume_values
    grad = (restraint * voxel_reciprocal_spread * deviation).astype(jnp.bfloat16)
    ghost_b = halo_sender_spots.reshape(2, N_BRICK, GHOST)
    nbr_b = paired_partner_lists.reshape(N_BRICK, CELLS, NBR)
    live_b = cell_usage_tally.reshape(N_BRICK, CELLS)
    planes = SX + 2 * HALO

    def force_one(inputs):
        coords, inv_var, amp, charge, brick, nbr, live, low, high = inputs
        x_val, x_der, y_val, y_der, z_pair = grids(coords, inv_var, brick)
        plane_ids = jnp.mod(brick * SX - HALO + jnp.arange(planes, dtype=jnp.int32), NX).astype(jnp.int32)
        grad_ext = jnp.take(grad, plane_ids, axis=0)
        restraint_force = map_forces(grad_ext, x_val, x_der, y_val, y_der, z_pair, amp)
        short = pair_forces(coords, charge, low, high, nbr, live, (NX, GY, GZ), NBR)
        return restraint_force + short

    def force_member(coords):
        packets = []
        for side in range(2):
            chosen = ghost_b[side]
            place = jnp.take_along_axis(coords, chosen[None], axis=2)
            charge_part = jnp.take_along_axis(charge_b, chosen, axis=1)
            packets.append(jnp.moveaxis(jnp.concatenate([place, charge_part[None]], 0), 1, 0))
        low = jnp.roll(packets[0], 1, axis=0)
        high = jnp.roll(packets[1], -1, axis=0)
        return lax.map(force_one, (jnp.moveaxis(coords, 1, 0), inv_b, amp_b, charge_b, bricks, nbr_b, live_b, low, high))
    forces = lax.map(force_member, coords_b)
    forces = jnp.moveaxis(forces, 1, 2).reshape(REPLICA_MEMBERS, 3, ATOMS)
    v_half = atom_speeds_vector + timestep * forces / inertial_amounts[None, None, :]
    kinetic = lax.optimization_barrier(jnp.sum(inertial_amounts[None, None, :] * v_half * v_half, axis=(1, 2)))
    present_moment = kinetic / (3 * ATOMS * boltzmann) + 1e-06
    rescale_ratio = jnp.sqrt(1.0 + heat_bath_damping * (target_warmth_levels.astype(jnp.float32) / present_moment - 1.0))
    new_velocities = rescale_ratio[:, None, None] * v_half
    new_positions = atom_locations + timestep * new_velocities
    return (new_positions, new_velocities, deviation)
```

```python
import functools

import jax
import jax.numpy as jnp
from jax import lax
from jax.experimental import pallas as pl
from jax.experimental.pallas import tpu as pltpu
from jax.sharding import PartitionSpec as P

HALO = 2
CELL = 128
RIM = 2 * HALO

restraint = 0.1
coupling = 5.0
softening = 1.0
timestep = 0.5
boltzmann = 0.015
heat_bath_damping = 0.5

F32 = jnp.float32
BF16 = jnp.bfloat16
NT = (((1,), (1,)), ((), ()))
VMEM = pl.BlockSpec(memory_space=pltpu.VMEM)
SMEM = pl.BlockSpec(memory_space=pltpu.SMEM)
ANY = pl.BlockSpec(memory_space=pl.ANY)


def wrapped(delta, period):
    return delta - period * jnp.floor(delta / period + 0.5)


def gauss(grid, coord, inv_var, period):
    delta = wrapped(grid - coord, period)
    value = jnp.exp(-0.5 * delta * delta * inv_var)
    return value, delta * inv_var * value


def iota(shape, dim):
    return lax.broadcasted_iota(jnp.int32, shape, dim)


def row_class(rows, members):
    share = rows // members
    bit = 0
    while (share << bit) % 8:
        bit += 1
    return share, bit, share << bit


def local_rows(shape, member, bit, block):
    row = iota(shape, 0)
    own = (member >> bit) & 1
    return ((row // block) * (2 * block) + own * block + row % block).astype(F32)


def prep_kernel(coords, par, spots, obs, weight, up, down, sem, *, thick, bit, half):
    own = (lax.axis_index("replica") >> bit) & 1
    block = obs.shape[3]
    copies = []
    for target, first in ((up, thick - HALO), (down, 0)):
        for n, source in enumerate((obs, weight)):
            for plane in range(HALO):
                for q in range(half // block):
                    row = (n * HALO + plane) * half + q * block
                    copies.append(
                        pltpu.make_async_copy(
                            source.at[first + plane, q, own],
                            target.at[pl.ds(row, block)],
                            sem.at[len(copies)],
                        )
                    )
                    copies[-1].start()
    data = jnp.concatenate([coords[...], par[1:2]], 0)
    high = data.astype(BF16)
    rest = data - high.astype(F32)
    mid = rest.astype(BF16)
    low = (rest - mid.astype(F32)).astype(BF16)
    pieces = jnp.concatenate([high.astype(F32), mid.astype(F32), low.astype(F32)], 0).astype(BF16)
    count = coords.shape[1]
    base = 2 * HALO * half
    for side, target in enumerate((up, down)):
        chosen = spots[side : side + 1, :]
        pick = (iota((count, chosen.shape[1]), 0) == chosen).astype(F32).astype(BF16)
        got = jnp.dot(pieces, pick, preferred_element_type=F32)
        got = got[0:4] + got[4:8] + got[8:12]
        groups = chosen.shape[1] // CELL
        for n in range(4):
            for g in range(groups):
                target[base + n * groups + g : base + n * groups + g + 1, :] = got[
                    n : n + 1, g * CELL : (g + 1) * CELL
                ]
    for copy in copies:
        copy.wait()


def spread_kernel(allc, par, out, up, down, left, *, thick, n_x, bit, block):
    members, _, count = allc.shape
    planes, half, depth = out.shape
    rows = 2 * half
    brick = lax.axis_index("brick")
    amp, inv_var = par[0:1], par[2:3]
    y_grid = local_rows((half, count), lax.axis_index("replica"), bit, block)
    z_grid = iota((depth, count), 0).astype(F32)
    x_grid = (iota((16, count), 0) + (brick * thick - HALO)).astype(F32)
    out[...] = jnp.zeros_like(out)

    def member(m, carry):
        place = allc[m]
        x_val, _ = gauss(x_grid, place[0:1], inv_var, n_x)
        y_val, _ = gauss(y_grid, place[1:2], inv_var, rows)
        z_val, _ = gauss(z_grid, place[2:3], inv_var, depth)
        x_amp = amp * x_val
        for i in range(planes):
            left[i * half : (i + 1) * half, :] = (x_amp[i : i + 1] * y_val).astype(BF16)
        got = lax.dot_general(left[...], z_val.astype(BF16), NT, preferred_element_type=F32)
        out[...] += got.reshape(planes, half, depth)
        return carry

    lax.fori_loop(0, members, member, 0)
    up[...] = out[thick:]
    down[...] = out[:RIM]


def pair_kernel(coords, par, low, high, lists, live, out, place_f, place_y, place_z, load, *, n_x, base):
    count = coords.shape[1]
    cells = count // CELL
    slabs = lax.axis_size("brick")
    brick = lax.axis_index("brick")
    scale = float(2**25)

    def fixed(v):
        whole = jnp.floor(v)
        return (whole.astype(jnp.int32) << 25) + ((v - whole) * scale).astype(jnp.int32)

    ghosts = (low.shape[0] - base) // 4
    shift_low = jnp.where(brick == 0, -float(n_x), 0.0).astype(F32)
    shift_high = jnp.where(brick == slabs - 1, float(n_x), 0.0).astype(F32)

    def column(row):
        return jnp.broadcast_to(row, (CELL, CELL)).T

    def enter(n, x, y, z, q):
        at = slice(n * CELL, (n + 1) * CELL)
        place_f[at, :] = column(x * scale)
        place_y[at, :] = column(fixed(y))
        place_z[at, :] = column(fixed(z))
        load[at, :] = column(q)

    for c in range(cells):
        at = slice(c * CELL, (c + 1) * CELL)
        enter(c, coords[0:1, at], coords[1:2, at], coords[2:3, at], par[1:2, at])
    for n, (ref, shift) in enumerate(((low, shift_low), (high, shift_high))):
        for g in range(ghosts):
            row = [ref[base + k * ghosts + g : base + k * ghosts + g + 1, :] for k in range(4)]
            enter(cells + n * ghosts + g, row[0] + shift, row[1], row[2], row[3])

    for c in range(cells):
        at = slice(c * CELL, (c + 1) * CELL)
        xi = jnp.broadcast_to(coords[0:1, at] * scale, (8, CELL))
        yi = jnp.broadcast_to(fixed(coords[1:2, at]), (8, CELL))
        zi = jnp.broadcast_to(fixed(coords[2:3, at]), (8, CELL))

        def slot(s, total):
            start = pl.multiple_of(lists[c, s] * CELL, CELL)
            tx, ty, tz = total
            for g in range(CELL // 8):
                here = pl.ds(start + g * 8, 8)
                dx = xi - place_f[here, :]
                dy = (yi - place_y[here, :]).astype(F32)
                dz = (zi - place_z[here, :]).astype(F32)
                dist = dx * dx + dy * dy + (dz * dz + softening * scale * scale)
                inv = lax.rsqrt(dist)
                w = load[here, :] * inv * (inv * inv)
                tx, ty, tz = tx + w * dx, ty + w * dy, tz + w * dz
            return tx, ty, tz

        zero = jnp.zeros((8, CELL), F32)
        total = lax.fori_loop(0, live[c], slot, (zero, zero, zero))
        factor = (coupling * scale * scale) * par[1:2, at]
        for k in range(3):
            out[k : k + 1, at] = factor * jnp.sum(total[k], axis=0, keepdims=True)


def force_kernel(
    allc, par, total, low, high, near_low, near_high, obs, weight,
    dev_out, own_out, partner_out,
    obs_s, weight_s, grad, dev_s, sem, *, thick, n_x, bit, share, members,
):
    planes, half, depth = total.shape
    count = allc.shape[2]
    rows = 2 * half
    block = obs.shape[3]
    member = lax.axis_index("replica")
    own = (member >> bit) & 1
    brick = lax.axis_index("brick")
    copies = []
    for n, (source, target) in enumerate(((obs, obs_s), (weight, weight_s))):
        for q in range(half // block):
            copies.append(
                pltpu.make_async_copy(
                    source.at[:, q, own],
                    target.at[pl.ds(HALO, thick), pl.ds(q * block, block)],
                    sem.at[len(copies)],
                )
            )
            copies[-1].start()
    for ref, first in ((near_low, 0), (near_high, thick + HALO)):
        for plane in range(HALO):
            obs_s[first + plane] = ref[plane * half : (plane + 1) * half, :]
            at = (HALO + plane) * half
            weight_s[first + plane] = ref[at : at + half, :]
    for copy in copies:
        copy.wait()
    for i in range(planes):
        summed = total[i]
        if i < RIM:
            summed = summed + low[i]
        if i >= thick:
            summed = summed + high[i - thick]
        dev = summed / members - obs_s[i]
        grad[i * half : (i + 1) * half, :] = (restraint * weight_s[i] * dev).astype(BF16)
        if HALO <= i < thick + HALO:
            dev_s[i - HALO] = dev
    first_row = member * share
    spot = (first_row // (2 * block)) * block + first_row % block
    for n in range(half // share):

        @pl.when(spot == n * share)
        def _(n=n):
            dev_out[...] = dev_s[:, n * share : (n + 1) * share, :]

    x_grid = (iota((16, CELL), 0) + (brick * thick - HALO)).astype(F32)
    y_grid = local_rows((half, CELL), member, bit, block)
    z_grid = iota((depth, CELL), 0).astype(F32)
    for out, m in ((own_out, member), (partner_out, member ^ (1 << bit))):
        for t in range(count // CELL):
            at = slice(t * CELL, (t + 1) * CELL)
            place = allc[m, :, at]
            inv_var = par[2:3, at]
            x_val, x_der = gauss(x_grid, place[0:1], inv_var, n_x)
            y_val, y_der = gauss(y_grid, place[1:2], inv_var, rows)
            z_val, z_der = gauss(z_grid, place[2:3], inv_var, depth)
            z_pair = jnp.concatenate([z_val, z_der], 1).astype(BF16)
            got = jnp.dot(grad[...], z_pair, preferred_element_type=F32)
            sums = [jnp.zeros((8, CELL), F32) for _ in range(3)]
            for i in range(planes):
                part = [jnp.zeros((8, CELL), F32) for _ in range(3)]
                for g in range(half // 8):
                    j = slice(g * 8, (g + 1) * 8)
                    k = slice(i * half + g * 8, i * half + (g + 1) * 8)
                    along, across = got[k, :CELL], got[k, CELL:]
                    part[0] += y_val[j] * along
                    part[1] += y_der[j] * along
                    part[2] += y_val[j] * across
                sums[0] += x_der[i : i + 1] * part[0]
                sums[1] += x_val[i : i + 1] * part[1]
                sums[2] += x_val[i : i + 1] * part[2]
            for k in range(3):
                out[k : k + 1, at] = -par[0:1, at] * jnp.sum(sums[k], axis=0, keepdims=True)


def local(
    atom_locations,
    atom_speeds_vector,
    inertial_amounts,
    electric_loads,
    scatter_strengths,
    gaussian_spreads_sigma,
    atom_present_flags,
    observed_volume_values,
    voxel_reciprocal_spread,
    paired_partner_lists,
    cell_usage_tally,
    halo_sender_spots,
    target_warmth_levels,
):
    thick, rows, depth = observed_volume_values.shape
    slabs = lax.axis_size("brick")
    members = lax.axis_size("replica")
    n_x = thick * slabs
    coords = atom_locations[0]
    count = coords.shape[1]
    planes = thick + 2 * HALO
    share, bit, block = row_class(rows, members)
    half = rows // 2
    base = 2 * HALO * half
    ghosts = halo_sender_spots.shape[1]
    near_rows = base + 4 * ghosts // CELL

    everyone = lax.all_to_all(
        jnp.broadcast_to(coords[None], (members,) + coords.shape), "replica", 0, 0
    )
    occupancy = atom_present_flags.astype(F32)
    par = jnp.stack(
        [
            occupancy * scatter_strengths,
            occupancy * electric_loads,
            1.0 / (gaussian_spreads_sigma * gaussian_spreads_sigma),
            inertial_amounts,
        ]
    )
    obs = observed_volume_values.reshape(thick, half // block, 2, block, depth)
    weight = voxel_reciprocal_spread.reshape(thick, half // block, 2, block, depth)
    near = jax.ShapeDtypeStruct((near_rows, CELL), F32)
    near_up, near_down = pl.pallas_call(
        functools.partial(prep_kernel, thick=thick, bit=bit, half=half),
        out_shape=(near, near),
        in_specs=[VMEM, VMEM, VMEM, ANY, ANY],
        out_specs=(VMEM, VMEM),
        scratch_shapes=[pltpu.SemaphoreType.DMA((4 * HALO * (half // block),))],
        name="prep",
    )(coords, par, halo_sender_spots, obs, weight)

    ring = [(i, (i + 1) % slabs) for i in range(slabs)]
    back = [(target, source) for source, target in ring]
    near_low = lax.ppermute(near_up, "brick", ring)
    near_high = lax.ppermute(near_down, "brick", back)

    rim = jax.ShapeDtypeStruct((RIM, half, depth), F32)
    total, rim_up, rim_down = pl.pallas_call(
        functools.partial(spread_kernel, thick=thick, n_x=n_x, bit=bit, block=block),
        out_shape=(jax.ShapeDtypeStruct((planes, half, depth), F32), rim, rim),
        in_specs=[VMEM, VMEM],
        out_specs=(VMEM, VMEM, VMEM),
        scratch_shapes=[pltpu.VMEM((planes * half, count), BF16)],
        name="spread",
    )(everyone, par)
    low = lax.ppermute(rim_up, "brick", ring)
    high = lax.ppermute(rim_down, "brick", back)

    blocks = count // CELL + 2 * ghosts // CELL
    short = pl.pallas_call(
        functools.partial(pair_kernel, n_x=n_x, base=base),
        out_shape=jax.ShapeDtypeStruct((3, count), F32),
        in_specs=[VMEM, VMEM, VMEM, VMEM, SMEM, SMEM],
        out_specs=VMEM,
        scratch_shapes=[
            pltpu.VMEM((blocks * CELL, CELL), F32),
            pltpu.VMEM((blocks * CELL, CELL), jnp.int32),
            pltpu.VMEM((blocks * CELL, CELL), jnp.int32),
            pltpu.VMEM((blocks * CELL, CELL), F32),
        ],
        cost_estimate=pl.CostEstimate(flops=40_000_000, bytes_accessed=400_000, transcendentals=0),
        name="pair",
    )(coords, par, near_low, near_high, paired_partner_lists, cell_usage_tally)

    force = jax.ShapeDtypeStruct((3, count), F32)
    deviation, own, partner = pl.pallas_call(
        functools.partial(
            force_kernel, thick=thick, n_x=n_x, bit=bit, share=share, members=members
        ),
        out_shape=(jax.ShapeDtypeStruct((thick, share, depth), F32), force, force),
        in_specs=[VMEM] * 7 + [ANY, ANY],
        out_specs=(VMEM, VMEM, VMEM),
        scratch_shapes=[
            pltpu.VMEM((planes, half, depth), F32),
            pltpu.VMEM((planes, half, depth), F32),
            pltpu.VMEM((planes * half, depth), BF16),
            pltpu.VMEM((thick, half, depth), F32),
            pltpu.SemaphoreType.DMA((2 * (half // block),)),
        ],
        name="force",
    )(everyone, par, total, low, high, near_low, near_high, obs, weight)

    swap = [(i, i ^ (1 << bit)) for i in range(members)]
    other = lax.ppermute(partner, "replica", swap)
    mass = par[3:4]
    v_half = atom_speeds_vector[0] + timestep * (own + other + short) / mass
    part = jnp.sum(mass * v_half * v_half).reshape(1, 1)
    kinetic = part
    if slabs <= 4:
        for step in range(1, slabs):
            route = [(i, (i + step) % slabs) for i in range(slabs)]
            kinetic = kinetic + lax.ppermute(part, "brick", route)
    else:
        kinetic = lax.psum(part, "brick")
    present_moment = kinetic / (3 * count * slabs * boltzmann) + 1e-06
    rescale_ratio = jnp.sqrt(
        1.0 + heat_bath_damping * (target_warmth_levels.astype(F32)[:, None] / present_moment - 1.0)
    )
    new_velocities = rescale_ratio * v_half
    new_positions = coords + timestep * new_velocities
    return (new_positions[None], new_velocities[None], deviation)


def solution(mesh):
    return jax.shard_map(
        local,
        mesh=mesh,
        in_specs=(
            P("replica", None, "brick"),
            P("replica", None, "brick"),
            P("brick"),
            P("brick"),
            P("brick"),
            P("brick"),
            P("brick"),
            P("brick", None, None),
            P("brick", None, None),
            P("brick", None),
            P("brick"),
            P(None, "brick"),
            P("replica"),
        ),
        out_specs=(
            P("replica", None, "brick"),
            P("replica", None, "brick"),
            P("brick", "replica", None),
        ),
        check_vma=False,
    )
```

```python
import functools
import math

import jax
import jax.numpy as jnp
from jax import lax
from jax.experimental import pallas as pl
from jax.experimental.pallas import tpu as pltpu
from jax.sharding import PartitionSpec as P

HALO = 2
CELL = 128
RIM = 2 * HALO

restraint = 0.1
coupling = 5.0
softening = 1.0
timestep = 0.5
boltzmann = 0.015
heat_bath_damping = 0.5

F32 = jnp.float32
BF16 = jnp.bfloat16
NT = (((1,), (1,)), ((), ()))
VMEM = pl.BlockSpec(memory_space=pltpu.VMEM)
SMEM = pl.BlockSpec(memory_space=pltpu.SMEM)
ANY = pl.BlockSpec(memory_space=pl.ANY)


def bell(grid, coord, rate, period=None):
    delta = grid - coord
    if period is not None:
        away = jnp.abs(delta)
        delta = jnp.minimum(away, period - away)
    return jnp.exp2(delta * delta * rate)


def bell_slope(grid, coord, inv_var, rate, period=None):
    delta = grid - coord
    if period is not None:
        delta = delta - period * jnp.floor(delta * (1.0 / period) + 0.5)
    value = jnp.exp2(delta * delta * rate)
    return value, delta * inv_var * value


def limit(mib):
    return pltpu.CompilerParams(vmem_limit_bytes=mib << 20)


def iota(shape, dim):
    return lax.broadcasted_iota(jnp.int32, shape, dim)


def row_class(rows, members):
    share = rows // members
    bit = 0
    while (share << bit) % 8:
        bit += 1
    return share, bit, share << bit


def local_rows(shape, member, bit, block):
    row = iota(shape, 0)
    own = (member >> bit) & 1
    return ((row // block) * (2 * block) + own * block + row % block).astype(F32)


def prep_kernel(
    coords, flags, scatter, loads, sigma, mass, spots, obs, weight, par, up, down, sem, *, thick, bit, half
):
    own = (lax.axis_index("replica") >> bit) & 1
    block = obs.shape[3]
    copies = []
    for target, first in ((up, thick - HALO), (down, 0)):
        for n, source in enumerate((obs, weight)):
            for plane in range(HALO):
                for q in range(half // block):
                    row = (n * HALO + plane) * half + q * block
                    copies.append(
                        pltpu.make_async_copy(
                            source.at[first + plane, q, own],
                            target.at[pl.ds(row, block)],
                            sem.at[len(copies)],
                        )
                    )
                    copies[-1].start()
    occupancy = flags[...].astype(F32)
    inv_var = 1.0 / (sigma[...] * sigma[...])
    charge = occupancy * loads[...]
    par[0:1] = occupancy * scatter[...]
    par[1:2] = charge
    par[2:3] = inv_var
    par[3:4] = (-0.5 * math.log2(math.e)) * inv_var
    par[4:5] = mass[...]
    data = jnp.concatenate([coords[0], coords[1], coords[2], charge], 0)
    high = data.astype(BF16)
    rest = data - high.astype(F32)
    mid = rest.astype(BF16)
    low = (rest - mid.astype(F32)).astype(BF16)
    pieces = jnp.concatenate([high.astype(F32), mid.astype(F32), low.astype(F32)], 0).astype(BF16)
    count = data.shape[1]
    base = 2 * HALO * half
    for side, target in enumerate((up, down)):
        chosen = spots[side : side + 1, :]
        pick = (iota((count, chosen.shape[1]), 0) == chosen).astype(F32).astype(BF16)
        got = jnp.dot(pieces, pick, preferred_element_type=F32)
        got = got[0:4] + got[4:8] + got[8:12]
        groups = chosen.shape[1] // CELL
        for n in range(4):
            for g in range(groups):
                target[base + n * groups + g : base + n * groups + g + 1, :] = got[
                    n : n + 1, g * CELL : (g + 1) * CELL
                ]
    for copy in copies:
        copy.wait()


def spread_kernel(allc, par, out, up, down, left_a, left_b, depth_a, depth_b, *, thick, bit, block):
    members, _, _, count = allc.shape
    planes, half, depth = out.shape
    rows = 2 * half
    brick = lax.axis_index("brick")
    amp, rate = par[0:1], par[3:4]
    y_grid = local_rows((half, count), lax.axis_index("replica"), bit, block)
    z_grid = iota((depth, count), 0).astype(F32)
    x_grid = (iota((16, count), 0) + (brick * thick - HALO)).astype(F32)

    def build(m, left, deep):
        x_amp = amp * bell(x_grid, allc[m, 0], rate)
        y_val = bell(y_grid, allc[m, 1], rate, rows)
        deep[...] = bell(z_grid, allc[m, 2], rate, depth).astype(BF16)
        for i in range(planes):
            left[i * half : (i + 1) * half, :] = (x_amp[i : i + 1] * y_val).astype(BF16)

    def product(left, deep):
        got = lax.dot_general(left[...], deep[...], NT, preferred_element_type=F32)
        return got.reshape(planes, half, depth)

    build(0, left_a, depth_a)
    out[...] = product(left_a, depth_a)
    build(1, left_b, depth_b)

    def two(n, carry):
        m = 2 * n
        out[...] += product(left_b, depth_b)
        build(m, left_a, depth_a)
        out[...] += product(left_a, depth_a)
        build(m + 1, left_b, depth_b)
        return carry

    lax.fori_loop(1, members // 2, two, 0)
    out[...] += product(left_b, depth_b)
    up[...] = out[thick:]
    down[...] = out[:RIM]


def pair_kernel(coords, par, low, high, lists, live, out, place_f, place_y, place_z, load, *, n_x, base):
    count = coords.shape[2]
    cells = count // CELL
    slabs = lax.axis_size("brick")
    brick = lax.axis_index("brick")
    scale = float(2**25)

    def fixed(v):
        whole = jnp.floor(v)
        return (whole.astype(jnp.int32) << 25) + ((v - whole) * scale).astype(jnp.int32)

    ghosts = (low.shape[0] - base) // 4
    shift_low = jnp.where(brick == 0, -float(n_x), 0.0).astype(F32)
    shift_high = jnp.where(brick == slabs - 1, float(n_x), 0.0).astype(F32)

    def column(row):
        return jnp.broadcast_to(row, (CELL, CELL)).T

    def enter(n, x, y, z, q):
        at = slice(n * CELL, (n + 1) * CELL)
        place_f[at, :] = column(x * scale)
        place_y[at, :] = column(fixed(y))
        place_z[at, :] = column(fixed(z))
        load[at, :] = column(q)

    for c in range(cells):
        at = slice(c * CELL, (c + 1) * CELL)
        enter(c, coords[0, :, at], coords[1, :, at], coords[2, :, at], par[1:2, at])
    for n, (ref, shift) in enumerate(((low, shift_low), (high, shift_high))):
        for g in range(ghosts):
            row = [ref[base + k * ghosts + g : base + k * ghosts + g + 1, :] for k in range(4)]
            enter(cells + n * ghosts + g, row[0] + shift, row[1], row[2], row[3])

    for c in range(cells):
        at = slice(c * CELL, (c + 1) * CELL)
        xi = jnp.broadcast_to(coords[0, :, at] * scale, (8, CELL))
        yi = jnp.broadcast_to(fixed(coords[1, :, at]), (8, CELL))
        zi = jnp.broadcast_to(fixed(coords[2, :, at]), (8, CELL))

        def slot(s, total):
            start = pl.multiple_of(lists[c, s] * CELL, CELL)
            tx, ty, tz = total
            for g in range(CELL // 8):
                here = pl.ds(start + g * 8, 8)
                dx = xi - place_f[here, :]
                dy = (yi - place_y[here, :]).astype(F32)
                dz = (zi - place_z[here, :]).astype(F32)
                dist = dx * dx + dy * dy + (dz * dz + softening * scale * scale)
                inv = lax.rsqrt(dist)
                w = load[here, :] * inv * (inv * inv)
                tx, ty, tz = tx + w * dx, ty + w * dy, tz + w * dz
            return tx, ty, tz

        zero = jnp.zeros((8, CELL), F32)
        total = lax.fori_loop(0, live[c], slot, (zero, zero, zero))
        factor = (coupling * scale * scale) * par[1:2, at]
        for k in range(3):
            out[k : k + 1, at] = factor * jnp.sum(total[k], axis=0, keepdims=True)


def force_kernel(
    allc, par, short, total, low, high, near_low, near_high, obs, weight,
    dev_out, own_out, partner_out,
    obs_s, weight_s, grad, dev_s, sem, *, thick, bit, share, members,
):
    planes, half, depth = total.shape
    count = allc.shape[3]
    rows = 2 * half
    block = obs.shape[3]
    member = lax.axis_index("replica")
    own = (member >> bit) & 1
    brick = lax.axis_index("brick")
    copies = []
    for n, (source, target) in enumerate(((obs, obs_s), (weight, weight_s))):
        for q in range(half // block):
            copies.append(
                pltpu.make_async_copy(
                    source.at[:, q, own],
                    target.at[pl.ds(HALO, thick), pl.ds(q * block, block)],
                    sem.at[len(copies)],
                )
            )
            copies[-1].start()
    for ref, first in ((near_low, 0), (near_high, thick + HALO)):
        for plane in range(HALO):
            obs_s[first + plane] = ref[plane * half : (plane + 1) * half, :]
            at = (HALO + plane) * half
            weight_s[first + plane] = ref[at : at + half, :]
    for copy in copies:
        copy.wait()
    for i in range(planes):
        summed = total[i]
        if i < RIM:
            summed = summed + low[i]
        if i >= thick:
            summed = summed + high[i - thick]
        dev = summed / members - obs_s[i]
        grad[i * half : (i + 1) * half, :] = (restraint * weight_s[i] * dev).astype(BF16)
        if HALO <= i < thick + HALO:
            dev_s[i - HALO] = dev
    first_row = member * share
    spot = (first_row // (2 * block)) * block + first_row % block
    for n in range(half // share):

        @pl.when(spot == n * share)
        def _(n=n):
            dev_out[...] = dev_s[:, n * share : (n + 1) * share, :]

    x_grid = (iota((16, CELL), 0) + (brick * thick - HALO)).astype(F32)
    y_grid = local_rows((half, CELL), member, bit, block)
    z_grid = iota((depth, CELL), 0).astype(F32)
    for out, m in ((own_out, member), (partner_out, member ^ (1 << bit))):
        for t in range(count // CELL):
            at = slice(t * CELL, (t + 1) * CELL)
            inv_var, rate = par[2:3, at], par[3:4, at]
            x_val, x_der = bell_slope(x_grid, allc[m, 0, :, at], inv_var, rate)
            y_val, y_der = bell_slope(y_grid, allc[m, 1, :, at], inv_var, rate, rows)
            z_val, z_der = bell_slope(z_grid, allc[m, 2, :, at], inv_var, rate, depth)
            z_pair = jnp.concatenate([z_val, z_der], 1).astype(BF16)
            got = jnp.dot(grad[...], z_pair, preferred_element_type=F32)
            sums = [jnp.zeros((8, CELL), F32) for _ in range(3)]
            for i in range(planes):
                part = [jnp.zeros((8, CELL), F32) for _ in range(3)]
                for g in range(half // 8):
                    j = slice(g * 8, (g + 1) * 8)
                    k = slice(i * half + g * 8, i * half + (g + 1) * 8)
                    along, across = got[k, :CELL], got[k, CELL:]
                    part[0] += y_val[j] * along
                    part[1] += y_der[j] * along
                    part[2] += y_val[j] * across
                sums[0] += x_der[i : i + 1] * part[0]
                sums[1] += x_val[i : i + 1] * part[1]
                sums[2] += x_val[i : i + 1] * part[2]
            for k in range(3):
                force = -par[0:1, at] * jnp.sum(sums[k], axis=0, keepdims=True)
                if out is own_out:
                    force = force + short[k : k + 1, at]
                out[k : k + 1, at] = force


def kick_kernel(own, other, par, speed, v_half, part):
    mass = par[4:5]
    energy = jnp.zeros_like(mass)
    for k in range(3):
        v = speed[k] + timestep * (own[k : k + 1] + other[k : k + 1]) / mass
        v_half[k : k + 1] = v
        energy = energy + mass * v * v
    part[...] = jnp.broadcast_to(jnp.sum(energy, axis=1, keepdims=True), part.shape)


def drift_kernel(*refs, freedom):
    parts, (v_half, coords, warmth, place_out, speed_out) = refs[:-5], refs[-5:]
    kinetic = parts[0][0:1]
    for part in parts[1:]:
        kinetic = kinetic + part[0:1]
    present_moment = kinetic / (freedom * boltzmann) + 1e-06
    ratio = jnp.sqrt(
        1.0 + heat_bath_damping * (warmth[0].astype(F32) / present_moment - 1.0)
    )
    ratio = jnp.concatenate([ratio] * (v_half.shape[1] // ratio.shape[1]), 1)
    for k in range(3):
        v = ratio * v_half[k : k + 1]
        speed_out[k] = v
        place_out[k] = coords[k] + timestep * v


def local(
    atom_locations,
    atom_speeds_vector,
    inertial_amounts,
    electric_loads,
    scatter_strengths,
    gaussian_spreads_sigma,
    atom_present_flags,
    observed_volume_values,
    voxel_reciprocal_spread,
    paired_partner_lists,
    cell_usage_tally,
    halo_sender_spots,
    target_warmth_levels,
):
    thick, rows, depth = observed_volume_values.shape
    slabs = lax.axis_size("brick")
    members = lax.axis_size("replica")
    n_x = thick * slabs
    coords = jnp.transpose(atom_locations, (1, 0, 2))
    speeds = jnp.transpose(atom_speeds_vector, (1, 0, 2))
    count = coords.shape[2]
    planes = thick + 2 * HALO
    share, bit, block = row_class(rows, members)
    half = rows // 2
    base = 2 * HALO * half
    ghosts = halo_sender_spots.shape[1]
    near_rows = base + 4 * ghosts // CELL
    assert slabs >= 4 and n_x >= 2 * (thick + HALO)

    everyone = lax.all_to_all(
        jnp.broadcast_to(coords[None], (members,) + coords.shape), "replica", 0, 0
    )
    obs = observed_volume_values.reshape(thick, half // block, 2, block, depth)
    weight = voxel_reciprocal_spread.reshape(thick, half // block, 2, block, depth)
    near = jax.ShapeDtypeStruct((near_rows, CELL), F32)
    par, near_up, near_down = pl.pallas_call(
        functools.partial(prep_kernel, thick=thick, bit=bit, half=half),
        out_shape=(jax.ShapeDtypeStruct((8, count), F32), near, near),
        in_specs=[VMEM] * 7 + [ANY, ANY],
        out_specs=(VMEM, VMEM, VMEM),
        scratch_shapes=[pltpu.SemaphoreType.DMA((4 * HALO * (half // block),))],
        compiler_params=limit(8),
        name="prep",
    )(
        coords,
        *(
            a.reshape(1, count)
            for a in (
                atom_present_flags,
                scatter_strengths,
                electric_loads,
                gaussian_spreads_sigma,
                inertial_amounts,
            )
        ),
        halo_sender_spots,
        obs,
        weight,
    )

    ring = [(i, (i + 1) % slabs) for i in range(slabs)]
    back = [(target, source) for source, target in ring]
    near_low = lax.ppermute(near_up, "brick", ring)
    near_high = lax.ppermute(near_down, "brick", back)

    rim = jax.ShapeDtypeStruct((RIM, half, depth), F32)
    total, rim_up, rim_down = pl.pallas_call(
        functools.partial(spread_kernel, thick=thick, bit=bit, block=block),
        out_shape=(jax.ShapeDtypeStruct((planes, half, depth), F32), rim, rim),
        in_specs=[VMEM, VMEM],
        out_specs=(VMEM, VMEM, VMEM),
        scratch_shapes=[pltpu.VMEM((planes * half, count), BF16)] * 2
        + [pltpu.VMEM((depth, count), BF16)] * 2,
        compiler_params=limit(16),
        name="spread",
    )(everyone, par)
    low = lax.ppermute(rim_up, "brick", ring)
    high = lax.ppermute(rim_down, "brick", back)

    blocks = count // CELL + 2 * ghosts // CELL
    table = pltpu.VMEM((blocks * CELL, CELL), F32)
    short = pl.pallas_call(
        functools.partial(pair_kernel, n_x=n_x, base=base),
        out_shape=jax.ShapeDtypeStruct((3, count), F32),
        in_specs=[VMEM, VMEM, VMEM, VMEM, SMEM, SMEM],
        out_specs=VMEM,
        scratch_shapes=[
            table,
            pltpu.VMEM((blocks * CELL, CELL), jnp.int32),
            pltpu.VMEM((blocks * CELL, CELL), jnp.int32),
            table,
        ],
        compiler_params=limit(8),
        cost_estimate=pl.CostEstimate(flops=40_000_000, bytes_accessed=400_000, transcendentals=0),
        name="pair",
    )(coords, par, near_low, near_high, paired_partner_lists, cell_usage_tally)

    force = jax.ShapeDtypeStruct((3, count), F32)
    deviation, own, partner = pl.pallas_call(
        functools.partial(force_kernel, thick=thick, bit=bit, share=share, members=members),
        out_shape=(jax.ShapeDtypeStruct((thick, share, depth), F32), force, force),
        in_specs=[VMEM] * 8 + [ANY, ANY],
        out_specs=(VMEM, VMEM, VMEM),
        scratch_shapes=[
            pltpu.VMEM((planes, half, depth), F32),
            pltpu.VMEM((planes, half, depth), F32),
            pltpu.VMEM((planes * half, depth), BF16),
            pltpu.VMEM((thick, half, depth), F32),
            pltpu.SemaphoreType.DMA((2 * (half // block),)),
        ],
        compiler_params=limit(16),
        name="force",
    )(everyone, par, short, total, low, high, near_low, near_high, obs, weight)

    swap = [(i, i ^ (1 << bit)) for i in range(members)]
    other = lax.ppermute(partner, "replica", swap)
    v_half, part = pl.pallas_call(
        kick_kernel,
        out_shape=(force, jax.ShapeDtypeStruct((8, CELL), F32)),
        in_specs=[VMEM] * 4,
        out_specs=(VMEM, VMEM),
        compiler_params=limit(2),
        name="kick",
    )(own, other, par, speeds)
    if slabs <= 4:
        parts = [part]
        for step in range(1, slabs):
            route = [(i, (i + step) % slabs) for i in range(slabs)]
            parts.append(lax.ppermute(part, "brick", route))
    else:
        parts = [lax.psum(part, "brick")]
    moved = jax.ShapeDtypeStruct((3, 1, count), F32)
    new_positions, new_velocities = pl.pallas_call(
        functools.partial(drift_kernel, freedom=3 * count * slabs),
        out_shape=(moved, moved),
        in_specs=[VMEM] * (len(parts) + 2) + [SMEM],
        out_specs=(VMEM, VMEM),
        compiler_params=limit(2),
        name="drift",
    )(*parts, v_half, coords, target_warmth_levels)
    return (
        jnp.transpose(new_positions, (1, 0, 2)),
        jnp.transpose(new_velocities, (1, 0, 2)),
        deviation,
    )


def solution(mesh):
    return jax.shard_map(
        local,
        mesh=mesh,
        in_specs=(
            P("replica", None, "brick"),
            P("replica", None, "brick"),
            P("brick"),
            P("brick"),
            P("brick"),
            P("brick"),
            P("brick"),
            P("brick", None, None),
            P("brick", None, None),
            P("brick", None),
            P("brick"),
            P(None, "brick"),
            P("replica"),
        ),
        out_specs=(
            P("replica", None, "brick"),
            P("replica", None, "brick"),
            P("brick", "replica", None),
        ),
        check_vma=False,
    )
```

```python
import functools
import math

import jax
import jax.numpy as jnp
from jax import lax
from jax.experimental import pallas as pl
from jax.experimental.pallas import tpu as pltpu
from jax.sharding import PartitionSpec as P

HALO = 2
CELL = 128
RIM = 2 * HALO

restraint = 0.1
coupling = 5.0
softening = 1.0
timestep = 0.5
boltzmann = 0.015
heat_bath_damping = 0.5

F32 = jnp.float32
BF16 = jnp.bfloat16
NT = (((1,), (1,)), ((), ()))
VMEM = pl.BlockSpec(memory_space=pltpu.VMEM)
SMEM = pl.BlockSpec(memory_space=pltpu.SMEM)
HBM = pl.BlockSpec(memory_space=pltpu.HBM)


def bell(grid, coord, rate, period=None):
    delta = grid - coord
    if period is not None:
        away = jnp.abs(delta)
        delta = jnp.minimum(away, period - away)
    return jnp.exp2(delta * delta * rate)


def bell_slope(grid, coord, inv_var, rate, period=None):
    delta = grid - coord
    if period is not None:
        delta = delta - period * jnp.floor(delta * (1.0 / period) + 0.5)
    value = jnp.exp2(delta * delta * rate)
    return value, delta * inv_var * value


def limit(mib):
    return pltpu.CompilerParams(vmem_limit_bytes=mib << 20)


def cost(us):
    return pl.CostEstimate(flops=us * 500_000_000, bytes_accessed=us * 1_000_000, transcendentals=0)


def iota(shape, dim):
    return lax.broadcasted_iota(jnp.int32, shape, dim)


def row_class(rows, members):
    share = rows // members
    bit = 0
    while (share << bit) % 8:
        bit += 1
    return share, bit, share << bit


def local_rows(shape, member, bit, block):
    row = iota(shape, 0)
    own = (member >> bit) & 1
    return ((row // block) * (2 * block) + own * block + row % block).astype(F32)


def prep_kernel(
    mine, flags, scatter, loads, sigma, mass, spots, obs, weight,
    par, up, down, flags_s, floats_s, spots_s, small_sem, sem, *, thick, bit, half,
):
    own = (lax.axis_index("replica") >> bit) & 1
    block = obs.shape[3]
    small = [
        pltpu.make_async_copy(flags, flags_s.at[0], small_sem.at[0]),
        pltpu.make_async_copy(spots, spots_s, small_sem.at[1]),
    ]
    for n, source in enumerate((scatter, loads, sigma, mass)):
        small.append(pltpu.make_async_copy(source, floats_s.at[n, 0], small_sem.at[2 + n]))
    for copy in small:
        copy.start()
    copies = []
    for target, first in ((up, thick - HALO), (down, 0)):
        for n, source in enumerate((obs, weight)):
            for plane in range(HALO):
                for q in range(half // block):
                    row = (n * HALO + plane) * half + q * block
                    copies.append(
                        pltpu.make_async_copy(
                            source.at[first + plane, q, own],
                            target.at[pl.ds(row, block)],
                            sem.at[len(copies)],
                        )
                    )
                    copies[-1].start()
    for copy in small:
        copy.wait()
    occupancy = flags_s[...].astype(F32)
    inv_var = 1.0 / (floats_s[2] * floats_s[2])
    charge = occupancy * floats_s[1]
    par[0:1] = occupancy * floats_s[0]
    par[1:2] = charge
    par[2:3] = inv_var
    par[3:4] = (-0.5 * math.log2(math.e)) * inv_var
    par[4:5] = floats_s[3]
    data = jnp.concatenate([mine[0, 0], mine[0, 1], mine[0, 2], charge], 0)
    high = data.astype(BF16)
    rest = data - high.astype(F32)
    mid = rest.astype(BF16)
    low = (rest - mid.astype(F32)).astype(BF16)
    pieces = jnp.concatenate([high.astype(F32), mid.astype(F32), low.astype(F32)], 0).astype(BF16)
    count = data.shape[1]
    base = 2 * HALO * half
    for side, target in enumerate((up, down)):
        chosen = spots_s[side : side + 1, :]
        pick = (iota((count, chosen.shape[1]), 0) == chosen).astype(F32).astype(BF16)
        got = jnp.dot(pieces, pick, preferred_element_type=F32)
        got = got[0:4] + got[4:8] + got[8:12]
        groups = chosen.shape[1] // CELL
        for n in range(4):
            for g in range(groups):
                target[base + n * groups + g : base + n * groups + g + 1, :] = got[
                    n : n + 1, g * CELL : (g + 1) * CELL
                ]
    for copy in copies:
        copy.wait()


def spread_grids(half, depth, count, thick, bit, block):
    first = lax.axis_index("brick") * thick - HALO
    x_grid = (iota((16, count), 0) + first).astype(F32)
    y_grid = local_rows((half, count), lax.axis_index("replica"), bit, block)
    z_grid = iota((depth, count), 0).astype(F32)
    return x_grid, y_grid, z_grid


def member_bells(place, amp, rate, grids):
    x_grid, y_grid, z_grid = grids
    x_amp = amp * bell(x_grid, place[0], rate)
    y_val = bell(y_grid, place[1], rate, 2 * y_grid.shape[0])
    z_val = bell(z_grid, place[2], rate, z_grid.shape[0]).astype(BF16)
    return x_amp, y_val, z_val


def layers(left, x_amp, y_val, planes):
    half = y_val.shape[0]
    for n, i in enumerate(planes):
        left[n * half : (n + 1) * half, :] = (x_amp[i : i + 1] * y_val).astype(BF16)


def product(left, z_val, shape):
    return lax.dot_general(left[...], z_val, NT, preferred_element_type=F32).reshape(shape)


def early_kernel(*refs, thick, bit, block):
    groups, par, out, lefts, deeps = refs[:-6], refs[-6], refs[-5], refs[-4:-2], refs[-2:]
    planes, half, depth = out.shape
    count = par.shape[1]
    amp, rate = par[0:1], par[3:4]
    grids = spread_grids(half, depth, count, thick, bit, block)
    places = [(g, n) for g in groups for n in range(g.shape[0])]

    def build(m):
        g, n = places[m]
        x_amp, y_val, z_val = member_bells(g.at[n], amp, rate, grids)
        deeps[m % 2][...] = z_val
        layers(lefts[m % 2], x_amp, y_val, range(planes))

    build(0)
    for m in range(len(places)):
        if m + 1 < len(places):
            build(m + 1)
        got = product(lefts[m % 2], deeps[m % 2][...], out.shape)
        out[...] = got if m == 0 else out[...] + got


def rim_kernel(late, par, total, up, down, x_out, y_out, z_out, left_a, left_b, *, thick, bit, block):
    members, _, _, count = late.shape
    _, half, depth = total.shape
    amp, rate = par[0:1], par[3:4]
    grids = spread_grids(half, depth, count, thick, bit, block)
    planes = [*range(RIM), *range(thick, thick + RIM)]
    lefts = (left_a, left_b)
    shape = (2 * RIM, half, depth)

    def build(m):
        x_amp, y_val, z_val = member_bells(late.at[m], amp, rate, grids)
        x_out[m], y_out[m], z_out[m] = x_amp, y_val, z_val
        layers(lefts[m % 2], x_amp, y_val, planes)

    down[...] = total[:RIM]
    up[...] = total[thick:]
    build(0)
    for m in range(members):
        if m + 1 < members:
            build(m + 1)
        got = product(lefts[m % 2], z_out[m], shape)
        down[...] += got[:RIM]
        up[...] += got[RIM:]


def middle_kernel(x_in, y_in, z_in, total, out, left_a, left_b, *, thick):
    planes = range(RIM, thick)
    lefts = (left_a, left_b)
    members = x_in.shape[0]
    layers(left_a, x_in[0], y_in[0], planes)
    for m in range(members):
        if m + 1 < members:
            layers(lefts[(m + 1) % 2], x_in[m + 1], y_in[m + 1], planes)
        got = product(lefts[m % 2], z_in[m], out.shape)
        out[...] = got + (total[RIM:thick] if m == 0 else out[...])


FIXED = float(2**25)


def fixed(v):
    whole = jnp.floor(v)
    return (whole.astype(jnp.int32) << 25) + ((v - whole) * FIXED).astype(jnp.int32)


def table_kernel(mine, par, low, high, place_x, place_y, place_z, load, *, n_x, base):
    cells = mine.shape[3] // CELL
    slabs = lax.axis_size("brick")
    brick = lax.axis_index("brick")
    ghosts = (low.shape[0] - base) // 4
    shift_low = jnp.where(brick == 0, -float(n_x), 0.0).astype(F32)
    shift_high = jnp.where(brick == slabs - 1, float(n_x), 0.0).astype(F32)

    def column(row):
        return jnp.broadcast_to(row, (CELL, CELL)).T

    def enter(n, x, y, z, q):
        at = slice(n * CELL, (n + 1) * CELL)
        place_x[at, :] = column(x * FIXED)
        place_y[at, :] = column(fixed(y))
        place_z[at, :] = column(fixed(z))
        load[at, :] = column(q)

    for c in range(cells):
        at = slice(c * CELL, (c + 1) * CELL)
        enter(c, mine[0, 0, :, at], mine[0, 1, :, at], mine[0, 2, :, at], par[1:2, at])
    for n, (ref, shift) in enumerate(((low, shift_low), (high, shift_high))):
        for g in range(ghosts):
            row = [ref[base + k * ghosts + g : base + k * ghosts + g + 1, :] for k in range(4)]
            enter(cells + n * ghosts + g, row[0] + shift, row[1], row[2], row[3])


def pair_kernel(after, mine, par, place_x, place_y, place_z, load, lists, live, out, *, first):
    del after
    for c in range(first, first + out.shape[1] // CELL):
        at = slice(c * CELL, (c + 1) * CELL)
        xi = jnp.broadcast_to(mine[0, 0, :, at] * FIXED, (8, CELL))
        yi = jnp.broadcast_to(fixed(mine[0, 1, :, at]), (8, CELL))
        zi = jnp.broadcast_to(fixed(mine[0, 2, :, at]), (8, CELL))

        def slot(s, total, c=c, xi=xi, yi=yi, zi=zi):
            start = pl.multiple_of(lists[c, s] * CELL, CELL)
            tx, ty, tz = total
            for g in range(CELL // 8):
                here = pl.ds(start + g * 8, 8)
                dx = xi - place_x[here, :]
                dy = (yi - place_y[here, :]).astype(F32)
                dz = (zi - place_z[here, :]).astype(F32)
                dist = dx * dx + dy * dy + (dz * dz + softening * FIXED * FIXED)
                inv = lax.rsqrt(dist)
                w = load[here, :] * inv * (inv * inv)
                tx, ty, tz = tx + w * dx, ty + w * dy, tz + w * dz
            return tx, ty, tz

        def two_slots(n, total, slot=slot):
            return slot(2 * n + 1, slot(2 * n, total))

        zero = jnp.zeros((8, CELL), F32)
        pairs = live[c] // 2
        total = lax.fori_loop(0, pairs, two_slots, (zero, zero, zero))
        total = lax.fori_loop(2 * pairs, live[c], slot, total)
        factor = (coupling * FIXED * FIXED) * par[1:2, at]
        here = slice((c - first) * CELL, (c - first + 1) * CELL)
        for k in range(3):
            out[k : k + 1, here] = factor * jnp.sum(total[k], axis=0, keepdims=True)


def member_force(place, par, grad, out, *, planes, half, thick, bit, block):
    count = par.shape[1]
    depth = grad.shape[1]
    x_grid, y_grid, z_grid = spread_grids(half, depth, CELL, thick, bit, block)
    for t in range(count // CELL):
        at = slice(t * CELL, (t + 1) * CELL)
        inv_var, rate = par[2:3, at], par[3:4, at]
        x_val, x_der = bell_slope(x_grid, place[0, :, at], inv_var, rate)
        y_val, y_der = bell_slope(y_grid, place[1, :, at], inv_var, rate, 2 * half)
        z_val, z_der = bell_slope(z_grid, place[2, :, at], inv_var, rate, depth)
        z_pair = jnp.concatenate([z_val, z_der], 1).astype(BF16)
        got = jnp.dot(grad[...], z_pair, preferred_element_type=F32)
        sums = [jnp.zeros((8, CELL), F32) for _ in range(3)]
        for i in range(planes):
            part = [jnp.zeros((8, CELL), F32) for _ in range(3)]
            for g in range(half // 8):
                j = slice(g * 8, (g + 1) * 8)
                k = slice(i * half + g * 8, i * half + (g + 1) * 8)
                along, across = got[k, :CELL], got[k, CELL:]
                part[0] += y_val[j] * along
                part[1] += y_der[j] * along
                part[2] += y_val[j] * across
            sums[0] += x_der[i : i + 1] * part[0]
            sums[1] += x_val[i : i + 1] * part[1]
            sums[2] += x_val[i : i + 1] * part[2]
        for k in range(3):
            out[k : k + 1, at] = -par[0:1, at] * jnp.sum(sums[k], axis=0, keepdims=True)


def grad_kernel(
    after, late, par, down, up, middle, low, high, near_low, near_high, obs, weight,
    dev_out, grad, partner_out, obs_s, weight_s, dev_s, sem, *, thick, bit, share, members,
):
    del after
    _, half, _ = middle.shape
    planes = thick + 2 * HALO
    block = obs.shape[3]
    member = lax.axis_index("replica")
    own = (member >> bit) & 1
    copies = []
    for source, target in ((obs, obs_s), (weight, weight_s)):
        for q in range(half // block):
            copies.append(
                pltpu.make_async_copy(
                    source.at[:, q, own],
                    target.at[pl.ds(HALO, thick), pl.ds(q * block, block)],
                    sem.at[len(copies)],
                )
            )
            copies[-1].start()
    for ref, first in ((near_low, 0), (near_high, thick + HALO)):
        for plane in range(HALO):
            obs_s[first + plane] = ref[plane * half : (plane + 1) * half, :]
            at = (HALO + plane) * half
            weight_s[first + plane] = ref[at : at + half, :]
    for copy in copies:
        copy.wait()
    for i in range(planes):
        if i < RIM:
            summed = down[i] + low[i]
        elif i >= thick:
            summed = up[i - thick] + high[i - thick]
        else:
            summed = middle[i - RIM]
        dev = summed / members - obs_s[i]
        grad[i * half : (i + 1) * half, :] = (restraint * weight_s[i] * dev).astype(BF16)
        if HALO <= i < thick + HALO:
            dev_s[i - HALO] = dev
    first_row = member * share
    spot = (first_row // (2 * block)) * block + first_row % block
    for n in range(half // share):

        @pl.when(spot == n * share)
        def _(n=n):
            dev_out[...] = dev_s[:, n * share : (n + 1) * share, :]

    member_force(
        late.at[0], par, grad, partner_out, planes=planes, half=half, thick=thick, bit=bit, block=block
    )


def force_kernel(mine, par, grad, out, *, thick, bit, block):
    planes = thick + 2 * HALO
    half = grad.shape[0] // planes
    member_force(
        mine.at[0], par, grad, out, planes=planes, half=half, thick=thick, bit=bit, block=block
    )


def kick_kernel(own, other, short_a, short_b, par, speed, v_half, part):
    mass = par[4:5]
    energy = jnp.zeros_like(mass)
    for k in range(3):
        short = jnp.concatenate([short_a[k : k + 1], short_b[k : k + 1]], 1)
        force = own[k : k + 1] + other[k : k + 1] + short
        v = speed[k] + timestep * force / mass
        v_half[k : k + 1] = v
        energy = energy + mass * v * v
    part[...] = jnp.broadcast_to(jnp.sum(energy, axis=1, keepdims=True), part.shape)


def drift_kernel(*refs, freedom):
    parts, (v_half, coords, warmth, place_out, speed_out) = refs[:-5], refs[-5:]
    kinetic = parts[0][0:1]
    for part in parts[1:]:
        kinetic = kinetic + part[0:1]
    present_moment = kinetic / (freedom * boltzmann) + 1e-06
    ratio = jnp.sqrt(
        1.0 + heat_bath_damping * (warmth[0].astype(F32) / present_moment - 1.0)
    )
    ratio = jnp.concatenate([ratio] * (v_half.shape[1] // ratio.shape[1]), 1)
    for k in range(3):
        v = ratio * v_half[k : k + 1]
        speed_out[k] = v
        place_out[k] = coords[0, k] + timestep * v


def local(
    atom_locations,
    atom_speeds_vector,
    inertial_amounts,
    electric_loads,
    scatter_strengths,
    gaussian_spreads_sigma,
    atom_present_flags,
    observed_volume_values,
    voxel_reciprocal_spread,
    paired_partner_lists,
    cell_usage_tally,
    halo_sender_spots,
    target_warmth_levels,
):
    thick, rows, depth = observed_volume_values.shape
    slabs = lax.axis_size("brick")
    members = lax.axis_size("replica")
    n_x = thick * slabs
    coords = jnp.transpose(atom_locations, (1, 0, 2))
    speeds = jnp.transpose(atom_speeds_vector, (1, 0, 2))
    count = coords.shape[2]
    planes = thick + 2 * HALO
    share, bit, block = row_class(rows, members)
    half = rows // 2
    base = 2 * HALO * half
    ghosts = halo_sender_spots.shape[1]
    near_rows = base + 4 * ghosts // CELL
    assert slabs >= 4 and thick >= RIM

    mine = coords[None]
    groups = [mine]
    masks = [m for m in (1 << n for n in range(members.bit_length() - 1)) if m != 1 << bit]
    order = masks[::-1] + [1 << bit]
    for mask in order:
        known = jnp.concatenate(groups) if len(groups) > 1 else mine
        groups.append(lax.ppermute(known, "replica", [(i, i ^ mask) for i in range(members)]))
    late = groups.pop()
    obs = observed_volume_values.reshape(thick, half // block, 2, block, depth)
    weight = voxel_reciprocal_spread.reshape(thick, half // block, 2, block, depth)
    near = jax.ShapeDtypeStruct((near_rows, CELL), F32)
    par, near_up, near_down = pl.pallas_call(
        functools.partial(prep_kernel, thick=thick, bit=bit, half=half),
        out_shape=(jax.ShapeDtypeStruct((8, count), F32), near, near),
        in_specs=[VMEM] + [HBM] * 8,
        out_specs=(VMEM, VMEM, VMEM),
        scratch_shapes=[
            pltpu.VMEM((1, count), jnp.int32),
            pltpu.VMEM((4, 1, count), F32),
            pltpu.VMEM((2, ghosts), jnp.int32),
            pltpu.SemaphoreType.DMA((6,)),
            pltpu.SemaphoreType.DMA((4 * HALO * (half // block),)),
        ],
        compiler_params=pltpu.CompilerParams(vmem_limit_bytes=64800 << 10),
        cost_estimate=cost(1),
        name="prep",
    )(
        mine,
        atom_present_flags,
        scatter_strengths,
        electric_loads,
        gaussian_spreads_sigma,
        inertial_amounts,
        halo_sender_spots,
        obs,
        weight,
    )

    ring = [(i, (i + 1) % slabs) for i in range(slabs)]
    back = [(target, source) for source, target in ring]
    near_low = lax.ppermute(near_up, "brick", ring)
    near_high = lax.ppermute(near_down, "brick", back)

    rim = jax.ShapeDtypeStruct((RIM, half, depth), F32)
    place = dict(thick=thick, bit=bit, block=block)
    total = pl.pallas_call(
        functools.partial(early_kernel, **place),
        out_shape=jax.ShapeDtypeStruct((planes, half, depth), F32),
        in_specs=[VMEM] * (len(groups) + 1),
        out_specs=VMEM,
        scratch_shapes=[pltpu.VMEM((planes * half, count), BF16)] * 2
        + [pltpu.VMEM((depth, count), BF16)] * 2,
        compiler_params=limit(12),
        cost_estimate=cost(2),
        name="early",
    )(*groups, par)
    held = late.shape[0]
    rim_up, rim_down, x_late, y_late, z_late = pl.pallas_call(
        functools.partial(rim_kernel, **place),
        out_shape=(
            rim,
            rim,
            jax.ShapeDtypeStruct((held, 16, count), F32),
            jax.ShapeDtypeStruct((held, half, count), F32),
            jax.ShapeDtypeStruct((held, depth, count), BF16),
        ),
        in_specs=[VMEM] * 3,
        out_specs=(VMEM,) * 5,
        scratch_shapes=[pltpu.VMEM((2 * RIM * half, count), BF16)] * 2,
        compiler_params=limit(12),
        cost_estimate=cost(2),
        name="rim",
    )(late, par, total)
    low = lax.ppermute(rim_up, "brick", ring)
    high = lax.ppermute(rim_down, "brick", back)
    middle = pl.pallas_call(
        functools.partial(middle_kernel, thick=thick),
        out_shape=jax.ShapeDtypeStruct((thick - RIM, half, depth), F32),
        in_specs=[VMEM] * 4,
        out_specs=VMEM,
        scratch_shapes=[pltpu.VMEM(((thick - RIM) * half, count), BF16)] * 2,
        compiler_params=limit(12),
        cost_estimate=cost(1),
        name="middle",
    )(x_late, y_late, z_late, total)

    blocks = count // CELL + 2 * ghosts // CELL
    table = jax.ShapeDtypeStruct((blocks * CELL, CELL), F32)
    table_int = jax.ShapeDtypeStruct((blocks * CELL, CELL), jnp.int32)
    tables = pl.pallas_call(
        functools.partial(table_kernel, n_x=n_x, base=base),
        out_shape=(table, table_int, table_int, table),
        in_specs=[VMEM] * 4,
        out_specs=(VMEM,) * 4,
        compiler_params=limit(6),
        cost_estimate=cost(1),
        name="table",
    )(mine, par, near_low, near_high)

    def pair(after, first, cells):
        return pl.pallas_call(
            functools.partial(pair_kernel, first=first),
            out_shape=jax.ShapeDtypeStruct((3, cells * CELL), F32),
            in_specs=[VMEM] * 7 + [SMEM] * 2,
            out_specs=VMEM,
            compiler_params=limit(6),
            cost_estimate=cost(2),
        )(after, mine, par, *tables, paired_partner_lists, cell_usage_tally)

    cells = count // CELL
    short_a = pair(par, 0, cells // 2)
    force = jax.ShapeDtypeStruct((3, count), F32)
    deviation, grad, partner = pl.pallas_call(
        functools.partial(grad_kernel, thick=thick, bit=bit, share=share, members=members),
        out_shape=(
            jax.ShapeDtypeStruct((thick, share, depth), F32),
            jax.ShapeDtypeStruct((planes * half, depth), BF16),
            force,
        ),
        in_specs=[VMEM] * 10 + [HBM, HBM],
        out_specs=(VMEM, VMEM, VMEM),
        scratch_shapes=[
            pltpu.VMEM((planes, half, depth), F32),
            pltpu.VMEM((planes, half, depth), F32),
            pltpu.VMEM((thick, half, depth), F32),
            pltpu.SemaphoreType.DMA((2 * (half // block),)),
        ],
        compiler_params=limit(12),
        cost_estimate=cost(2),
        name="grad",
    )(short_a, late, par, rim_down, rim_up, middle, low, high, near_low, near_high, obs, weight)

    swap = [(i, i ^ (1 << bit)) for i in range(members)]
    other = lax.ppermute(partner, "replica", swap)
    own = pl.pallas_call(
        functools.partial(force_kernel, **place),
        out_shape=force,
        in_specs=[VMEM] * 3,
        out_specs=VMEM,
        compiler_params=limit(8),
        cost_estimate=cost(1),
        name="force",
    )(mine, par, grad)
    short_b = pair(partner, cells // 2, cells - cells // 2)
    v_half, part = pl.pallas_call(
        kick_kernel,
        out_shape=(force, jax.ShapeDtypeStruct((8, CELL), F32)),
        in_specs=[VMEM] * 6,
        out_specs=(VMEM, VMEM),
        compiler_params=limit(2),
        name="kick",
    )(own, other, short_a, short_b, par, speeds)
    if slabs <= 4:
        parts = [part]
        for step in range(1, slabs):
            route = [(i, (i + step) % slabs) for i in range(slabs)]
            parts.append(lax.ppermute(part, "brick", route))
    else:
        parts = [lax.psum(part, "brick")]
    moved = jax.ShapeDtypeStruct((3, 1, count), F32)
    new_positions, new_velocities = pl.pallas_call(
        functools.partial(drift_kernel, freedom=3 * count * slabs),
        out_shape=(moved, moved),
        in_specs=[VMEM] * (len(parts) + 2) + [SMEM],
        out_specs=(VMEM, VMEM),
        compiler_params=limit(2),
        name="drift",
    )(*parts, v_half, mine, target_warmth_levels)
    return (
        jnp.transpose(new_positions, (1, 0, 2)),
        jnp.transpose(new_velocities, (1, 0, 2)),
        deviation,
    )


def solution(mesh):
    return jax.shard_map(
        local,
        mesh=mesh,
        in_specs=(
            P("replica", None, "brick"),
            P("replica", None, "brick"),
            P("brick"),
            P("brick"),
            P("brick"),
            P("brick"),
            P("brick"),
            P("brick", None, None),
            P("brick", None, None),
            P("brick", None),
            P("brick"),
            P(None, "brick"),
            P("replica"),
        ),
        out_specs=(
            P("replica", None, "brick"),
            P("replica", None, "brick"),
            P("brick", "replica", None),
        ),
        check_vma=False,
    )
```

```python
import functools
import math

import jax
import jax.numpy as jnp
from jax import lax
from jax.experimental import pallas as pl
from jax.experimental.pallas import tpu as pltpu
from jax.sharding import PartitionSpec as P

HALO = 2
CELL = 128
RIM = 2 * HALO

restraint = 0.1
coupling = 5.0
softening = 1.0
timestep = 0.5
boltzmann = 0.015
heat_bath_damping = 0.5

F32 = jnp.float32
BF16 = jnp.bfloat16
NT = (((1,), (1,)), ((), ()))
VMEM = pl.BlockSpec(memory_space=pltpu.VMEM)
SMEM = pl.BlockSpec(memory_space=pltpu.SMEM)
HBM = pl.BlockSpec(memory_space=pltpu.HBM)


def bell(grid, coord, rate, period=None):
    delta = grid - coord
    if period is not None:
        away = jnp.abs(delta)
        delta = jnp.minimum(away, period - away)
    return jnp.exp2(delta * delta * rate)


def bell_slope(grid, coord, inv_var, rate, period=None):
    delta = grid - coord
    if period is not None:
        delta = delta - period * jnp.floor(delta * (1.0 / period) + 0.5)
    value = jnp.exp2(delta * delta * rate)
    return value, delta * inv_var * value


def limit(mib):
    return pltpu.CompilerParams(vmem_limit_bytes=mib << 20)


def in_hbm(x):
    return pltpu.with_memory_space_constraint(x, pltpu.HBM)


def cost(us):
    return pl.CostEstimate(flops=us * 500_000_000, bytes_accessed=us * 1_000_000, transcendentals=0)


def iota(shape, dim):
    return lax.broadcasted_iota(jnp.int32, shape, dim)


def row_class(rows, members):
    share = rows // members
    bit = 0
    while (share << bit) % 8:
        bit += 1
    return share, bit, share << bit


def local_rows(shape, member, bit, block):
    row = iota(shape, 0)
    own = (member >> bit) & 1
    return ((row // block) * (2 * block) + own * block + row % block).astype(F32)


def prep_kernel(
    coords, speeds, flags, scatter, loads, sigma, mass, spots, lists, live, obs, weight,
    mine, speed_out, par, plan, up, down, obs_out, weight_out,
    flags_s, floats_s, spots_s, lists_s, live_s, small_sem, sem, row_sem, *, thick, bit, half,
):
    own = (lax.axis_index("replica") >> bit) & 1
    block = obs.shape[3]
    small = [
        pltpu.make_async_copy(flags, flags_s.at[0], small_sem.at[0]),
        pltpu.make_async_copy(spots, spots_s, small_sem.at[1]),
        pltpu.make_async_copy(coords, mine.at[0], small_sem.at[6]),
        pltpu.make_async_copy(speeds, speed_out, small_sem.at[9]),
        pltpu.make_async_copy(lists, lists_s, small_sem.at[7]),
        pltpu.make_async_copy(live, live_s, small_sem.at[8]),
    ]
    for n, source in enumerate((scatter, loads, sigma, mass)):
        small.append(pltpu.make_async_copy(source, floats_s.at[n, 0], small_sem.at[2 + n]))
    for copy in small:
        copy.start()
    copies = []
    deals = half // block
    for target, first in ((up, thick - HALO), (down, 0)):
        for n, source in enumerate((obs, weight)):
            for plane in range(HALO):
                copies.append(
                    pltpu.make_async_copy(
                        source.at[first + plane, :, own],
                        target.at[pl.ds((n * HALO + plane) * deals, deals)],
                        sem.at[len(copies)],
                    )
                )
                copies[-1].start()
    for source, target in ((obs, obs_out), (weight, weight_out)):
        for q in range(deals):
            copies.append(
                pltpu.make_async_copy(
                    source.at[:, q, own],
                    target.at[:, pl.ds(q * block, block)],
                    row_sem.at[len(copies) - 4 * HALO],
                )
            )
            copies[-1].start()
    for copy in small:
        copy.wait()
    occupancy = flags_s[...].astype(F32)
    inv_var = 1.0 / (floats_s[2] * floats_s[2])
    charge = occupancy * floats_s[1]
    par[0:1] = occupancy * floats_s[0]
    par[1:2] = charge
    par[2:3] = inv_var
    par[3:4] = (-0.5 * math.log2(math.e)) * inv_var
    par[4:5] = floats_s[3]
    data = jnp.concatenate([mine[0, 0], mine[0, 1], mine[0, 2], charge], 0)
    high = data.astype(BF16)
    rest = data - high.astype(F32)
    mid = rest.astype(BF16)
    low = (rest - mid.astype(F32)).astype(BF16)
    pieces = jnp.concatenate([high.astype(F32), mid.astype(F32), low.astype(F32)], 0).astype(BF16)
    count = data.shape[1]
    cells, slots = lists_s.shape
    lane, row = iota((8, CELL), 1), iota((8, CELL), 0)
    used = jnp.zeros((8, CELL), jnp.int32)
    for c in range(cells):
        used = jnp.where(row == c, live_s[c], used)
    listed = jnp.concatenate([lists_s[...], jnp.zeros((8 - cells, slots), jnp.int32)], 0)
    picked = [jnp.zeros((8, CELL), jnp.int32)] * 2
    length = [jnp.zeros((8, CELL), jnp.int32)] * 2
    for s in range(slots):
        block_of = jnp.broadcast_to(listed[:, s : s + 1], (8, CELL))
        for kind in range(2):
            takes = (s < used) & ((block_of < cells) if kind == 0 else (block_of >= cells))
            picked[kind] = jnp.where(takes & (lane == length[kind]), block_of - kind * cells, picked[kind])
            length[kind] = length[kind] + takes.astype(jnp.int32)
    for kind in range(2):
        plan[kind] = jnp.where(lane == COUNT_AT, length[kind], picked[kind])
    for side, target in enumerate((up, down)):
        chosen = spots_s[side : side + 1, :]
        pick = (iota((count, chosen.shape[1]), 0) == chosen).astype(F32).astype(BF16)
        got = jnp.dot(pieces, pick, preferred_element_type=F32)
        got = got[0:4] + got[4:8] + got[8:12]
        groups = chosen.shape[1] // CELL
        for n in range(4):
            for g in range(groups):
                row = n * groups + g
                target[2 * HALO * deals, row : row + 1, :] = got[
                    n : n + 1, g * CELL : (g + 1) * CELL
                ]
    for copy in copies:
        copy.wait()


def spread_grids(half, depth, count, thick, bit, block):
    first = lax.axis_index("brick") * thick - HALO
    x_grid = (iota((16, count), 0) + first).astype(F32)
    y_grid = local_rows((half, count), lax.axis_index("replica"), bit, block)
    z_grid = iota((depth, count), 0).astype(F32)
    return x_grid, y_grid, z_grid


def member_bells(place, amp, rate, grids):
    x_grid, y_grid, z_grid = grids
    x_amp = amp * bell(x_grid, place[0], rate)
    y_val = bell(y_grid, place[1], rate, 2 * y_grid.shape[0])
    z_val = bell(z_grid, place[2], rate, z_grid.shape[0]).astype(BF16)
    return x_amp, y_val, z_val


def layers(left, x_amp, y_val, planes):
    half = y_val.shape[0]
    for n, i in enumerate(planes):
        left[n * half : (n + 1) * half, :] = (x_amp[i : i + 1] * y_val).astype(BF16)


def product(left, z_val, shape):
    return lax.dot_general(left[...], z_val, NT, preferred_element_type=F32).reshape(shape)


def early_kernel(*refs, thick, bit, block):
    groups, par, out, lefts, deeps = refs[:-6], refs[-6], refs[-5], refs[-4:-2], refs[-2:]
    planes, half, depth = out.shape
    count = par.shape[1]
    amp, rate = par[0:1], par[3:4]
    grids = spread_grids(half, depth, count, thick, bit, block)
    places = [(g, n) for g in groups for n in range(g.shape[0])]

    def build(m):
        g, n = places[m]
        x_amp, y_val, z_val = member_bells(g.at[n], amp, rate, grids)
        deeps[m % 2][...] = z_val
        layers(lefts[m % 2], x_amp, y_val, range(planes))

    build(0)
    for m in range(len(places)):
        if m + 1 < len(places):
            build(m + 1)
        got = product(lefts[m % 2], deeps[m % 2][...], out.shape)
        out[...] = got if m == 0 else out[...] + got


def rim_side(across, thick):
    odd = lax.axis_index("brick") % 2
    return thick * (odd if across else 1 - odd)


def pack_rim(rim, packet, base):
    packet[:RIM] = rim[...].astype(BF16)
    exact = rim[pl.ds(jnp.where(base == 0, 0, HALO), HALO)]
    packet[RIM:] = (exact - exact.astype(BF16).astype(F32)).astype(BF16)


def unpack_rim(packet, n, low):
    value = packet[n].astype(F32)
    extra = n - HALO if low else n
    return value + packet[RIM + extra].astype(F32) if 0 <= extra < HALO else value


def rim_bells(base, place, amp, rate, thick):
    first = lax.axis_index("brick") * thick - HALO + base
    grid = (iota((8, amp.shape[1]), 0) + first).astype(F32)
    return amp * bell(grid, place[0], rate)


def across_kernel(late, par, total, out, packet, x_out, y_out, z_out, left_a, left_b, *, thick, bit, block):
    members = late.shape[0]
    _, half, depth = total.shape
    amp, rate = par[0:1], par[3:4]
    grids = spread_grids(half, depth, par.shape[1], thick, bit, block)
    lefts = (left_a, left_b)
    base = rim_side(True, thick)

    def build(m):
        x_amp, y_val, z_val = member_bells(late.at[m], amp, rate, grids)
        x_out[m], y_out[m], z_out[m] = x_amp, y_val, z_val
        layers(lefts[m % 2], rim_bells(base, late.at[m], amp, rate, thick), y_val, range(RIM))

    build(0)
    for m in range(members):
        if m + 1 < members:
            build(m + 1)
        got = product(lefts[m % 2], z_out[m], out.shape)
        out[...] = got + (total[pl.ds(base, RIM)] if m == 0 else out[...])
    pack_rim(out, packet, base)


def beside_kernel(late, par, total, y_in, z_in, out, packet, left_a, left_b, *, thick):
    members = late.shape[0]
    amp, rate = par[0:1], par[3:4]
    lefts = (left_a, left_b)
    base = rim_side(False, thick)

    def build(m):
        layers(lefts[m % 2], rim_bells(base, late.at[m], amp, rate, thick), y_in[m], range(RIM))

    build(0)
    for m in range(members):
        if m + 1 < members:
            build(m + 1)
        got = product(lefts[m % 2], z_in[m], out.shape)
        out[...] = got + (total[pl.ds(base, RIM)] if m == 0 else out[...])
    pack_rim(out, packet, base)


FIXED = float(2**25)


def fixed(v):
    whole = jnp.floor(v)
    return (whole.astype(jnp.int32) << 25) + ((v - whole) * FIXED).astype(jnp.int32)


def enter(tables, n, x, y, z, q):
    at = slice(n * CELL, (n + 1) * CELL)
    for table, row in zip(tables, (x * FIXED, fixed(y), fixed(z), q)):
        table[at, :] = jnp.broadcast_to(row, (CELL, CELL)).T


def ghost_kernel(low, high, *tables, n_x, ghosts):
    slabs = lax.axis_size("brick")
    brick = lax.axis_index("brick")
    last = low.shape[0] - 1
    shift_low = jnp.where(brick == 0, -float(n_x), 0.0).astype(F32)
    shift_high = jnp.where(brick == slabs - 1, float(n_x), 0.0).astype(F32)
    for n, (ref, shift) in enumerate(((low, shift_low), (high, shift_high))):
        for g in range(ghosts):
            row = [ref[last, k * ghosts + g : k * ghosts + g + 1, :] for k in range(4)]
            enter(tables, n * ghosts + g, row[0] + shift, row[1], row[2], row[3])


def own_kernel(mine, par, plan, *refs):
    tables, (out, plan_s, sem) = refs[:4], refs[4:]
    copy = pltpu.make_async_copy(plan, plan_s, sem)
    copy.start()
    for c in range(mine.shape[3] // CELL):
        at = slice(c * CELL, (c + 1) * CELL)
        enter(tables, c, mine[0, 0, :, at], mine[0, 1, :, at], mine[0, 2, :, at], par[1:2, at])
    copy.wait()
    pair_cells(mine, par, [tables], [0], plan_s, out, 0)


COUNT_AT = 127


def pair_cells(mine, par, kinds, which, plan, out, first):
    for c in range(first, first + out.shape[1] // CELL):
        at = slice(c * CELL, (c + 1) * CELL)
        xi = jnp.broadcast_to(mine[0, 0, :, at] * FIXED, (8, CELL))
        yi = jnp.broadcast_to(fixed(mine[0, 1, :, at]), (8, CELL))
        zi = jnp.broadcast_to(fixed(mine[0, 2, :, at]), (8, CELL))
        zero = jnp.zeros((8, CELL), F32)
        total = (zero, zero, zero)
        for kind, tables in zip(which, kinds):
            place_x, place_y, place_z, load = tables

            def slot(s, total):
                start = pl.multiple_of(plan[kind, c, s] * CELL, CELL)
                tx, ty, tz = total
                for g in range(CELL // 8):
                    here = pl.ds(start + g * 8, 8)
                    dx = xi - place_x[here, :]
                    dy = (yi - place_y[here, :]).astype(F32)
                    dz = (zi - place_z[here, :]).astype(F32)
                    dist = dx * dx + dy * dy + (dz * dz + softening * FIXED * FIXED)
                    inv = lax.rsqrt(dist)
                    w = load[here, :] * inv * (inv * inv)
                    tx, ty, tz = tx + w * dx, ty + w * dy, tz + w * dz
                return tx, ty, tz

            def two_slots(n, total):
                return slot(2 * n + 1, slot(2 * n, total))

            slots = plan[kind, c, COUNT_AT]
            total = lax.fori_loop(0, slots // 2, two_slots, total)
            total = lax.fori_loop(2 * (slots // 2), slots, slot, total)
        factor = (coupling * FIXED * FIXED) * par[1:2, at]
        here = slice((c - first) * CELL, (c - first + 1) * CELL)
        for k in range(3):
            out[k : k + 1, here] = factor * jnp.sum(total[k], axis=0, keepdims=True)


def middle_kernel(
    late, x_in, y_in, z_in, total, mine, par, plan, obs, weight, *refs, thick, bit, block, members
):
    ghosts, (dev_out, grad, partner_out, short, left_a, left_b, plan_s, sem) = refs[:4], refs[4:]
    copy = pltpu.make_async_copy(plan, plan_s, sem)
    copy.start()
    planes = range(RIM, thick)
    lefts = (left_a, left_b)
    held = x_in.shape[0]
    half = total.shape[1]
    layers(left_a, x_in[0], y_in[0], planes)
    for m in range(held):
        if m + 1 < held:
            layers(lefts[(m + 1) % 2], x_in[m + 1], y_in[m + 1], planes)
        got = product(lefts[m % 2], z_in[m], dev_out.shape)
        dev_out[...] = got + (total[RIM:thick] if m == 0 else dev_out[...])
    for n, i in enumerate(planes):
        dev = dev_out[n] / members - obs[i - HALO]
        dev_out[n] = dev
        grad[n * half : (n + 1) * half, :] = (restraint * weight[i - HALO] * dev).astype(BF16)
    member_force(
        late.at[0], par, grad, partner_out,
        planes=planes, half=half, thick=thick, bit=bit, block=block,
    )
    copy.wait()
    pair_cells(mine, par, [ghosts], [1], plan_s, short, 0)


def member_force(place, par, grad, out, *, planes, half, thick, bit, block, plus=None):
    count = par.shape[1]
    depth = grad.shape[1]
    x_grid, y_grid, z_grid = spread_grids(half, depth, CELL, thick, bit, block)
    for t in range(count // CELL):
        at = slice(t * CELL, (t + 1) * CELL)
        inv_var, rate = par[2:3, at], par[3:4, at]
        x_val, x_der = bell_slope(x_grid, place[0, :, at], inv_var, rate)
        y_val, y_der = bell_slope(y_grid, place[1, :, at], inv_var, rate, 2 * half)
        z_val, z_der = bell_slope(z_grid, place[2, :, at], inv_var, rate, depth)
        z_pair = jnp.concatenate([z_val, z_der], 1).astype(BF16)
        got = jnp.dot(grad[...], z_pair, preferred_element_type=F32)
        sums = [jnp.zeros((8, CELL), F32) for _ in range(3)]
        for n, i in enumerate(planes):
            part = [jnp.zeros((8, CELL), F32) for _ in range(3)]
            for g in range(half // 8):
                j = slice(g * 8, (g + 1) * 8)
                k = slice(n * half + g * 8, n * half + (g + 1) * 8)
                along, across = got[k, :CELL], got[k, CELL:]
                part[0] += y_val[j] * along
                part[1] += y_der[j] * along
                part[2] += y_val[j] * across
            sums[0] += x_der[i : i + 1] * part[0]
            sums[1] += x_val[i : i + 1] * part[1]
            sums[2] += x_val[i : i + 1] * part[2]
        for k in range(3):
            force = -par[0:1, at] * jnp.sum(sums[k], axis=0, keepdims=True)
            out[k : k + 1, at] = force if plus is None else force + plus[k : k + 1, at]


def grad_kernel(
    late, par, sent_y, got_y, sent_c, got_c, dev_middle, grad_middle, partner_middle,
    near_low, near_high, obs, weight,
    dev_out, grad, partner_out, grad_rim, dev_s, *, thick, bit, share, block, members,
):
    _, half, _ = dev_middle.shape
    deals = near_low.shape[0] // (2 * HALO)
    member = lax.axis_index("replica")

    def near_rows(ref, n, plane):
        at = (n * HALO + plane) * deals
        return jnp.concatenate([ref[at + q] for q in range(deals)], 0)

    even = lax.axis_index("brick") % 2 == 0
    rims = [*range(RIM), *range(thick, thick + RIM)]
    for at, i in enumerate(rims):
        low, n = i < RIM, at % RIM
        across = sent_y[n] + unpack_rim(got_y, n, low)
        beside = sent_c[n] + unpack_rim(got_c, n, low)
        summed = jnp.where(even == low, across, beside)
        if i < HALO:
            wanted, trust = near_rows(near_low, 0, i), near_rows(near_low, 1, i)
        elif i >= thick + HALO:
            beyond = i - thick - HALO
            wanted, trust = near_rows(near_high, 0, beyond), near_rows(near_high, 1, beyond)
        else:
            wanted, trust = obs[i - HALO], weight[i - HALO]
        dev = summed / members - wanted
        slope = (restraint * trust * dev).astype(BF16)
        grad_rim[at * half : (at + 1) * half, :] = slope
        grad[i * half : (i + 1) * half, :] = slope
        if HALO <= i < thick + HALO:
            dev_s[i - HALO] = dev
    grad[RIM * half : thick * half, :] = grad_middle[...]
    dev_s[RIM - HALO : thick - HALO] = dev_middle[...]
    first_row = member * share
    spot = (first_row // (2 * block)) * block + first_row % block
    for n in range(half // share):

        @pl.when(spot == n * share)
        def _(n=n):
            dev_out[...] = dev_s[:, n * share : (n + 1) * share, :]

    member_force(
        late.at[0], par, grad_rim, partner_out,
        planes=rims, half=half, thick=thick, bit=bit, block=block, plus=partner_middle,
    )


def force_kernel(grad, mine, par, plan, *refs, thick, bit, block, first):
    own, (out, short, plan_s, sem) = refs[:4], refs[4:]
    copy = pltpu.make_async_copy(plan, plan_s, sem)
    copy.start()
    planes = range(thick + 2 * HALO)
    half = grad.shape[0] // len(planes)
    member_force(
        mine.at[0], par, grad, out, planes=planes, half=half, thick=thick, bit=bit, block=block
    )
    copy.wait()
    pair_cells(mine, par, [own], [0], plan_s, short, first)


def kick_kernel(own, other, short_own, short_a, short_b, par, speed, v_half, part):
    mass = par[4:5]
    energy = jnp.zeros_like(mass)
    for k in range(3):
        short = jnp.concatenate([short_own[k : k + 1], short_b[k : k + 1]], 1)
        short = short + short_a[k : k + 1]
        force = own[k : k + 1] + other[k : k + 1] + short
        v = speed[k] + timestep * force / mass
        v_half[k : k + 1] = v
        energy = energy + mass * v * v
    part[...] = jnp.broadcast_to(jnp.sum(energy, axis=1, keepdims=True), part.shape)


def drift_kernel(*refs, freedom):
    parts, (v_half, coords, warmth, place_out, speed_out) = refs[:-5], refs[-5:]
    kinetic = parts[0][0:1]
    for part in parts[1:]:
        kinetic = kinetic + part[0:1]
    present_moment = kinetic / (freedom * boltzmann) + 1e-06
    ratio = jnp.sqrt(
        1.0 + heat_bath_damping * (warmth[0].astype(F32) / present_moment - 1.0)
    )
    ratio = jnp.concatenate([ratio] * (v_half.shape[1] // ratio.shape[1]), 1)
    for k in range(3):
        v = ratio * v_half[k : k + 1]
        speed_out[k] = v
        place_out[k] = coords[0, k] + timestep * v


def local(
    atom_locations,
    atom_speeds_vector,
    inertial_amounts,
    electric_loads,
    scatter_strengths,
    gaussian_spreads_sigma,
    atom_present_flags,
    observed_volume_values,
    voxel_reciprocal_spread,
    paired_partner_lists,
    cell_usage_tally,
    halo_sender_spots,
    target_warmth_levels,
):
    thick, rows, depth = observed_volume_values.shape
    slabs = lax.axis_size("brick")
    members = lax.axis_size("replica")
    n_x = thick * slabs
    coords = jnp.transpose(atom_locations, (1, 0, 2))
    speeds = jnp.transpose(atom_speeds_vector, (1, 0, 2))
    count = coords.shape[2]
    planes = thick + 2 * HALO
    share, bit, block = row_class(rows, members)
    half = rows // 2
    deals = half // block
    ghosts = halo_sender_spots.shape[1]
    assert 4 * ghosts // CELL <= block
    assert slabs >= 4 and slabs % 2 == 0 and thick >= RIM and count // CELL <= 8

    bits = [1 << n for n in range(members.bit_length() - 1) if n != bit][::-1]

    def hop(known, mask):
        return lax.ppermute(known, "replica", [(i, i ^ mask) for i in range(members)])

    first = hop(coords[None], bits[0])
    obs = in_hbm(observed_volume_values.reshape(thick, deals, 2, block, depth))
    weight = in_hbm(voxel_reciprocal_spread.reshape(thick, deals, 2, block, depth))
    near = jax.ShapeDtypeStruct((2 * HALO * deals + 1, block, CELL), F32)
    own_rows = jax.ShapeDtypeStruct((thick, half, depth), F32)
    mine, speed, par, plan, near_up, near_down, own_obs, own_weight = pl.pallas_call(
        functools.partial(prep_kernel, thick=thick, bit=bit, half=half),
        out_shape=(
            jax.ShapeDtypeStruct((1,) + coords.shape, F32),
            jax.ShapeDtypeStruct(speeds.shape, F32),
            jax.ShapeDtypeStruct((8, count), F32),
            jax.ShapeDtypeStruct((2, 8, CELL), jnp.int32),
            near,
            near,
            own_rows,
            own_rows,
        ),
        in_specs=[HBM] * 12,
        out_specs=(VMEM,) * 8,
        scratch_shapes=[
            pltpu.VMEM((1, count), jnp.int32),
            pltpu.VMEM((4, 1, count), F32),
            pltpu.VMEM((2, ghosts), jnp.int32),
            pltpu.VMEM(paired_partner_lists.shape, jnp.int32),
            pltpu.SMEM(cell_usage_tally.shape, jnp.int32),
            pltpu.SemaphoreType.DMA((10,)),
            pltpu.SemaphoreType.DMA((4 * HALO,)),
            pltpu.SemaphoreType.DMA((2 * deals,)),
        ],
        compiler_params=limit(4),
        cost_estimate=cost(1),
        name="prep",
    )(
        *(
            in_hbm(a)
            for a in (
                coords,
                speeds,
                atom_present_flags,
                scatter_strengths,
                electric_loads,
                gaussian_spreads_sigma,
                inertial_amounts,
                halo_sender_spots,
                paired_partner_lists,
                cell_usage_tally,
            )
        ),
        obs,
        weight,
    )
    groups = [mine, first]
    for mask in bits[1:]:
        groups.append(hop(jnp.concatenate(groups), mask))
    late = hop(jnp.concatenate(groups), 1 << bit)

    ring = [(i, (i + 1) % slabs) for i in range(slabs)]
    back = [(target, source) for source, target in ring]
    near_low = lax.ppermute(near_up, "brick", ring)
    near_high = lax.ppermute(near_down, "brick", back)

    cells = count // CELL
    now = 2 * cells // 3

    def tables(blocks):
        table = jax.ShapeDtypeStruct((blocks * CELL, CELL), F32)
        table_int = jax.ShapeDtypeStruct((blocks * CELL, CELL), jnp.int32)
        return table, table_int, table_int, table

    planned = [pltpu.SMEM(plan.shape, jnp.int32), pltpu.SemaphoreType.DMA]
    *own_tables, short_own = pl.pallas_call(
        own_kernel,
        out_shape=(*tables(cells), jax.ShapeDtypeStruct((3, now * CELL), F32)),
        in_specs=[VMEM] * 3,
        out_specs=(VMEM,) * 5,
        scratch_shapes=planned,
        compiler_params=limit(6),
        cost_estimate=cost(2),
        name="own_pairs",
    )(mine, par, plan)
    ghost_tables = pl.pallas_call(
        functools.partial(ghost_kernel, n_x=n_x, ghosts=ghosts // CELL),
        out_shape=tables(2 * ghosts // CELL),
        in_specs=[VMEM] * 2,
        out_specs=(VMEM,) * 4,
        compiler_params=limit(6),
        cost_estimate=cost(1),
        name="ghosts",
    )(near_low, near_high)

    place = dict(thick=thick, bit=bit, block=block)
    total = pl.pallas_call(
        functools.partial(early_kernel, **place),
        out_shape=jax.ShapeDtypeStruct((planes, half, depth), F32),
        in_specs=[VMEM] * (len(groups) + 1),
        out_specs=VMEM,
        scratch_shapes=[pltpu.VMEM((planes * half, count), BF16)] * 2
        + [pltpu.VMEM((depth, count), BF16)] * 2,
        compiler_params=limit(12),
        cost_estimate=cost(2),
        name="early",
    )(*groups, par)
    held = late.shape[0]
    rim = jax.ShapeDtypeStruct((RIM, half, depth), F32)
    packet = jax.ShapeDtypeStruct((RIM + HALO, half, depth), BF16)
    sent_y, packet_y, x_late, y_late, z_late = pl.pallas_call(
        functools.partial(across_kernel, **place),
        out_shape=(
            rim,
            packet,
            jax.ShapeDtypeStruct((held, 16, count), F32),
            jax.ShapeDtypeStruct((held, half, count), F32),
            jax.ShapeDtypeStruct((held, depth, count), BF16),
        ),
        in_specs=[VMEM] * 3,
        out_specs=(VMEM,) * 5,
        scratch_shapes=[pltpu.VMEM((RIM * half, count), BF16)] * 2,
        compiler_params=limit(12),
        cost_estimate=cost(1),
        name="across",
    )(late, par, total)
    route = [(i, (i + 1 if i % 2 else i - 1) % slabs) for i in range(slabs)]
    got_y = lax.ppermute(packet_y, "brick", route)
    sent_c, packet_c = pl.pallas_call(
        functools.partial(beside_kernel, thick=thick),
        out_shape=(rim, packet),
        in_specs=[VMEM] * 5,
        out_specs=(VMEM, VMEM),
        scratch_shapes=[pltpu.VMEM((RIM * half, count), BF16)] * 2,
        compiler_params=limit(12),
        cost_estimate=cost(1),
        name="beside",
    )(late, par, total, y_late, z_late)
    got_c = lax.ppermute(packet_c, "brick", [(i, i ^ 1) for i in range(slabs)])
    force = jax.ShapeDtypeStruct((3, count), F32)
    inner = thick - RIM
    dev_middle, grad_middle, partner_middle, short_a = pl.pallas_call(
        functools.partial(middle_kernel, **place, members=members),
        out_shape=(
            jax.ShapeDtypeStruct((inner, half, depth), F32),
            jax.ShapeDtypeStruct((inner * half, depth), BF16),
            force,
            force,
        ),
        in_specs=[VMEM] * 14,
        out_specs=(VMEM,) * 4,
        scratch_shapes=[pltpu.VMEM((inner * half, count), BF16)] * 2 + planned,
        compiler_params=limit(12),
        cost_estimate=cost(2),
        name="middle",
    )(late, x_late, y_late, z_late, total, mine, par, plan, own_obs, own_weight, *ghost_tables)
    deviation, grad, partner = pl.pallas_call(
        functools.partial(grad_kernel, **place, share=share, members=members),
        out_shape=(
            jax.ShapeDtypeStruct((thick, share, depth), F32),
            jax.ShapeDtypeStruct((planes * half, depth), BF16),
            force,
        ),
        in_specs=[VMEM] * 13,
        out_specs=(VMEM, VMEM, VMEM),
        scratch_shapes=[
            pltpu.VMEM((2 * RIM * half, depth), BF16),
            pltpu.VMEM((thick, half, depth), F32),
        ],
        compiler_params=limit(12),
        cost_estimate=cost(1),
        name="grad",
    )(
        late, par, sent_y, got_y, sent_c, got_c, dev_middle, grad_middle, partner_middle,
        near_low, near_high, own_obs, own_weight,
    )

    swap = [(i, i ^ (1 << bit)) for i in range(members)]
    other = lax.ppermute(partner, "replica", swap)
    own, short_b = pl.pallas_call(
        functools.partial(force_kernel, **place, first=now),
        out_shape=(force, jax.ShapeDtypeStruct((3, count - now * CELL), F32)),
        in_specs=[VMEM] * 8,
        out_specs=(VMEM, VMEM),
        scratch_shapes=planned,
        compiler_params=limit(8),
        cost_estimate=cost(2),
        name="force",
    )(grad, mine, par, plan, *own_tables)
    v_half, part = pl.pallas_call(
        kick_kernel,
        out_shape=(force, jax.ShapeDtypeStruct((8, CELL), F32)),
        in_specs=[VMEM] * 7,
        out_specs=(VMEM, VMEM),
        compiler_params=limit(2),
        name="kick",
    )(own, other, short_own, short_a, short_b, par, speed)
    if slabs <= 4:
        parts = [part]
        for step in range(1, slabs):
            route = [(i, (i + step) % slabs) for i in range(slabs)]
            parts.append(lax.ppermute(part, "brick", route))
    else:
        parts = [lax.psum(part, "brick")]
    moved = jax.ShapeDtypeStruct((3, 1, count), F32)
    new_positions, new_velocities = pl.pallas_call(
        functools.partial(drift_kernel, freedom=3 * count * slabs),
        out_shape=(moved, moved),
        in_specs=[VMEM] * (len(parts) + 2) + [SMEM],
        out_specs=(VMEM, VMEM),
        compiler_params=limit(2),
        name="drift",
    )(*parts, v_half, mine, target_warmth_levels)
    return (
        jnp.transpose(new_positions, (1, 0, 2)),
        jnp.transpose(new_velocities, (1, 0, 2)),
        deviation,
    )


def solution(mesh):
    return jax.shard_map(
        local,
        mesh=mesh,
        in_specs=(
            P("replica", None, "brick"),
            P("replica", None, "brick"),
            P("brick"),
            P("brick"),
            P("brick"),
            P("brick"),
            P("brick"),
            P("brick", None, None),
            P("brick", None, None),
            P("brick", None),
            P("brick"),
            P(None, "brick"),
            P("replica"),
        ),
        out_specs=(
            P("replica", None, "brick"),
            P("replica", None, "brick"),
            P("brick", "replica", None),
        ),
        check_vma=False,
    )
```

```python
import functools
import math

import jax
import jax.numpy as jnp
from jax import lax
from jax.experimental import pallas as pl
from jax.experimental.pallas import tpu as pltpu
from jax.sharding import PartitionSpec as P

HALO = 2
CELL = 128
RIM = 2 * HALO

restraint = 0.1
coupling = 5.0
softening = 1.0
timestep = 0.5
boltzmann = 0.015
heat_bath_damping = 0.5

F32 = jnp.float32
BF16 = jnp.bfloat16
NT = (((1,), (1,)), ((), ()))
VMEM = pl.BlockSpec(memory_space=pltpu.VMEM)
SMEM = pl.BlockSpec(memory_space=pltpu.SMEM)
HBM = pl.BlockSpec(memory_space=pltpu.HBM)


def fixed(v, unit):
    whole = jnp.floor(v)
    part = ((v - whole) * float(unit)).astype(jnp.int32)
    return (whole.astype(jnp.int32) << (unit.bit_length() - 1)) + part


def bell(grid, coord, rate):
    delta = grid - coord
    return jnp.exp2(delta * delta * rate)


def ring_bell(grid, coord, rate, unit):
    delta = (grid - fixed(coord, unit)).astype(F32)
    return jnp.exp2(delta * delta * (rate * (1.0 / unit / unit)))


def bell_slope(grid, coord, inv_var, rate):
    delta = grid - coord
    value = jnp.exp2(delta * delta * rate)
    return value, delta * inv_var * value


def ring_bell_slope(grid, coord, inv_var, rate, unit):
    delta = (grid - fixed(coord, unit)).astype(F32)
    value = jnp.exp2(delta * delta * (rate * (1.0 / unit / unit)))
    return value, delta * (inv_var * (1.0 / unit)) * value


def limit(mib):
    return pltpu.CompilerParams(vmem_limit_bytes=mib << 20)


def in_hbm(x):
    return pltpu.with_memory_space_constraint(x, pltpu.HBM)


def cost(us):
    return pl.CostEstimate(flops=us * 500_000_000, bytes_accessed=us * 1_000_000, transcendentals=0)


def iota(shape, dim):
    return lax.broadcasted_iota(jnp.int32, shape, dim)


def row_class(rows, members):
    share = rows // members
    bit = 0
    while (share << bit) % 8:
        bit += 1
    return share, bit, share << bit


def local_rows(shape, member, bit, block):
    row = iota(shape, 0)
    own = (member >> bit) & 1
    return (row // block) * (2 * block) + own * block + row % block


def prep_kernel(
    coords, speeds, flags, scatter, loads, sigma, mass, spots, lists, live, obs, weight,
    mine, speed_out, par, plan, up, down, obs_out, weight_out,
    flags_s, floats_s, spots_s, lists_s, live_s, small_sem, sem, row_sem, *, thick, bit, half,
):
    own = (lax.axis_index("replica") >> bit) & 1
    block = obs.shape[3]
    small = [
        pltpu.make_async_copy(flags, flags_s.at[0], small_sem.at[0]),
        pltpu.make_async_copy(spots, spots_s, small_sem.at[1]),
        pltpu.make_async_copy(coords, mine.at[0], small_sem.at[6]),
        pltpu.make_async_copy(speeds, speed_out, small_sem.at[9]),
        pltpu.make_async_copy(lists, lists_s, small_sem.at[7]),
        pltpu.make_async_copy(live, live_s, small_sem.at[8]),
    ]
    for n, source in enumerate((scatter, loads, sigma, mass)):
        small.append(pltpu.make_async_copy(source, floats_s.at[n, 0], small_sem.at[2 + n]))
    for copy in small:
        copy.start()
    copies = []
    deals = half // block
    for target, first in ((up, thick - HALO), (down, 0)):
        for n, source in enumerate((obs, weight)):
            for plane in range(HALO):
                copies.append(
                    pltpu.make_async_copy(
                        source.at[first + plane, :, own],
                        target.at[pl.ds((n * HALO + plane) * deals, deals)],
                        sem.at[len(copies)],
                    )
                )
                copies[-1].start()
    for source, target in ((obs, obs_out), (weight, weight_out)):
        for q in range(deals):
            copies.append(
                pltpu.make_async_copy(
                    source.at[:, q, own],
                    target.at[:, pl.ds(q * block, block)],
                    row_sem.at[len(copies) - 4 * HALO],
                )
            )
            copies[-1].start()
    for copy in small:
        copy.wait()
    occupancy = flags_s[...].astype(F32)
    inv_var = 1.0 / (floats_s[2] * floats_s[2])
    charge = occupancy * floats_s[1]
    par[0:1] = occupancy * floats_s[0]
    par[1:2] = charge
    par[2:3] = inv_var
    par[3:4] = (-0.5 * math.log2(math.e)) * inv_var
    par[4:5] = floats_s[3]
    data = jnp.concatenate([mine[0, 0], mine[0, 1], mine[0, 2], charge], 0)
    high = data.astype(BF16)
    rest = data - high.astype(F32)
    mid = rest.astype(BF16)
    low = (rest - mid.astype(F32)).astype(BF16)
    pieces = jnp.concatenate([high.astype(F32), mid.astype(F32), low.astype(F32)], 0).astype(BF16)
    count = data.shape[1]
    cells, slots = lists_s.shape
    lane, row = iota((8, CELL), 1), iota((8, CELL), 0)
    used = jnp.zeros((8, CELL), jnp.int32)
    for c in range(cells):
        used = jnp.where(row == c, live_s[c], used)
    listed = jnp.concatenate([lists_s[...], jnp.zeros((8 - cells, slots), jnp.int32)], 0)
    picked = [jnp.zeros((8, CELL), jnp.int32)] * 2
    length = [jnp.zeros((8, CELL), jnp.int32)] * 2
    for s in range(slots):
        block_of = jnp.broadcast_to(listed[:, s : s + 1], (8, CELL))
        for kind in range(2):
            takes = (s < used) & ((block_of < cells) if kind == 0 else (block_of >= cells))
            picked[kind] = jnp.where(takes & (lane == length[kind]), block_of - kind * cells, picked[kind])
            length[kind] = length[kind] + takes.astype(jnp.int32)
    for kind in range(2):
        plan[kind] = jnp.where(lane == COUNT_AT, length[kind], picked[kind])
    for side, target in enumerate((up, down)):
        chosen = spots_s[side : side + 1, :]
        pick = (iota((count, chosen.shape[1]), 0) == chosen).astype(F32).astype(BF16)
        got = jnp.dot(pieces, pick, preferred_element_type=F32)
        got = got[0:4] + got[4:8] + got[8:12]
        groups = chosen.shape[1] // CELL
        for n in range(4):
            for g in range(groups):
                row = n * groups + g
                target[2 * HALO * deals, row : row + 1, :] = got[
                    n : n + 1, g * CELL : (g + 1) * CELL
                ]
    for copy in copies:
        copy.wait()


def ring_unit(period):
    unit = 2**32 // period
    assert unit * period == 2**32
    return unit


def spread_grids(half, depth, count, thick, bit, block):
    first = lax.axis_index("brick") * thick - HALO
    x_grid = (iota((16, count), 0) + first).astype(F32)
    y_grid = local_rows((half, count), lax.axis_index("replica"), bit, block) * ring_unit(2 * half)
    z_grid = iota((depth, count), 0) * ring_unit(depth)
    return x_grid, y_grid, z_grid


def member_bells(place, amp, rate, grids):
    x_grid, y_grid, z_grid = grids
    x_amp = amp * bell(x_grid, place[0], rate)
    y_val = ring_bell(y_grid, place[1], rate, ring_unit(2 * y_grid.shape[0]))
    z_val = ring_bell(z_grid, place[2], rate, ring_unit(z_grid.shape[0])).astype(BF16)
    return x_amp, y_val, z_val


def layers(left, x_amp, y_val, planes):
    half = y_val.shape[0]
    for n, i in enumerate(planes):
        left[n * half : (n + 1) * half, :] = (x_amp[i : i + 1] * y_val).astype(BF16)


def product(left, z_val, shape):
    return lax.dot_general(left[...], z_val, NT, preferred_element_type=F32).reshape(shape)


def early_kernel(*refs, thick, bit, block):
    groups, par, out, lefts, deeps = refs[:-6], refs[-6], refs[-5], refs[-4:-2], refs[-2:]
    planes, half, depth = out.shape
    count = par.shape[1]
    amp, rate = par[0:1], par[3:4]
    grids = spread_grids(half, depth, count, thick, bit, block)
    places = [(g, n) for g in groups for n in range(g.shape[0])]

    def build(m):
        g, n = places[m]
        x_amp, y_val, z_val = member_bells(g.at[n], amp, rate, grids)
        deeps[m % 2][...] = z_val
        layers(lefts[m % 2], x_amp, y_val, range(planes))

    build(0)
    for m in range(len(places)):
        if m + 1 < len(places):
            build(m + 1)
        got = product(lefts[m % 2], deeps[m % 2][...], out.shape)
        out[...] = got if m == 0 else out[...] + got


def rim_side(across, thick):
    odd = lax.axis_index("brick") % 2
    return thick * (odd if across else 1 - odd)


def pack_rim(rim, packet, base):
    packet[:RIM] = rim[...].astype(BF16)
    exact = rim[pl.ds(jnp.where(base == 0, 0, HALO), HALO)]
    packet[RIM:] = (exact - exact.astype(BF16).astype(F32)).astype(BF16)


def unpack_rim(packet, n, low):
    value = packet[n].astype(F32)
    extra = n - HALO if low else n
    return value + packet[RIM + extra].astype(F32) if 0 <= extra < HALO else value


def rim_bells(base, place, amp, rate, thick):
    first = lax.axis_index("brick") * thick - HALO + base
    grid = (iota((8, amp.shape[1]), 0) + first).astype(F32)
    return amp * bell(grid, place[0], rate)


def across_kernel(late, par, total, out, packet, x_out, y_out, z_out, left_a, left_b, *, thick, bit, block):
    members = late.shape[0]
    _, half, depth = total.shape
    amp, rate = par[0:1], par[3:4]
    grids = spread_grids(half, depth, par.shape[1], thick, bit, block)
    lefts = (left_a, left_b)
    base = rim_side(True, thick)

    def build(m):
        x_amp, y_val, z_val = member_bells(late.at[m], amp, rate, grids)
        x_out[m], y_out[m], z_out[m] = x_amp, y_val, z_val
        layers(lefts[m % 2], rim_bells(base, late.at[m], amp, rate, thick), y_val, range(RIM))

    build(0)
    for m in range(members):
        if m + 1 < members:
            build(m + 1)
        got = product(lefts[m % 2], z_out[m], out.shape)
        out[...] = got + (total[pl.ds(base, RIM)] if m == 0 else out[...])
    pack_rim(out, packet, base)


def beside_kernel(late, par, total, y_in, z_in, out, packet, left_a, left_b, *, thick):
    members = late.shape[0]
    amp, rate = par[0:1], par[3:4]
    lefts = (left_a, left_b)
    base = rim_side(False, thick)

    def build(m):
        layers(lefts[m % 2], rim_bells(base, late.at[m], amp, rate, thick), y_in[m], range(RIM))

    build(0)
    for m in range(members):
        if m + 1 < members:
            build(m + 1)
        got = product(lefts[m % 2], z_in[m], out.shape)
        out[...] = got + (total[pl.ds(base, RIM)] if m == 0 else out[...])
    pack_rim(out, packet, base)


def enter(tables, n, x, y, z, q, unit):
    at = slice(n * CELL, (n + 1) * CELL)
    for table, row in zip(tables, (x * float(unit), fixed(y, unit), fixed(z, unit), q)):
        table[at, :] = jnp.broadcast_to(row, (CELL, CELL)).T


def ghost_kernel(low, high, *tables, n_x, ghosts, unit):
    slabs = lax.axis_size("brick")
    brick = lax.axis_index("brick")
    last = low.shape[0] - 1
    shift_low = jnp.where(brick == 0, -float(n_x), 0.0).astype(F32)
    shift_high = jnp.where(brick == slabs - 1, float(n_x), 0.0).astype(F32)
    for n, (ref, shift) in enumerate(((low, shift_low), (high, shift_high))):
        for g in range(ghosts):
            row = [ref[last, k * ghosts + g : k * ghosts + g + 1, :] for k in range(4)]
            enter(tables, n * ghosts + g, row[0] + shift, row[1], row[2], row[3], unit)


def own_kernel(mine, par, plan, *refs, unit, cells):
    tables, (out, plan_s, sem) = refs[:4], refs[4:]
    copy = pltpu.make_async_copy(plan, plan_s, sem)
    copy.start()
    for c in range(mine.shape[3] // CELL):
        at = slice(c * CELL, (c + 1) * CELL)
        place = [mine[0, k, :, at] for k in range(3)]
        enter(tables, c, *place, par[1:2, at], unit)
    copy.wait()
    pair_cells(mine, par, {0: tables}, plan_s, out, cells, unit)


COUNT_AT = 127


def pair_cells(mine, par, tables, plan, out, work, unit):
    one = float(unit)
    for n, (c, kinds) in enumerate(work):
        at = slice(c * CELL, (c + 1) * CELL)
        xi = jnp.broadcast_to(mine[0, 0, :, at] * one, (8, CELL))
        yi = jnp.broadcast_to(fixed(mine[0, 1, :, at], unit), (8, CELL))
        zi = jnp.broadcast_to(fixed(mine[0, 2, :, at], unit), (8, CELL))
        zero = jnp.zeros((8, CELL), F32)
        total = (zero, zero, zero)
        for kind in kinds:
            place_x, place_y, place_z, load = tables[kind]

            def slot(s, total):
                start = pl.multiple_of(plan[kind, c, s] * CELL, CELL)
                tx, ty, tz = total
                for g in range(CELL // 8):
                    here = pl.ds(start + g * 8, 8)
                    dx = xi - place_x[here, :]
                    dy = (yi - place_y[here, :]).astype(F32)
                    dz = (zi - place_z[here, :]).astype(F32)
                    dist = dx * dx + dy * dy + (dz * dz + softening * one * one)
                    inv = lax.rsqrt(dist)
                    w = load[here, :] * inv * (inv * inv)
                    tx, ty, tz = tx + w * dx, ty + w * dy, tz + w * dz
                return tx, ty, tz

            def two_slots(n, total):
                return slot(2 * n + 1, slot(2 * n, total))

            slots = plan[kind, c, COUNT_AT]
            total = lax.fori_loop(0, slots // 2, two_slots, total)
            total = lax.fori_loop(2 * (slots // 2), slots, slot, total)
        factor = (coupling * one * one) * par[1:2, at]
        here = slice(n * CELL, (n + 1) * CELL)
        for k in range(3):
            out[k : k + 1, here] = factor * jnp.sum(total[k], axis=0, keepdims=True)


def middle_kernel(
    late, x_in, y_in, z_in, total, mine, par, plan, obs, weight, *refs,
    thick, bit, block, members, unit, work,
):
    ghosts, (dev_out, grad, partner_out, short, left_a, left_b, plan_s, sem) = refs[:4], refs[4:]
    copy = pltpu.make_async_copy(plan, plan_s, sem)
    copy.start()
    planes = range(RIM, thick)
    lefts = (left_a, left_b)
    held = x_in.shape[0]
    half = total.shape[1]
    layers(left_a, x_in[0], y_in[0], planes)
    for m in range(held):
        if m + 1 < held:
            layers(lefts[(m + 1) % 2], x_in[m + 1], y_in[m + 1], planes)
        got = product(lefts[m % 2], z_in[m], dev_out.shape)
        dev_out[...] = got + (total[RIM:thick] if m == 0 else dev_out[...])
    for n, i in enumerate(planes):
        dev = dev_out[n] * (1.0 / members) - obs[i - HALO]
        dev_out[n] = dev
        grad[n * half : (n + 1) * half, :] = (restraint * weight[i - HALO] * dev).astype(BF16)
    member_force(
        late.at[0], par, grad, partner_out,
        planes=planes, half=half, thick=thick, bit=bit, block=block,
    )
    copy.wait()
    pair_cells(mine, par, {1: ghosts}, plan_s, short, work, unit)


def member_force(place, par, grad, out, *, planes, half, thick, bit, block, plus=None):
    count = par.shape[1]
    depth = grad.shape[1]
    x_grid, y_grid, z_grid = spread_grids(half, depth, CELL, thick, bit, block)
    for t in range(count // CELL):
        at = slice(t * CELL, (t + 1) * CELL)
        inv_var, rate = par[2:3, at], par[3:4, at]
        x_val, x_der = bell_slope(x_grid, place[0, :, at], inv_var, rate)
        y_val, y_der = ring_bell_slope(y_grid, place[1, :, at], inv_var, rate, ring_unit(2 * half))
        z_val, z_der = ring_bell_slope(z_grid, place[2, :, at], inv_var, rate, ring_unit(depth))
        z_pair = jnp.concatenate([z_val, z_der], 1).astype(BF16)
        got = jnp.dot(grad[...], z_pair, preferred_element_type=F32)
        sums = [jnp.zeros((8, CELL), F32) for _ in range(3)]
        for n, i in enumerate(planes):
            part = [jnp.zeros((8, CELL), F32) for _ in range(3)]
            for g in range(half // 8):
                j = slice(g * 8, (g + 1) * 8)
                k = slice(n * half + g * 8, n * half + (g + 1) * 8)
                along, across = got[k, :CELL], got[k, CELL:]
                part[0] += y_val[j] * along
                part[1] += y_der[j] * along
                part[2] += y_val[j] * across
            sums[0] += x_der[i : i + 1] * part[0]
            sums[1] += x_val[i : i + 1] * part[1]
            sums[2] += x_val[i : i + 1] * part[2]
        for k in range(3):
            force = -par[0:1, at] * jnp.sum(sums[k], axis=0, keepdims=True)
            out[k : k + 1, at] = force if plus is None else force + plus[k : k + 1, at]


def grad_kernel(
    late, par, sent_y, got_y, sent_c, got_c, dev_middle, grad_middle, partner_middle,
    near_low, near_high, obs, weight,
    dev_out, grad, partner_out, grad_rim, dev_s, *, thick, bit, share, block, members,
):
    _, half, _ = dev_middle.shape
    deals = near_low.shape[0] // (2 * HALO)
    member = lax.axis_index("replica")

    def near_rows(ref, n, plane):
        at = (n * HALO + plane) * deals
        return jnp.concatenate([ref[at + q] for q in range(deals)], 0)

    even = lax.axis_index("brick") % 2 == 0
    rims = [*range(RIM), *range(thick, thick + RIM)]
    for at, i in enumerate(rims):
        low, n = i < RIM, at % RIM
        across = sent_y[n] + unpack_rim(got_y, n, low)
        beside = sent_c[n] + unpack_rim(got_c, n, low)
        summed = jnp.where(even == low, across, beside)
        if i < HALO:
            wanted, trust = near_rows(near_low, 0, i), near_rows(near_low, 1, i)
        elif i >= thick + HALO:
            beyond = i - thick - HALO
            wanted, trust = near_rows(near_high, 0, beyond), near_rows(near_high, 1, beyond)
        else:
            wanted, trust = obs[i - HALO], weight[i - HALO]
        dev = summed * (1.0 / members) - wanted
        slope = (restraint * trust * dev).astype(BF16)
        grad_rim[at * half : (at + 1) * half, :] = slope
        grad[i * half : (i + 1) * half, :] = slope
        if HALO <= i < thick + HALO:
            dev_s[i - HALO] = dev
    grad[RIM * half : thick * half, :] = grad_middle[...]
    dev_s[RIM - HALO : thick - HALO] = dev_middle[...]
    first_row = member * share
    spot = (first_row // (2 * block)) * block + first_row % block
    for n in range(half // share):

        @pl.when(spot == n * share)
        def _(n=n):
            dev_out[...] = dev_s[:, n * share : (n + 1) * share, :]

    member_force(
        late.at[0], par, grad_rim, partner_out,
        planes=rims, half=half, thick=thick, bit=bit, block=block, plus=partner_middle,
    )


def force_kernel(
    grad, deviation, mine, par, plan, *refs, thick, bit, block, unit, work
):
    own, ghosts, refs = refs[:4], refs[4:8], refs[8:]
    dev_out, out, short, plan_s, sem, dev_sem = refs
    copies = [
        pltpu.make_async_copy(plan, plan_s, sem),
        pltpu.make_async_copy(deviation, dev_out, dev_sem),
    ]
    for copy in copies:
        copy.start()
    planes = range(thick + 2 * HALO)
    half = grad.shape[0] // len(planes)
    member_force(
        mine.at[0], par, grad, out, planes=planes, half=half, thick=thick, bit=bit, block=block
    )
    copies[0].wait()
    pair_cells(mine, par, {0: own, 1: ghosts}, plan_s, short, work, unit)
    copies[1].wait()


def kick_kernel(own, other, short_own, short_a, short_b, par, speed, v_half, part, *, works):
    mass = par[4:5]
    energy = jnp.zeros_like(mass)
    for k in range(3):
        shorts = {}
        for short, work in zip((short_own, short_a, short_b), works):
            for n, (c, _) in enumerate(work):
                term = short[k : k + 1, n * CELL : (n + 1) * CELL]
                shorts[c] = shorts[c] + term if c in shorts else term
        short = jnp.concatenate([shorts[c] for c in sorted(shorts)], 1)
        force = own[k : k + 1] + other[k : k + 1] + short
        v = speed[k] + timestep * force / mass
        v_half[k : k + 1] = v
        energy = energy + mass * v * v
    part[...] = jnp.broadcast_to(jnp.sum(energy, axis=1, keepdims=True), part.shape)


def drift_kernel(*refs, freedom):
    parts, (v_half, coords, warmth, place_out, speed_out) = refs[:-5], refs[-5:]
    kinetic = parts[0][0:1]
    for part in parts[1:]:
        kinetic = kinetic + part[0:1]
    present_moment = kinetic / (freedom * boltzmann) + 1e-06
    ratio = jnp.sqrt(
        1.0 + heat_bath_damping * (warmth[0].astype(F32) / present_moment - 1.0)
    )
    ratio = jnp.concatenate([ratio] * (v_half.shape[1] // ratio.shape[1]), 1)
    for k in range(3):
        v = ratio * v_half[k : k + 1]
        speed_out[k] = v
        place_out[k] = coords[0, k] + timestep * v


def local(
    atom_locations,
    atom_speeds_vector,
    inertial_amounts,
    electric_loads,
    scatter_strengths,
    gaussian_spreads_sigma,
    atom_present_flags,
    observed_volume_values,
    voxel_reciprocal_spread,
    paired_partner_lists,
    cell_usage_tally,
    halo_sender_spots,
    target_warmth_levels,
):
    thick, rows, depth = observed_volume_values.shape
    slabs = lax.axis_size("brick")
    members = lax.axis_size("replica")
    n_x = thick * slabs
    coords = jnp.transpose(atom_locations, (1, 0, 2))
    speeds = jnp.transpose(atom_speeds_vector, (1, 0, 2))
    count = coords.shape[2]
    planes = thick + 2 * HALO
    share, bit, block = row_class(rows, members)
    half = rows // 2
    deals = half // block
    ghosts = halo_sender_spots.shape[1]
    assert 4 * ghosts // CELL <= block
    assert slabs >= 4 and slabs % 2 == 0 and thick >= RIM and count // CELL <= 8

    bits = [1 << n for n in range(members.bit_length() - 1) if n != bit][::-1]

    def hop(known, mask):
        return lax.ppermute(known, "replica", [(i, i ^ mask) for i in range(members)])

    first = hop(coords[None], bits[0])
    obs = in_hbm(observed_volume_values.reshape(thick, deals, 2, block, depth))
    weight = in_hbm(voxel_reciprocal_spread.reshape(thick, deals, 2, block, depth))
    near = jax.ShapeDtypeStruct((2 * HALO * deals + 1, block, CELL), F32)
    own_rows = jax.ShapeDtypeStruct((thick, half, depth), F32)
    mine, speed, par, plan, near_up, near_down, own_obs, own_weight = pl.pallas_call(
        functools.partial(prep_kernel, thick=thick, bit=bit, half=half),
        out_shape=(
            jax.ShapeDtypeStruct((1,) + coords.shape, F32),
            jax.ShapeDtypeStruct(speeds.shape, F32),
            jax.ShapeDtypeStruct((8, count), F32),
            jax.ShapeDtypeStruct((2, 8, CELL), jnp.int32),
            near,
            near,
            own_rows,
            own_rows,
        ),
        in_specs=[HBM] * 12,
        out_specs=(VMEM,) * 8,
        scratch_shapes=[
            pltpu.VMEM((1, count), jnp.int32),
            pltpu.VMEM((4, 1, count), F32),
            pltpu.VMEM((2, ghosts), jnp.int32),
            pltpu.VMEM(paired_partner_lists.shape, jnp.int32),
            pltpu.SMEM(cell_usage_tally.shape, jnp.int32),
            pltpu.SemaphoreType.DMA((10,)),
            pltpu.SemaphoreType.DMA((4 * HALO,)),
            pltpu.SemaphoreType.DMA((2 * deals,)),
        ],
        compiler_params=limit(4),
        cost_estimate=cost(1),
        name="prep",
    )(
        *(
            in_hbm(a)
            for a in (
                coords,
                speeds,
                atom_present_flags,
                scatter_strengths,
                electric_loads,
                gaussian_spreads_sigma,
                inertial_amounts,
                halo_sender_spots,
                paired_partner_lists,
                cell_usage_tally,
            )
        ),
        obs,
        weight,
    )
    groups = [mine, first]
    for mask in bits[1:]:
        groups.append(hop(jnp.concatenate(groups), mask))
    late = hop(jnp.concatenate(groups), 1 << bit)

    ring = [(i, (i + 1) % slabs) for i in range(slabs)]
    back = [(target, source) for source, target in ring]
    near_low = lax.ppermute(near_up, "brick", ring)
    near_high = lax.ppermute(near_down, "brick", back)

    cells = count // CELL
    unit = ring_unit(rows)
    assert rows == depth and members & (members - 1) == 0
    first_cells = 2 * cells // 3
    works = (
        [(c, [0]) for c in range(first_cells)],
        [(c, [1]) for c in range(cells - 1)],
        [(c, [0]) for c in range(first_cells, cells - 1)] + [(cells - 1, [0, 1])],
    )

    def shorts(work):
        return jax.ShapeDtypeStruct((3, len(work) * CELL), F32)

    def tables(blocks):
        table = jax.ShapeDtypeStruct((blocks * CELL, CELL), F32)
        table_int = jax.ShapeDtypeStruct((blocks * CELL, CELL), jnp.int32)
        return table, table_int, table_int, table

    planned = [pltpu.SMEM(plan.shape, jnp.int32), pltpu.SemaphoreType.DMA]
    *own_tables, short_own = pl.pallas_call(
        functools.partial(own_kernel, unit=unit, cells=works[0]),
        out_shape=(*tables(cells), shorts(works[0])),
        in_specs=[VMEM] * 3,
        out_specs=(VMEM,) * 5,
        scratch_shapes=planned,
        compiler_params=limit(6),
        cost_estimate=cost(2),
        name="own_pairs",
    )(mine, par, plan)
    ghost_tables = pl.pallas_call(
        functools.partial(ghost_kernel, n_x=n_x, ghosts=ghosts // CELL, unit=unit),
        out_shape=tables(2 * ghosts // CELL),
        in_specs=[VMEM] * 2,
        out_specs=(VMEM,) * 4,
        compiler_params=limit(6),
        cost_estimate=cost(1),
        name="ghosts",
    )(near_low, near_high)

    place = dict(thick=thick, bit=bit, block=block)
    total = pl.pallas_call(
        functools.partial(early_kernel, **place),
        out_shape=jax.ShapeDtypeStruct((planes, half, depth), F32),
        in_specs=[VMEM] * (len(groups) + 1),
        out_specs=VMEM,
        scratch_shapes=[pltpu.VMEM((planes * half, count), BF16)] * 2
        + [pltpu.VMEM((depth, count), BF16)] * 2,
        compiler_params=limit(12),
        cost_estimate=cost(2),
        name="early",
    )(*groups, par)
    held = late.shape[0]
    rim = jax.ShapeDtypeStruct((RIM, half, depth), F32)
    packet = jax.ShapeDtypeStruct((RIM + HALO, half, depth), BF16)
    sent_y, packet_y, x_late, y_late, z_late = pl.pallas_call(
        functools.partial(across_kernel, **place),
        out_shape=(
            rim,
            packet,
            jax.ShapeDtypeStruct((held, 16, count), F32),
            jax.ShapeDtypeStruct((held, half, count), F32),
            jax.ShapeDtypeStruct((held, depth, count), BF16),
        ),
        in_specs=[VMEM] * 3,
        out_specs=(VMEM,) * 5,
        scratch_shapes=[pltpu.VMEM((RIM * half, count), BF16)] * 2,
        compiler_params=limit(12),
        cost_estimate=cost(1),
        name="across",
    )(late, par, total)
    route = [(i, (i + 1 if i % 2 else i - 1) % slabs) for i in range(slabs)]
    got_y = lax.ppermute(packet_y, "brick", route)
    sent_c, packet_c = pl.pallas_call(
        functools.partial(beside_kernel, thick=thick),
        out_shape=(rim, packet),
        in_specs=[VMEM] * 5,
        out_specs=(VMEM, VMEM),
        scratch_shapes=[pltpu.VMEM((RIM * half, count), BF16)] * 2,
        compiler_params=limit(12),
        cost_estimate=cost(1),
        name="beside",
    )(late, par, total, y_late, z_late)
    got_c = lax.ppermute(packet_c, "brick", [(i, i ^ 1) for i in range(slabs)])
    force = jax.ShapeDtypeStruct((3, count), F32)
    inner = thick - RIM
    dev_middle, grad_middle, partner_middle, short_a = pl.pallas_call(
        functools.partial(middle_kernel, **place, members=members, unit=unit, work=works[1]),
        out_shape=(
            jax.ShapeDtypeStruct((inner, half, depth), F32),
            jax.ShapeDtypeStruct((inner * half, depth), BF16),
            force,
            shorts(works[1]),
        ),
        in_specs=[VMEM] * 14,
        out_specs=(VMEM,) * 4,
        scratch_shapes=[pltpu.VMEM((inner * half, count), BF16)] * 2 + planned,
        compiler_params=limit(12),
        cost_estimate=cost(2),
        name="middle",
    )(late, x_late, y_late, z_late, total, mine, par, plan, own_obs, own_weight, *ghost_tables)
    deviation, grad, partner = pl.pallas_call(
        functools.partial(grad_kernel, **place, share=share, members=members),
        out_shape=(
            jax.ShapeDtypeStruct((thick, share, depth), F32),
            jax.ShapeDtypeStruct((planes * half, depth), BF16),
            force,
        ),
        in_specs=[VMEM] * 13,
        out_specs=(VMEM, VMEM, VMEM),
        scratch_shapes=[
            pltpu.VMEM((2 * RIM * half, depth), BF16),
            pltpu.VMEM((thick, half, depth), F32),
        ],
        compiler_params=limit(12),
        cost_estimate=cost(1),
        name="grad",
    )(
        late, par, sent_y, got_y, sent_c, got_c, dev_middle, grad_middle, partner_middle,
        near_low, near_high, own_obs, own_weight,
    )

    swap = [(i, i ^ (1 << bit)) for i in range(members)]
    other = lax.ppermute(partner, "replica", swap)
    deviation, own, short_b = pl.pallas_call(
        functools.partial(force_kernel, **place, unit=unit, work=works[2]),
        out_shape=(
            jax.ShapeDtypeStruct(deviation.shape, F32),
            force,
            shorts(works[2]),
        ),
        in_specs=[VMEM] * 13,
        out_specs=(HBM, VMEM, VMEM),
        scratch_shapes=planned + [pltpu.SemaphoreType.DMA],
        compiler_params=limit(8),
        cost_estimate=cost(2),
        name="force",
    )(grad, deviation, mine, par, plan, *own_tables, *ghost_tables)
    v_half, part = pl.pallas_call(
        functools.partial(kick_kernel, works=works),
        out_shape=(force, jax.ShapeDtypeStruct((8, CELL), F32)),
        in_specs=[VMEM] * 7,
        out_specs=(VMEM, VMEM),
        compiler_params=limit(2),
        name="kick",
    )(own, other, short_own, short_a, short_b, par, speed)
    if slabs == 4:
        parts = [part]
        for mask in (2, 3, 1):
            parts.append(lax.ppermute(part, "brick", [(i, i ^ mask) for i in range(slabs)]))
    else:
        parts = [lax.psum(part, "brick")]
    moved = jax.ShapeDtypeStruct((3, 1, count), F32)
    new_positions, new_velocities = pl.pallas_call(
        functools.partial(drift_kernel, freedom=3 * count * slabs),
        out_shape=(moved, moved),
        in_specs=[VMEM] * (len(parts) + 2) + [SMEM],
        out_specs=(VMEM, VMEM),
        compiler_params=limit(2),
        name="drift",
    )(*parts, v_half, mine, target_warmth_levels)
    return (
        jnp.transpose(new_positions, (1, 0, 2)),
        jnp.transpose(new_velocities, (1, 0, 2)),
        deviation,
    )


def solution(mesh):
    return jax.shard_map(
        local,
        mesh=mesh,
        in_specs=(
            P("replica", None, "brick"),
            P("replica", None, "brick"),
            P("brick"),
            P("brick"),
            P("brick"),
            P("brick"),
            P("brick"),
            P("brick", None, None),
            P("brick", None, None),
            P("brick", None),
            P("brick"),
            P(None, "brick"),
            P("replica"),
        ),
        out_specs=(
            P("replica", None, "brick"),
            P("replica", None, "brick"),
            P("brick", "replica", None),
        ),
        check_vma=False,
    )
```

```python
import functools
import math

import jax
import jax.numpy as jnp
from jax import lax
from jax.experimental import pallas as pl
from jax.experimental.pallas import tpu as pltpu
from jax.sharding import PartitionSpec as P

HALO = 2
CELL = 128
RIM = 2 * HALO

restraint = 0.1
coupling = 5.0
softening = 1.0
timestep = 0.5
boltzmann = 0.015
heat_bath_damping = 0.5

F32 = jnp.float32
BF16 = jnp.bfloat16
NT = (((1,), (1,)), ((), ()))
VMEM = pl.BlockSpec(memory_space=pltpu.VMEM)
SMEM = pl.BlockSpec(memory_space=pltpu.SMEM)
HBM = pl.BlockSpec(memory_space=pltpu.HBM)


def fixed(v, unit):
    whole = jnp.floor(v)
    part = ((v - whole) * float(unit)).astype(jnp.int32)
    return (whole.astype(jnp.int32) << (unit.bit_length() - 1)) + part


def bell(grid, coord, rate):
    delta = grid - coord
    return jnp.exp2(delta * delta * rate)


def ring_bell(grid, coord, rate, unit):
    delta = (grid - fixed(coord, unit)).astype(F32)
    return jnp.exp2(delta * delta * (rate * (1.0 / unit / unit)))


def bell_slope(grid, coord, inv_var, rate):
    delta = grid - coord
    value = jnp.exp2(delta * delta * rate)
    return value, delta * inv_var * value


def ring_bell_slope(grid, coord, inv_var, rate, unit):
    delta = (grid - fixed(coord, unit)).astype(F32)
    value = jnp.exp2(delta * delta * (rate * (1.0 / unit / unit)))
    return value, delta * (inv_var * (1.0 / unit)) * value


def limit(mib):
    return pltpu.CompilerParams(vmem_limit_bytes=mib << 20)


def in_hbm(x):
    return pltpu.with_memory_space_constraint(x, pltpu.HBM)


def cost(us):
    return pl.CostEstimate(flops=us * 500_000_000, bytes_accessed=us * 1_000_000, transcendentals=0)


def iota(shape, dim):
    return lax.broadcasted_iota(jnp.int32, shape, dim)


def row_class(rows, members):
    share = rows // members
    bit = 0
    while (share << bit) % 8:
        bit += 1
    return share, bit, share << bit


def local_rows(shape, member, bit, block):
    row = iota(shape, 0)
    own = (member >> bit) & 1
    return (row // block) * (2 * block) + own * block + row % block


def prep_kernel(
    coords, speeds, flags, scatter, loads, sigma, mass, spots, lists, live, obs, weight,
    mine, speed_out, par, plan, up, down, obs_out, weight_out,
    flags_s, floats_s, spots_s, lists_s, live_s, small_sem, sem, row_sem, *, thick, bit, half,
):
    own = (lax.axis_index("replica") >> bit) & 1
    block = obs.shape[3]
    small = [
        pltpu.make_async_copy(flags, flags_s.at[0], small_sem.at[0]),
        pltpu.make_async_copy(spots, spots_s, small_sem.at[1]),
        pltpu.make_async_copy(coords, mine.at[0], small_sem.at[6]),
        pltpu.make_async_copy(speeds, speed_out, small_sem.at[9]),
        pltpu.make_async_copy(lists, lists_s, small_sem.at[7]),
        pltpu.make_async_copy(live, live_s, small_sem.at[8]),
    ]
    for n, source in enumerate((scatter, loads, sigma, mass)):
        small.append(pltpu.make_async_copy(source, floats_s.at[n, 0], small_sem.at[2 + n]))
    for copy in small:
        copy.start()
    copies = []
    deals = half // block
    for target, first in ((up, thick - HALO), (down, 0)):
        for n, source in enumerate((obs, weight)):
            for plane in range(HALO):
                copies.append(
                    pltpu.make_async_copy(
                        source.at[first + plane, :, own],
                        target.at[pl.ds((n * HALO + plane) * deals, deals)],
                        sem.at[len(copies)],
                    )
                )
                copies[-1].start()
    for source, target in ((obs, obs_out), (weight, weight_out)):
        for q in range(deals):
            copies.append(
                pltpu.make_async_copy(
                    source.at[:, q, own],
                    target.at[:, pl.ds(q * block, block)],
                    row_sem.at[len(copies) - 4 * HALO],
                )
            )
            copies[-1].start()
    for copy in small:
        copy.wait()
    occupancy = flags_s[...].astype(F32)
    inv_var = 1.0 / (floats_s[2] * floats_s[2])
    charge = occupancy * floats_s[1]
    par[0:1] = occupancy * floats_s[0]
    par[1:2] = charge
    par[2:3] = inv_var
    par[3:4] = (-0.5 * math.log2(math.e)) * inv_var
    par[4:5] = floats_s[3]
    data = jnp.concatenate([mine[0, 0], mine[0, 1], mine[0, 2], charge], 0)
    high = data.astype(BF16)
    rest = data - high.astype(F32)
    mid = rest.astype(BF16)
    low = (rest - mid.astype(F32)).astype(BF16)
    pieces = jnp.concatenate([high.astype(F32), mid.astype(F32), low.astype(F32)], 0).astype(BF16)
    count = data.shape[1]
    cells, slots = lists_s.shape
    lane, row = iota((8, CELL), 1), iota((8, CELL), 0)
    used = jnp.zeros((8, CELL), jnp.int32)
    for c in range(cells):
        used = jnp.where(row == c, live_s[c], used)
    listed = jnp.concatenate([lists_s[...], jnp.zeros((8 - cells, slots), jnp.int32)], 0)
    picked = [jnp.zeros((8, CELL), jnp.int32)] * 2
    length = [jnp.zeros((8, CELL), jnp.int32)] * 2
    for s in range(slots):
        block_of = jnp.broadcast_to(listed[:, s : s + 1], (8, CELL))
        for kind in range(2):
            takes = (s < used) & ((block_of < cells) if kind == 0 else (block_of >= cells))
            picked[kind] = jnp.where(takes & (lane == length[kind]), block_of - kind * cells, picked[kind])
            length[kind] = length[kind] + takes.astype(jnp.int32)
    for kind in range(2):
        plan[kind] = jnp.where(lane == COUNT_AT, length[kind], picked[kind])
    for side, target in enumerate((up, down)):
        chosen = spots_s[side : side + 1, :]
        pick = (iota((count, chosen.shape[1]), 0) == chosen).astype(F32).astype(BF16)
        got = jnp.dot(pieces, pick, preferred_element_type=F32)
        got = got[0:4] + got[4:8] + got[8:12]
        groups = chosen.shape[1] // CELL
        for n in range(4):
            for g in range(groups):
                row = n * groups + g
                target[2 * HALO * deals, row : row + 1, :] = got[
                    n : n + 1, g * CELL : (g + 1) * CELL
                ]
    for copy in copies:
        copy.wait()


def ring_unit(period):
    unit = 2**32 // period
    assert unit * period == 2**32
    return unit


def spread_grids(half, depth, count, thick, bit, block):
    first = lax.axis_index("brick") * thick - HALO
    x_grid = (iota((16, count), 0) + first).astype(F32)
    y_grid = local_rows((half, count), lax.axis_index("replica"), bit, block) * ring_unit(2 * half)
    z_grid = iota((depth, count), 0) * ring_unit(depth)
    return x_grid, y_grid, z_grid


def member_bells(place, amp, rate, grids):
    x_grid, y_grid, z_grid = grids
    x_amp = amp * bell(x_grid, place[0], rate)
    y_val = ring_bell(y_grid, place[1], rate, ring_unit(2 * y_grid.shape[0]))
    z_val = ring_bell(z_grid, place[2], rate, ring_unit(z_grid.shape[0])).astype(BF16)
    return x_amp, y_val, z_val


def layers(left, x_amp, y_val, planes):
    half = y_val.shape[0]
    for n, i in enumerate(planes):
        left[n * half : (n + 1) * half, :] = (x_amp[i : i + 1] * y_val).astype(BF16)


def product(left, z_val, shape):
    return lax.dot_general(left[...], z_val, NT, preferred_element_type=F32).reshape(shape)


def early_kernel(*refs, thick, bit, block):
    groups, par, out, lefts, deeps = refs[:-6], refs[-6], refs[-5], refs[-4:-2], refs[-2:]
    planes, half, depth = out.shape
    count = par.shape[1]
    amp, rate = par[0:1], par[3:4]
    grids = spread_grids(half, depth, count, thick, bit, block)
    places = [(g, n) for g in groups for n in range(g.shape[0])]

    def build(m):
        g, n = places[m]
        x_amp, y_val, z_val = member_bells(g.at[n], amp, rate, grids)
        deeps[m % 2][...] = z_val
        layers(lefts[m % 2], x_amp, y_val, range(planes))

    build(0)
    for m in range(len(places)):
        if m + 1 < len(places):
            build(m + 1)
        got = product(lefts[m % 2], deeps[m % 2][...], out.shape)
        out[...] = got if m == 0 else out[...] + got


def rim_side(across, thick):
    odd = lax.axis_index("brick") % 2
    return thick * (odd if across else 1 - odd)


def rim_bells(base, place, amp, rate, thick):
    first = lax.axis_index("brick") * thick - HALO + base
    grid = (iota((8, amp.shape[1]), 0) + first).astype(F32)
    return amp * bell(grid, place[0], rate)


def across_kernel(late, par, total, out, packet, x_out, y_out, z_out, left_a, left_b, *, thick, bit, block):
    members = late.shape[0]
    _, half, depth = total.shape
    amp, rate = par[0:1], par[3:4]
    grids = spread_grids(half, depth, par.shape[1], thick, bit, block)
    lefts = (left_a, left_b)
    base = rim_side(True, thick)

    def build(m):
        x_amp, y_val, z_val = member_bells(late.at[m], amp, rate, grids)
        x_out[m], y_out[m], z_out[m] = x_amp, y_val, z_val
        layers(lefts[m % 2], rim_bells(base, late.at[m], amp, rate, thick), y_val, range(RIM))

    build(0)
    for m in range(members):
        if m + 1 < members:
            build(m + 1)
        got = product(lefts[m % 2], z_out[m], out.shape)
        out[...] = got + (total[pl.ds(base, RIM)] if m == 0 else out[...])
    packet[...] = out[...].astype(BF16)


def beside_kernel(late, par, total, y_in, z_in, out, packet, left_a, left_b, *, thick):
    members = late.shape[0]
    amp, rate = par[0:1], par[3:4]
    lefts = (left_a, left_b)
    base = rim_side(False, thick)

    def build(m):
        layers(lefts[m % 2], rim_bells(base, late.at[m], amp, rate, thick), y_in[m], range(RIM))

    build(0)
    for m in range(members):
        if m + 1 < members:
            build(m + 1)
        got = product(lefts[m % 2], z_in[m], out.shape)
        out[...] = got + (total[pl.ds(base, RIM)] if m == 0 else out[...])
    packet[...] = out[...].astype(BF16)


def enter(tables, n, x, y, z, q, unit):
    at = slice(n * CELL, (n + 1) * CELL)
    for table, row in zip(tables, (x * float(unit), fixed(y, unit), fixed(z, unit), q)):
        table[at, :] = jnp.broadcast_to(row, (CELL, CELL)).T


def ghost_kernel(low, high, *tables, n_x, ghosts, unit):
    slabs = lax.axis_size("brick")
    brick = lax.axis_index("brick")
    last = low.shape[0] - 1
    shift_low = jnp.where(brick == 0, -float(n_x), 0.0).astype(F32)
    shift_high = jnp.where(brick == slabs - 1, float(n_x), 0.0).astype(F32)
    for n, (ref, shift) in enumerate(((low, shift_low), (high, shift_high))):
        for g in range(ghosts):
            row = [ref[last, k * ghosts + g : k * ghosts + g + 1, :] for k in range(4)]
            enter(tables, n * ghosts + g, row[0] + shift, row[1], row[2], row[3], unit)


def own_kernel(mine, par, plan, *refs, unit, cells):
    tables, (out, plan_s, sem) = refs[:4], refs[4:]
    copy = pltpu.make_async_copy(plan, plan_s, sem)
    copy.start()
    for c in range(mine.shape[3] // CELL):
        at = slice(c * CELL, (c + 1) * CELL)
        place = [mine[0, k, :, at] for k in range(3)]
        enter(tables, c, *place, par[1:2, at], unit)
    copy.wait()
    pair_cells(mine, par, {0: tables}, plan_s, out, cells, unit)


COUNT_AT = 127


def pair_cells(mine, par, tables, plan, out, work, unit):
    one = float(unit)
    for n, (c, kinds) in enumerate(work):
        at = slice(c * CELL, (c + 1) * CELL)
        xi = jnp.broadcast_to(mine[0, 0, :, at] * one, (8, CELL))
        yi = jnp.broadcast_to(fixed(mine[0, 1, :, at], unit), (8, CELL))
        zi = jnp.broadcast_to(fixed(mine[0, 2, :, at], unit), (8, CELL))
        zero = jnp.zeros((8, CELL), F32)
        total = (zero, zero, zero)
        for kind in kinds:
            place_x, place_y, place_z, load = tables[kind]

            def slot(s, total):
                start = pl.multiple_of(plan[kind, c, s] * CELL, CELL)
                tx, ty, tz = total
                for g in range(CELL // 8):
                    here = pl.ds(start + g * 8, 8)
                    dx = xi - place_x[here, :]
                    dy = (yi - place_y[here, :]).astype(F32)
                    dz = (zi - place_z[here, :]).astype(F32)
                    dist = dx * dx + dy * dy + (dz * dz + softening * one * one)
                    inv = lax.rsqrt(dist)
                    w = load[here, :] * inv * (inv * inv)
                    tx, ty, tz = tx + w * dx, ty + w * dy, tz + w * dz
                return tx, ty, tz

            def two_slots(n, total):
                return slot(2 * n + 1, slot(2 * n, total))

            slots = plan[kind, c, COUNT_AT]
            total = lax.fori_loop(0, slots // 2, two_slots, total)
            total = lax.fori_loop(2 * (slots // 2), slots, slot, total)
        factor = (coupling * one * one) * par[1:2, at]
        here = slice(n * CELL, (n + 1) * CELL)
        for k in range(3):
            out[k : k + 1, here] = factor * jnp.sum(total[k], axis=0, keepdims=True)


def middle_kernel(
    late, x_in, y_in, z_in, total, mine, par, plan, obs, weight, *refs,
    thick, bit, block, members, unit, work,
):
    ghosts, (dev_out, grad, partner_out, short, left_a, left_b, plan_s, sem) = refs[:4], refs[4:]
    copy = pltpu.make_async_copy(plan, plan_s, sem)
    copy.start()
    planes = range(RIM, thick)
    lefts = (left_a, left_b)
    held = x_in.shape[0]
    half = total.shape[1]
    layers(left_a, x_in[0], y_in[0], planes)
    for m in range(held):
        if m + 1 < held:
            layers(lefts[(m + 1) % 2], x_in[m + 1], y_in[m + 1], planes)
        got = product(lefts[m % 2], z_in[m], dev_out.shape)
        dev_out[...] = got + (total[RIM:thick] if m == 0 else dev_out[...])
    for n, i in enumerate(planes):
        dev = dev_out[n] * (1.0 / members) - obs[i - HALO]
        dev_out[n] = dev
        grad[n * half : (n + 1) * half, :] = (restraint * weight[i - HALO] * dev).astype(BF16)
    member_force(
        late.at[0], par, grad, partner_out,
        planes=planes, half=half, thick=thick, bit=bit, block=block,
    )
    copy.wait()
    pair_cells(mine, par, {1: ghosts}, plan_s, short, work, unit)


def member_force(place, par, grad, out, *, planes, half, thick, bit, block, plus=None):
    count = par.shape[1]
    depth = grad.shape[1]
    x_grid, y_grid, z_grid = spread_grids(half, depth, CELL, thick, bit, block)
    for t in range(count // CELL):
        at = slice(t * CELL, (t + 1) * CELL)
        inv_var, rate = par[2:3, at], par[3:4, at]
        x_val, x_der = bell_slope(x_grid, place[0, :, at], inv_var, rate)
        y_val, y_der = ring_bell_slope(y_grid, place[1, :, at], inv_var, rate, ring_unit(2 * half))
        z_val, z_der = ring_bell_slope(z_grid, place[2, :, at], inv_var, rate, ring_unit(depth))
        z_pair = jnp.concatenate([z_val, z_der], 1).astype(BF16)
        got = jnp.dot(grad[...], z_pair, preferred_element_type=F32)
        sums = [jnp.zeros((8, CELL), F32) for _ in range(3)]
        for n, i in enumerate(planes):
            part = [jnp.zeros((8, CELL), F32) for _ in range(3)]
            for g in range(half // 8):
                j = slice(g * 8, (g + 1) * 8)
                k = slice(n * half + g * 8, n * half + (g + 1) * 8)
                along, across = got[k, :CELL], got[k, CELL:]
                part[0] += y_val[j] * along
                part[1] += y_der[j] * along
                part[2] += y_val[j] * across
            sums[0] += x_der[i : i + 1] * part[0]
            sums[1] += x_val[i : i + 1] * part[1]
            sums[2] += x_val[i : i + 1] * part[2]
        for k in range(3):
            force = -par[0:1, at] * jnp.sum(sums[k], axis=0, keepdims=True)
            out[k : k + 1, at] = force if plus is None else force + plus[k : k + 1, at]


def grad_kernel(
    late, par, sent_y, got_y, sent_c, got_c, dev_middle, grad_middle, partner_middle,
    near_low, near_high, obs, weight,
    dev_out, grad, partner_out, grad_rim, dev_s, *, thick, bit, share, block, members,
):
    _, half, _ = dev_middle.shape
    deals = near_low.shape[0] // (2 * HALO)
    member = lax.axis_index("replica")

    def near_rows(ref, n, plane):
        at = (n * HALO + plane) * deals
        return jnp.concatenate([ref[at + q] for q in range(deals)], 0)

    even = lax.axis_index("brick") % 2 == 0
    rims = [*range(RIM), *range(thick, thick + RIM)]
    for at, i in enumerate(rims):
        low, n = i < RIM, at % RIM
        across = sent_y[n] + got_y[n].astype(F32)
        beside = sent_c[n] + got_c[n].astype(F32)
        summed = jnp.where(even == low, across, beside)
        if i < HALO:
            wanted, trust = near_rows(near_low, 0, i), near_rows(near_low, 1, i)
        elif i >= thick + HALO:
            beyond = i - thick - HALO
            wanted, trust = near_rows(near_high, 0, beyond), near_rows(near_high, 1, beyond)
        else:
            wanted, trust = obs[i - HALO], weight[i - HALO]
        dev = summed * (1.0 / members) - wanted
        slope = (restraint * trust * dev).astype(BF16)
        grad_rim[at * half : (at + 1) * half, :] = slope
        grad[i * half : (i + 1) * half, :] = slope
        if HALO <= i < thick + HALO:
            dev_s[i - HALO] = dev
    grad[RIM * half : thick * half, :] = grad_middle[...]
    dev_s[RIM - HALO : thick - HALO] = dev_middle[...]
    first_row = member * share
    spot = (first_row // (2 * block)) * block + first_row % block
    for n in range(half // share):

        @pl.when(spot == n * share)
        def _(n=n):
            dev_out[...] = dev_s[:, n * share : (n + 1) * share, :]

    member_force(
        late.at[0], par, grad_rim, partner_out,
        planes=rims, half=half, thick=thick, bit=bit, block=block, plus=partner_middle,
    )


def force_kernel(
    grad, deviation, mine, par, plan, *refs, thick, bit, block, unit, work
):
    own, ghosts, refs = refs[:4], refs[4:8], refs[8:]
    dev_out, out, short, plan_s, sem, dev_sem = refs
    copies = [
        pltpu.make_async_copy(plan, plan_s, sem),
        pltpu.make_async_copy(deviation, dev_out, dev_sem),
    ]
    for copy in copies:
        copy.start()
    planes = range(thick + 2 * HALO)
    half = grad.shape[0] // len(planes)
    member_force(
        mine.at[0], par, grad, out, planes=planes, half=half, thick=thick, bit=bit, block=block
    )
    copies[0].wait()
    pair_cells(mine, par, {0: own, 1: ghosts}, plan_s, short, work, unit)
    copies[1].wait()


def kick_kernel(own, other, *refs, works):
    given, (par, speed, v_half, part) = refs[:-4], refs[-4:]
    mass = par[4:5]
    energy = jnp.zeros_like(mass)
    for k in range(3):
        shorts = {}
        for short, work in zip(given, works):
            for n, (c, _) in enumerate(work):
                term = short[k : k + 1, n * CELL : (n + 1) * CELL]
                shorts[c] = shorts[c] + term if c in shorts else term
        short = jnp.concatenate([shorts[c] for c in sorted(shorts)], 1)
        force = own[k : k + 1] + other[k : k + 1] + short
        v = speed[k] + timestep * force / mass
        v_half[k : k + 1] = v
        energy = energy + mass * v * v
    part[...] = jnp.broadcast_to(jnp.sum(energy, axis=1, keepdims=True), part.shape)


def drift_kernel(*refs, freedom):
    parts, (v_half, coords, warmth, place_out, speed_out) = refs[:-5], refs[-5:]
    kinetic = parts[0][0:1]
    for part in parts[1:]:
        kinetic = kinetic + part[0:1]
    present_moment = kinetic / (freedom * boltzmann) + 1e-06
    ratio = jnp.sqrt(
        1.0 + heat_bath_damping * (warmth[0].astype(F32) / present_moment - 1.0)
    )
    ratio = jnp.concatenate([ratio] * (v_half.shape[1] // ratio.shape[1]), 1)
    for k in range(3):
        v = ratio * v_half[k : k + 1]
        speed_out[k] = v
        place_out[k] = coords[0, k] + timestep * v


def local(
    atom_locations,
    atom_speeds_vector,
    inertial_amounts,
    electric_loads,
    scatter_strengths,
    gaussian_spreads_sigma,
    atom_present_flags,
    observed_volume_values,
    voxel_reciprocal_spread,
    paired_partner_lists,
    cell_usage_tally,
    halo_sender_spots,
    target_warmth_levels,
):
    thick, rows, depth = observed_volume_values.shape
    slabs = lax.axis_size("brick")
    members = lax.axis_size("replica")
    n_x = thick * slabs
    coords = jnp.transpose(atom_locations, (1, 0, 2))
    speeds = jnp.transpose(atom_speeds_vector, (1, 0, 2))
    count = coords.shape[2]
    planes = thick + 2 * HALO
    share, bit, block = row_class(rows, members)
    half = rows // 2
    deals = half // block
    ghosts = halo_sender_spots.shape[1]
    assert 4 * ghosts // CELL <= block
    assert slabs >= 4 and slabs % 2 == 0 and thick >= RIM and count // CELL <= 8

    bits = [1 << n for n in range(members.bit_length() - 1) if n != bit][::-1]

    def hop(known, mask):
        return lax.ppermute(known, "replica", [(i, i ^ mask) for i in range(members)])

    first = hop(coords[None], bits[0])
    obs = in_hbm(observed_volume_values.reshape(thick, deals, 2, block, depth))
    weight = in_hbm(voxel_reciprocal_spread.reshape(thick, deals, 2, block, depth))
    near = jax.ShapeDtypeStruct((2 * HALO * deals + 1, block, CELL), F32)
    own_rows = jax.ShapeDtypeStruct((thick, half, depth), F32)
    mine, speed, par, plan, near_up, near_down, own_obs, own_weight = pl.pallas_call(
        functools.partial(prep_kernel, thick=thick, bit=bit, half=half),
        out_shape=(
            jax.ShapeDtypeStruct((1,) + coords.shape, F32),
            jax.ShapeDtypeStruct(speeds.shape, F32),
            jax.ShapeDtypeStruct((8, count), F32),
            jax.ShapeDtypeStruct((2, 8, CELL), jnp.int32),
            near,
            near,
            own_rows,
            own_rows,
        ),
        in_specs=[HBM] * 12,
        out_specs=(VMEM,) * 8,
        scratch_shapes=[
            pltpu.VMEM((1, count), jnp.int32),
            pltpu.VMEM((4, 1, count), F32),
            pltpu.VMEM((2, ghosts), jnp.int32),
            pltpu.VMEM(paired_partner_lists.shape, jnp.int32),
            pltpu.SMEM(cell_usage_tally.shape, jnp.int32),
            pltpu.SemaphoreType.DMA((10,)),
            pltpu.SemaphoreType.DMA((4 * HALO,)),
            pltpu.SemaphoreType.DMA((2 * deals,)),
        ],
        compiler_params=limit(4),
        cost_estimate=cost(1),
        name="prep",
    )(
        *(
            in_hbm(a)
            for a in (
                coords,
                speeds,
                atom_present_flags,
                scatter_strengths,
                electric_loads,
                gaussian_spreads_sigma,
                inertial_amounts,
                halo_sender_spots,
                paired_partner_lists,
                cell_usage_tally,
            )
        ),
        obs,
        weight,
    )
    groups = [mine, first]
    for mask in bits[1:]:
        groups.append(hop(jnp.concatenate(groups), mask))
    late = hop(jnp.concatenate(groups), 1 << bit)

    ring = [(i, (i + 1) % slabs) for i in range(slabs)]
    back = [(target, source) for source, target in ring]
    near_low = lax.ppermute(near_up, "brick", ring)
    near_high = lax.ppermute(near_down, "brick", back)

    cells = count // CELL
    unit = ring_unit(rows)
    assert rows == depth and members & (members - 1) == 0
    first_cells = 2 * cells // 3
    works = (
        [(c, [0]) for c in range(first_cells)],
        [(c, [1]) for c in range(first_cells)],
        [(c, [0, 1]) for c in range(first_cells, cells)],
    )

    def shorts(work):
        return jax.ShapeDtypeStruct((3, len(work) * CELL), F32)

    def tables(blocks):
        table = jax.ShapeDtypeStruct((blocks * CELL, CELL), F32)
        table_int = jax.ShapeDtypeStruct((blocks * CELL, CELL), jnp.int32)
        return table, table_int, table_int, table

    planned = [pltpu.SMEM(plan.shape, jnp.int32), pltpu.SemaphoreType.DMA]
    *own_tables, short_own = pl.pallas_call(
        functools.partial(own_kernel, unit=unit, cells=works[0]),
        out_shape=(*tables(cells), shorts(works[0])),
        in_specs=[VMEM] * 3,
        out_specs=(VMEM,) * 5,
        scratch_shapes=planned,
        compiler_params=limit(6),
        cost_estimate=cost(2),
        name="own_pairs",
    )(mine, par, plan)
    ghost_tables = pl.pallas_call(
        functools.partial(ghost_kernel, n_x=n_x, ghosts=ghosts // CELL, unit=unit),
        out_shape=tables(2 * ghosts // CELL),
        in_specs=[VMEM] * 2,
        out_specs=(VMEM,) * 4,
        compiler_params=limit(6),
        cost_estimate=cost(1),
        name="ghosts",
    )(near_low, near_high)

    place = dict(thick=thick, bit=bit, block=block)
    total = pl.pallas_call(
        functools.partial(early_kernel, **place),
        out_shape=jax.ShapeDtypeStruct((planes, half, depth), F32),
        in_specs=[VMEM] * (len(groups) + 1),
        out_specs=VMEM,
        scratch_shapes=[pltpu.VMEM((planes * half, count), BF16)] * 2
        + [pltpu.VMEM((depth, count), BF16)] * 2,
        compiler_params=limit(12),
        cost_estimate=cost(2),
        name="early",
    )(*groups, par)
    held = late.shape[0]
    rim = jax.ShapeDtypeStruct((RIM, half, depth), F32)
    packet = jax.ShapeDtypeStruct((RIM, half, depth), BF16)
    sent_y, packet_y, x_late, y_late, z_late = pl.pallas_call(
        functools.partial(across_kernel, **place),
        out_shape=(
            rim,
            packet,
            jax.ShapeDtypeStruct((held, 16, count), F32),
            jax.ShapeDtypeStruct((held, half, count), F32),
            jax.ShapeDtypeStruct((held, depth, count), BF16),
        ),
        in_specs=[VMEM] * 3,
        out_specs=(VMEM,) * 5,
        scratch_shapes=[pltpu.VMEM((RIM * half, count), BF16)] * 2,
        compiler_params=limit(12),
        cost_estimate=cost(1),
        name="across",
    )(late, par, total)
    route = [(i, (i + 1 if i % 2 else i - 1) % slabs) for i in range(slabs)]
    got_y = lax.ppermute(packet_y, "brick", route)
    sent_c, packet_c = pl.pallas_call(
        functools.partial(beside_kernel, thick=thick),
        out_shape=(rim, packet),
        in_specs=[VMEM] * 5,
        out_specs=(VMEM, VMEM),
        scratch_shapes=[pltpu.VMEM((RIM * half, count), BF16)] * 2,
        compiler_params=limit(12),
        cost_estimate=cost(1),
        name="beside",
    )(late, par, total, y_late, z_late)
    got_c = lax.ppermute(packet_c, "brick", [(i, i ^ 1) for i in range(slabs)])
    force = jax.ShapeDtypeStruct((3, count), F32)
    inner = thick - RIM
    dev_middle, grad_middle, partner_middle, short_a = pl.pallas_call(
        functools.partial(middle_kernel, **place, members=members, unit=unit, work=works[1]),
        out_shape=(
            jax.ShapeDtypeStruct((inner, half, depth), F32),
            jax.ShapeDtypeStruct((inner * half, depth), BF16),
            force,
            shorts(works[1]),
        ),
        in_specs=[VMEM] * 14,
        out_specs=(VMEM,) * 4,
        scratch_shapes=[pltpu.VMEM((inner * half, count), BF16)] * 2 + planned,
        compiler_params=limit(12),
        cost_estimate=cost(2),
        name="middle",
    )(late, x_late, y_late, z_late, total, mine, par, plan, own_obs, own_weight, *ghost_tables)
    deviation, grad, partner = pl.pallas_call(
        functools.partial(grad_kernel, **place, share=share, members=members),
        out_shape=(
            jax.ShapeDtypeStruct((thick, share, depth), F32),
            jax.ShapeDtypeStruct((planes * half, depth), BF16),
            force,
        ),
        in_specs=[VMEM] * 13,
        out_specs=(VMEM, VMEM, VMEM),
        scratch_shapes=[
            pltpu.VMEM((2 * RIM * half, depth), BF16),
            pltpu.VMEM((thick, half, depth), F32),
        ],
        compiler_params=limit(12),
        cost_estimate=cost(1),
        name="grad",
    )(
        late, par, sent_y, got_y, sent_c, got_c, dev_middle, grad_middle, partner_middle,
        near_low, near_high, own_obs, own_weight,
    )

    swap = [(i, i ^ (1 << bit)) for i in range(members)]
    other = lax.ppermute(partner, "replica", swap)
    deviation, own, short_b = pl.pallas_call(
        functools.partial(force_kernel, **place, unit=unit, work=works[2]),
        out_shape=(
            jax.ShapeDtypeStruct(deviation.shape, F32),
            force,
            shorts(works[2]),
        ),
        in_specs=[VMEM] * 13,
        out_specs=(HBM, VMEM, VMEM),
        scratch_shapes=planned + [pltpu.SemaphoreType.DMA],
        compiler_params=limit(8),
        cost_estimate=cost(2),
        name="force",
    )(grad, deviation, mine, par, plan, *own_tables, *ghost_tables)
    v_half, part = pl.pallas_call(
        functools.partial(kick_kernel, works=works),
        out_shape=(force, jax.ShapeDtypeStruct((8, CELL), F32)),
        in_specs=[VMEM] * 7,
        out_specs=(VMEM, VMEM),
        compiler_params=limit(2),
        name="kick",
    )(own, other, short_own, short_a, short_b, par, speed)
    if slabs == 4:
        parts = [part]
        for mask in (2, 3, 1):
            parts.append(lax.ppermute(part, "brick", [(i, i ^ mask) for i in range(slabs)]))
    else:
        parts = [lax.psum(part, "brick")]
    moved = jax.ShapeDtypeStruct((3, 1, count), F32)
    new_positions, new_velocities = pl.pallas_call(
        functools.partial(drift_kernel, freedom=3 * count * slabs),
        out_shape=(moved, moved),
        in_specs=[VMEM] * (len(parts) + 2) + [SMEM],
        out_specs=(VMEM, VMEM),
        compiler_params=limit(2),
        name="drift",
    )(*parts, v_half, mine, target_warmth_levels)
    return (
        jnp.transpose(new_positions, (1, 0, 2)),
        jnp.transpose(new_velocities, (1, 0, 2)),
        deviation,
    )


def solution(mesh):
    return jax.shard_map(
        local,
        mesh=mesh,
        in_specs=(
            P("replica", None, "brick"),
            P("replica", None, "brick"),
            P("brick"),
            P("brick"),
            P("brick"),
            P("brick"),
            P("brick"),
            P("brick", None, None),
            P("brick", None, None),
            P("brick", None),
            P("brick"),
            P(None, "brick"),
            P("replica"),
        ),
        out_specs=(
            P("replica", None, "brick"),
            P("replica", None, "brick"),
            P("brick", "replica", None),
        ),
        check_vma=False,
    )
```

```python
import functools
import math

import jax
import jax.numpy as jnp
from jax import lax
from jax.experimental import pallas as pl
from jax.experimental.pallas import tpu as pltpu
from jax.sharding import PartitionSpec as P

HALO = 2
CELL = 128
RIM = 2 * HALO

restraint = 0.1
coupling = 5.0
softening = 1.0
timestep = 0.5
boltzmann = 0.015
heat_bath_damping = 0.5

F32 = jnp.float32
BF16 = jnp.bfloat16
NT = (((1,), (1,)), ((), ()))
VMEM = pl.BlockSpec(memory_space=pltpu.VMEM)
SMEM = pl.BlockSpec(memory_space=pltpu.SMEM)
HBM = pl.BlockSpec(memory_space=pltpu.HBM)


def fixed(v, unit):
    whole = jnp.floor(v)
    part = ((v - whole) * float(unit)).astype(jnp.int32)
    return (whole.astype(jnp.int32) << (unit.bit_length() - 1)) + part


def bell(grid, coord, rate):
    delta = grid - coord
    return jnp.exp2(delta * delta * rate)


def ring_bell(grid, coord, rate, unit):
    delta = (grid - fixed(coord, unit)).astype(F32)
    return jnp.exp2(delta * delta * (rate * (1.0 / unit / unit)))


def bell_slope(grid, coord, inv_var, rate):
    delta = grid - coord
    value = jnp.exp2(delta * delta * rate)
    return value, delta * inv_var * value


def ring_bell_slope(grid, coord, inv_var, rate, unit):
    delta = (grid - fixed(coord, unit)).astype(F32)
    value = jnp.exp2(delta * delta * (rate * (1.0 / unit / unit)))
    return value, delta * (inv_var * (1.0 / unit)) * value


def limit(mib):
    return pltpu.CompilerParams(vmem_limit_bytes=mib << 20)


def in_hbm(x):
    return pltpu.with_memory_space_constraint(x, pltpu.HBM)


def cost(us):
    return pl.CostEstimate(flops=us * 500_000_000, bytes_accessed=us * 1_000_000, transcendentals=0)


def iota(shape, dim):
    return lax.broadcasted_iota(jnp.int32, shape, dim)


def row_class(rows, members):
    share = rows // members
    bit = 0
    while (share << bit) % 8:
        bit += 1
    return share, bit, share << bit


def local_rows(shape, member, bit, block):
    row = iota(shape, 0)
    own = (member >> bit) & 1
    return (row // block) * (2 * block) + own * block + row % block


def prep_kernel(
    coords, speeds, flags, scatter, loads, sigma, mass, spots, lists, live, obs, weight,
    mine, speed_out, par, plan, up, down, obs_out, weight_out,
    flags_s, floats_s, spots_s, lists_s, live_s, small_sem, sem, row_sem, *, thick, bit, half,
):
    own = (lax.axis_index("replica") >> bit) & 1
    block = obs.shape[3]
    small = [
        pltpu.make_async_copy(flags, flags_s.at[0], small_sem.at[0]),
        pltpu.make_async_copy(spots, spots_s, small_sem.at[1]),
        pltpu.make_async_copy(coords, mine.at[0], small_sem.at[6]),
        pltpu.make_async_copy(speeds, speed_out, small_sem.at[9]),
        pltpu.make_async_copy(lists, lists_s, small_sem.at[7]),
        pltpu.make_async_copy(live, live_s, small_sem.at[8]),
    ]
    for n, source in enumerate((scatter, loads, sigma, mass)):
        small.append(pltpu.make_async_copy(source, floats_s.at[n, 0], small_sem.at[2 + n]))
    for copy in small:
        copy.start()
    copies = []
    deals = half // block
    for target, first in ((up, thick - HALO), (down, 0)):
        for n, source in enumerate((obs, weight)):
            for plane in range(HALO):
                copies.append(
                    pltpu.make_async_copy(
                        source.at[first + plane, :, own],
                        target.at[pl.ds((n * HALO + plane) * deals, deals)],
                        sem.at[len(copies)],
                    )
                )
                copies[-1].start()
    for source, target in ((obs, obs_out), (weight, weight_out)):
        for q in range(deals):
            copies.append(
                pltpu.make_async_copy(
                    source.at[:, q, own],
                    target.at[:, pl.ds(q * block, block)],
                    row_sem.at[len(copies) - 4 * HALO],
                )
            )
            copies[-1].start()
    for copy in small:
        copy.wait()
    occupancy = flags_s[...].astype(F32)
    inv_var = 1.0 / (floats_s[2] * floats_s[2])
    charge = occupancy * floats_s[1]
    par[0:1] = occupancy * floats_s[0]
    par[1:2] = charge
    par[2:3] = inv_var
    par[3:4] = (-0.5 * math.log2(math.e)) * inv_var
    par[4:5] = floats_s[3]
    data = jnp.concatenate([mine[0, 0], mine[0, 1], mine[0, 2], charge], 0)
    high = data.astype(BF16)
    rest = data - high.astype(F32)
    mid = rest.astype(BF16)
    low = (rest - mid.astype(F32)).astype(BF16)
    pieces = jnp.concatenate([high.astype(F32), mid.astype(F32), low.astype(F32)], 0).astype(BF16)
    count = data.shape[1]
    cells, slots = lists_s.shape
    lane, row = iota((8, CELL), 1), iota((8, CELL), 0)
    used = jnp.zeros((8, CELL), jnp.int32)
    for c in range(cells):
        used = jnp.where(row == c, live_s[c], used)
    listed = jnp.concatenate([lists_s[...], jnp.zeros((8 - cells, slots), jnp.int32)], 0)
    picked = [jnp.zeros((8, CELL), jnp.int32)] * 2
    length = [jnp.zeros((8, CELL), jnp.int32)] * 2
    for s in range(slots):
        block_of = jnp.broadcast_to(listed[:, s : s + 1], (8, CELL))
        for kind in range(2):
            takes = (s < used) & ((block_of < cells) if kind == 0 else (block_of >= cells))
            picked[kind] = jnp.where(takes & (lane == length[kind]), block_of - kind * cells, picked[kind])
            length[kind] = length[kind] + takes.astype(jnp.int32)
    for kind in range(2):
        plan[kind] = jnp.where(lane == COUNT_AT, length[kind], picked[kind])
    for side, target in enumerate((up, down)):
        chosen = spots_s[side : side + 1, :]
        pick = (iota((count, chosen.shape[1]), 0) == chosen).astype(F32).astype(BF16)
        got = jnp.dot(pieces, pick, preferred_element_type=F32)
        got = got[0:4] + got[4:8] + got[8:12]
        groups = chosen.shape[1] // CELL
        for n in range(4):
            for g in range(groups):
                row = n * groups + g
                target[2 * HALO * deals, row : row + 1, :] = got[
                    n : n + 1, g * CELL : (g + 1) * CELL
                ]
    for copy in copies:
        copy.wait()


def ring_unit(period):
    unit = 2**32 // period
    assert unit * period == 2**32
    return unit


def spread_grids(half, depth, count, thick, bit, block):
    first = lax.axis_index("brick") * thick - HALO
    x_grid = (iota((16, count), 0) + first).astype(F32)
    y_grid = local_rows((half, count), lax.axis_index("replica"), bit, block) * ring_unit(2 * half)
    z_grid = iota((depth, count), 0) * ring_unit(depth)
    return x_grid, y_grid, z_grid


def member_bells(place, amp, rate, grids):
    x_grid, y_grid, z_grid = grids
    x_amp = amp * bell(x_grid, place[0], rate)
    y_val = ring_bell(y_grid, place[1], rate, ring_unit(2 * y_grid.shape[0]))
    z_val = ring_bell(z_grid, place[2], rate, ring_unit(z_grid.shape[0])).astype(BF16)
    return x_amp, y_val, z_val


def layers(left, x_amp, y_val, planes):
    half = y_val.shape[0]
    for n, i in enumerate(planes):
        left[n * half : (n + 1) * half, :] = (x_amp[i : i + 1] * y_val).astype(BF16)


def product(left, z_val, shape):
    return lax.dot_general(left[...], z_val, NT, preferred_element_type=F32).reshape(shape)


def early_kernel(*refs, thick, bit, block, unit, work):
    groups, refs = refs[:-14], refs[-14:]
    par, plan, tables, refs = refs[0], refs[1], refs[2:6], refs[6:]
    out, short, lefts, deeps, (plan_s, sem) = refs[0], refs[1], refs[2:4], refs[4:6], refs[6:]
    copy = pltpu.make_async_copy(plan, plan_s, sem)
    copy.start()
    planes, half, depth = out.shape
    count = par.shape[1]
    amp, rate = par[0:1], par[3:4]
    grids = spread_grids(half, depth, count, thick, bit, block)
    places = [(g, n) for g in groups for n in range(g.shape[0])]

    def build(m):
        g, n = places[m]
        x_amp, y_val, z_val = member_bells(g.at[n], amp, rate, grids)
        deeps[m % 2][...] = z_val
        layers(lefts[m % 2], x_amp, y_val, range(planes))

    build(0)
    for m in range(len(places)):
        if m + 1 < len(places):
            build(m + 1)
        got = product(lefts[m % 2], deeps[m % 2][...], out.shape)
        out[...] = got if m == 0 else out[...] + got
    copy.wait()
    pair_cells(groups[0], par, {0: tables}, plan_s, short, work, unit)


def rim_side(across, thick):
    odd = lax.axis_index("brick") % 2
    return thick * (odd if across else 1 - odd)


def rim_bells(base, place, amp, rate, thick):
    first = lax.axis_index("brick") * thick - HALO + base
    grid = (iota((8, amp.shape[1]), 0) + first).astype(F32)
    return amp * bell(grid, place[0], rate)


def across_kernel(late, par, total, out, packet, x_out, y_out, z_out, left_a, left_b, *, thick, bit, block):
    members = late.shape[0]
    _, half, depth = total.shape
    amp, rate = par[0:1], par[3:4]
    grids = spread_grids(half, depth, par.shape[1], thick, bit, block)
    lefts = (left_a, left_b)
    base = rim_side(True, thick)

    def build(m):
        x_amp, y_val, z_val = member_bells(late.at[m], amp, rate, grids)
        x_out[m], y_out[m], z_out[m] = x_amp, y_val, z_val
        layers(lefts[m % 2], rim_bells(base, late.at[m], amp, rate, thick), y_val, range(RIM))

    build(0)
    for m in range(members):
        if m + 1 < members:
            build(m + 1)
        got = product(lefts[m % 2], z_out[m], out.shape)
        out[...] = got + (total[pl.ds(base, RIM)] if m == 0 else out[...])
    packet[...] = out[...].astype(BF16)


def beside_kernel(late, par, total, y_in, z_in, out, packet, left_a, left_b, *, thick):
    members = late.shape[0]
    amp, rate = par[0:1], par[3:4]
    lefts = (left_a, left_b)
    base = rim_side(False, thick)

    def build(m):
        layers(lefts[m % 2], rim_bells(base, late.at[m], amp, rate, thick), y_in[m], range(RIM))

    build(0)
    for m in range(members):
        if m + 1 < members:
            build(m + 1)
        got = product(lefts[m % 2], z_in[m], out.shape)
        out[...] = got + (total[pl.ds(base, RIM)] if m == 0 else out[...])
    packet[...] = out[...].astype(BF16)


def enter(tables, n, x, y, z, q, unit):
    at = slice(n * CELL, (n + 1) * CELL)
    for table, row in zip(tables, (x * float(unit), fixed(y, unit), fixed(z, unit), q)):
        table[at, :] = jnp.broadcast_to(row, (CELL, CELL)).T


def ghost_kernel(low, high, *tables, n_x, ghosts, unit):
    slabs = lax.axis_size("brick")
    brick = lax.axis_index("brick")
    last = low.shape[0] - 1
    shift_low = jnp.where(brick == 0, -float(n_x), 0.0).astype(F32)
    shift_high = jnp.where(brick == slabs - 1, float(n_x), 0.0).astype(F32)
    for n, (ref, shift) in enumerate(((low, shift_low), (high, shift_high))):
        for g in range(ghosts):
            row = [ref[last, k * ghosts + g : k * ghosts + g + 1, :] for k in range(4)]
            enter(tables, n * ghosts + g, row[0] + shift, row[1], row[2], row[3], unit)


def own_kernel(mine, par, plan, *refs, unit, cells):
    tables, (out, plan_s, sem) = refs[:4], refs[4:]
    copy = pltpu.make_async_copy(plan, plan_s, sem)
    copy.start()
    for c in range(mine.shape[3] // CELL):
        at = slice(c * CELL, (c + 1) * CELL)
        place = [mine[0, k, :, at] for k in range(3)]
        enter(tables, c, *place, par[1:2, at], unit)
    copy.wait()
    pair_cells(mine, par, {0: tables}, plan_s, out, cells, unit)


COUNT_AT = 127


def pair_cells(mine, par, tables, plan, out, work, unit):
    one = float(unit)
    for n, (c, kinds) in enumerate(work):
        at = slice(c * CELL, (c + 1) * CELL)
        xi = jnp.broadcast_to(mine[0, 0, :, at] * one, (8, CELL))
        yi = jnp.broadcast_to(fixed(mine[0, 1, :, at], unit), (8, CELL))
        zi = jnp.broadcast_to(fixed(mine[0, 2, :, at], unit), (8, CELL))
        zero = jnp.zeros((8, CELL), F32)
        total = (zero, zero, zero)
        for kind in kinds:
            place_x, place_y, place_z, load = tables[kind]

            def slot(s, total):
                start = pl.multiple_of(plan[kind, c, s] * CELL, CELL)
                tx, ty, tz = total
                for g in range(CELL // 8):
                    here = pl.ds(start + g * 8, 8)
                    dx = xi - place_x[here, :]
                    dy = (yi - place_y[here, :]).astype(F32)
                    dz = (zi - place_z[here, :]).astype(F32)
                    dist = dx * dx + dy * dy + (dz * dz + softening * one * one)
                    inv = lax.rsqrt(dist)
                    w = load[here, :] * inv * (inv * inv)
                    tx, ty, tz = tx + w * dx, ty + w * dy, tz + w * dz
                return tx, ty, tz

            def two_slots(n, total):
                return slot(2 * n + 1, slot(2 * n, total))

            slots = plan[kind, c, COUNT_AT]
            total = lax.fori_loop(0, slots // 2, two_slots, total)
            total = lax.fori_loop(2 * (slots // 2), slots, slot, total)
        factor = (coupling * one * one) * par[1:2, at]
        here = slice(n * CELL, (n + 1) * CELL)
        for k in range(3):
            out[k : k + 1, here] = factor * jnp.sum(total[k], axis=0, keepdims=True)


def middle_kernel(
    late, x_in, y_in, z_in, total, mine, par, plan, obs, weight, *refs,
    thick, bit, block, members, unit, work,
):
    ghosts, (dev_out, grad, partner_out, short, left_a, left_b, plan_s, sem) = refs[:4], refs[4:]
    copy = pltpu.make_async_copy(plan, plan_s, sem)
    copy.start()
    planes = range(RIM, thick)
    lefts = (left_a, left_b)
    held = x_in.shape[0]
    half = total.shape[1]
    layers(left_a, x_in[0], y_in[0], planes)
    for m in range(held):
        if m + 1 < held:
            layers(lefts[(m + 1) % 2], x_in[m + 1], y_in[m + 1], planes)
        got = product(lefts[m % 2], z_in[m], dev_out.shape)
        dev_out[...] = got + (total[RIM:thick] if m == 0 else dev_out[...])
    for n, i in enumerate(planes):
        dev = dev_out[n] * (1.0 / members) - obs[i - HALO]
        dev_out[n] = dev
        grad[n * half : (n + 1) * half, :] = (restraint * weight[i - HALO] * dev).astype(BF16)
    member_force(
        late.at[0], par, grad, partner_out,
        planes=planes, half=half, thick=thick, bit=bit, block=block,
    )
    copy.wait()
    pair_cells(mine, par, {1: ghosts}, plan_s, short, work, unit)


def member_force(place, par, grad, out, *, planes, half, thick, bit, block, plus=None):
    count = par.shape[1]
    depth = grad.shape[1]
    x_grid, y_grid, z_grid = spread_grids(half, depth, CELL, thick, bit, block)
    for t in range(count // CELL):
        at = slice(t * CELL, (t + 1) * CELL)
        inv_var, rate = par[2:3, at], par[3:4, at]
        x_val, x_der = bell_slope(x_grid, place[0, :, at], inv_var, rate)
        y_val, y_der = ring_bell_slope(y_grid, place[1, :, at], inv_var, rate, ring_unit(2 * half))
        z_val, z_der = ring_bell_slope(z_grid, place[2, :, at], inv_var, rate, ring_unit(depth))
        z_pair = jnp.concatenate([z_val, z_der], 1).astype(BF16)
        got = jnp.dot(grad[...], z_pair, preferred_element_type=F32)
        sums = [jnp.zeros((8, CELL), F32) for _ in range(3)]
        for n, i in enumerate(planes):
            part = [jnp.zeros((8, CELL), F32) for _ in range(3)]
            for g in range(half // 8):
                j = slice(g * 8, (g + 1) * 8)
                k = slice(n * half + g * 8, n * half + (g + 1) * 8)
                along, across = got[k, :CELL], got[k, CELL:]
                part[0] += y_val[j] * along
                part[1] += y_der[j] * along
                part[2] += y_val[j] * across
            sums[0] += x_der[i : i + 1] * part[0]
            sums[1] += x_val[i : i + 1] * part[1]
            sums[2] += x_val[i : i + 1] * part[2]
        for k in range(3):
            force = -par[0:1, at] * jnp.sum(sums[k], axis=0, keepdims=True)
            out[k : k + 1, at] = force if plus is None else force + plus[k : k + 1, at]


def grad_kernel(
    late, par, sent_y, got_y, sent_c, got_c, dev_middle, grad_middle, partner_middle,
    near_low, near_high, obs, weight,
    dev_out, grad, partner_out, grad_rim, dev_s, *, thick, bit, share, block, members,
):
    _, half, _ = dev_middle.shape
    deals = near_low.shape[0] // (2 * HALO)
    member = lax.axis_index("replica")

    def near_rows(ref, n, plane):
        at = (n * HALO + plane) * deals
        return jnp.concatenate([ref[at + q] for q in range(deals)], 0)

    even = lax.axis_index("brick") % 2 == 0
    rims = [*range(RIM), *range(thick, thick + RIM)]
    for at, i in enumerate(rims):
        low, n = i < RIM, at % RIM
        across = sent_y[n] + got_y[n].astype(F32)
        beside = sent_c[n] + got_c[n].astype(F32)
        summed = jnp.where(even == low, across, beside)
        if i < HALO:
            wanted, trust = near_rows(near_low, 0, i), near_rows(near_low, 1, i)
        elif i >= thick + HALO:
            beyond = i - thick - HALO
            wanted, trust = near_rows(near_high, 0, beyond), near_rows(near_high, 1, beyond)
        else:
            wanted, trust = obs[i - HALO], weight[i - HALO]
        dev = summed * (1.0 / members) - wanted
        slope = (restraint * trust * dev).astype(BF16)
        grad_rim[at * half : (at + 1) * half, :] = slope
        grad[i * half : (i + 1) * half, :] = slope
        if HALO <= i < thick + HALO:
            dev_s[i - HALO] = dev
    grad[RIM * half : thick * half, :] = grad_middle[...]
    dev_s[RIM - HALO : thick - HALO] = dev_middle[...]
    first_row = member * share
    spot = (first_row // (2 * block)) * block + first_row % block
    for n in range(half // share):

        @pl.when(spot == n * share)
        def _(n=n):
            dev_out[...] = dev_s[:, n * share : (n + 1) * share, :]

    member_force(
        late.at[0], par, grad_rim, partner_out,
        planes=rims, half=half, thick=thick, bit=bit, block=block, plus=partner_middle,
    )


def force_kernel(
    grad, deviation, mine, par, plan, *refs, thick, bit, block, unit, work
):
    own, ghosts, refs = refs[:4], refs[4:8], refs[8:]
    dev_out, out, short, plan_s, sem, dev_sem = refs
    copies = [
        pltpu.make_async_copy(plan, plan_s, sem),
        pltpu.make_async_copy(deviation, dev_out, dev_sem),
    ]
    for copy in copies:
        copy.start()
    planes = range(thick + 2 * HALO)
    half = grad.shape[0] // len(planes)
    member_force(
        mine.at[0], par, grad, out, planes=planes, half=half, thick=thick, bit=bit, block=block
    )
    copies[0].wait()
    pair_cells(mine, par, {0: own, 1: ghosts}, plan_s, short, work, unit)
    copies[1].wait()


def kick_kernel(own, other, *refs, works):
    given, (par, speed, v_half, part) = refs[:-4], refs[-4:]
    mass = par[4:5]
    energy = jnp.zeros_like(mass)
    for k in range(3):
        shorts = {}
        for short, work in zip(given, works):
            for n, (c, _) in enumerate(work):
                term = short[k : k + 1, n * CELL : (n + 1) * CELL]
                shorts[c] = shorts[c] + term if c in shorts else term
        short = jnp.concatenate([shorts[c] for c in sorted(shorts)], 1)
        force = own[k : k + 1] + other[k : k + 1] + short
        v = speed[k] + timestep * force / mass
        v_half[k : k + 1] = v
        energy = energy + mass * v * v
    part[...] = jnp.broadcast_to(jnp.sum(energy, axis=1, keepdims=True), part.shape)


def drift_kernel(*refs, freedom):
    parts, (v_half, coords, warmth, place_out, speed_out) = refs[:-5], refs[-5:]
    kinetic = parts[0][0:1]
    for part in parts[1:]:
        kinetic = kinetic + part[0:1]
    present_moment = kinetic / (freedom * boltzmann) + 1e-06
    ratio = jnp.sqrt(
        1.0 + heat_bath_damping * (warmth[0].astype(F32) / present_moment - 1.0)
    )
    ratio = jnp.concatenate([ratio] * (v_half.shape[1] // ratio.shape[1]), 1)
    for k in range(3):
        v = ratio * v_half[k : k + 1]
        speed_out[k] = v
        place_out[k] = coords[0, k] + timestep * v


def local(
    atom_locations,
    atom_speeds_vector,
    inertial_amounts,
    electric_loads,
    scatter_strengths,
    gaussian_spreads_sigma,
    atom_present_flags,
    observed_volume_values,
    voxel_reciprocal_spread,
    paired_partner_lists,
    cell_usage_tally,
    halo_sender_spots,
    target_warmth_levels,
):
    thick, rows, depth = observed_volume_values.shape
    slabs = lax.axis_size("brick")
    members = lax.axis_size("replica")
    n_x = thick * slabs
    coords = jnp.transpose(atom_locations, (1, 0, 2))
    speeds = jnp.transpose(atom_speeds_vector, (1, 0, 2))
    count = coords.shape[2]
    planes = thick + 2 * HALO
    share, bit, block = row_class(rows, members)
    half = rows // 2
    deals = half // block
    ghosts = halo_sender_spots.shape[1]
    assert 4 * ghosts // CELL <= block
    assert slabs >= 4 and slabs % 2 == 0 and thick >= RIM and count // CELL <= 8

    bits = [1 << n for n in range(members.bit_length() - 1) if n != bit][::-1]

    def hop(known, mask):
        return lax.ppermute(known, "replica", [(i, i ^ mask) for i in range(members)])

    first = hop(coords[None], bits[0])
    obs = in_hbm(observed_volume_values.reshape(thick, deals, 2, block, depth))
    weight = in_hbm(voxel_reciprocal_spread.reshape(thick, deals, 2, block, depth))
    near = jax.ShapeDtypeStruct((2 * HALO * deals + 1, block, CELL), F32)
    own_rows = jax.ShapeDtypeStruct((thick, half, depth), F32)
    mine, speed, par, plan, near_up, near_down, own_obs, own_weight = pl.pallas_call(
        functools.partial(prep_kernel, thick=thick, bit=bit, half=half),
        out_shape=(
            jax.ShapeDtypeStruct((1,) + coords.shape, F32),
            jax.ShapeDtypeStruct(speeds.shape, F32),
            jax.ShapeDtypeStruct((8, count), F32),
            jax.ShapeDtypeStruct((2, 8, CELL), jnp.int32),
            near,
            near,
            own_rows,
            own_rows,
        ),
        in_specs=[HBM] * 12,
        out_specs=(VMEM,) * 8,
        scratch_shapes=[
            pltpu.VMEM((1, count), jnp.int32),
            pltpu.VMEM((4, 1, count), F32),
            pltpu.VMEM((2, ghosts), jnp.int32),
            pltpu.VMEM(paired_partner_lists.shape, jnp.int32),
            pltpu.SMEM(cell_usage_tally.shape, jnp.int32),
            pltpu.SemaphoreType.DMA((10,)),
            pltpu.SemaphoreType.DMA((4 * HALO,)),
            pltpu.SemaphoreType.DMA((2 * deals,)),
        ],
        compiler_params=limit(4),
        cost_estimate=cost(1),
        name="prep",
    )(
        *(
            in_hbm(a)
            for a in (
                coords,
                speeds,
                atom_present_flags,
                scatter_strengths,
                electric_loads,
                gaussian_spreads_sigma,
                inertial_amounts,
                halo_sender_spots,
                paired_partner_lists,
                cell_usage_tally,
            )
        ),
        obs,
        weight,
    )
    groups = [mine, first]
    for mask in bits[1:]:
        groups.append(hop(jnp.concatenate(groups), mask))
    late = hop(jnp.concatenate(groups), 1 << bit)

    ring = [(i, (i + 1) % slabs) for i in range(slabs)]
    back = [(target, source) for source, target in ring]
    near_low = lax.ppermute(near_up, "brick", ring)
    near_high = lax.ppermute(near_down, "brick", back)

    cells = count // CELL
    unit = ring_unit(rows)
    assert rows == depth and members & (members - 1) == 0
    first_cells = 2 * cells // 3
    works = (
        [(c, [0]) for c in range(first_cells)],
        [(c, [1]) for c in range(first_cells)],
        [(c, [0, 1] if c > first_cells else [1]) for c in range(first_cells, cells)],
        [(first_cells, [0])],
    )

    def shorts(work):
        return jax.ShapeDtypeStruct((3, len(work) * CELL), F32)

    def tables(blocks):
        table = jax.ShapeDtypeStruct((blocks * CELL, CELL), F32)
        table_int = jax.ShapeDtypeStruct((blocks * CELL, CELL), jnp.int32)
        return table, table_int, table_int, table

    planned = [pltpu.SMEM(plan.shape, jnp.int32), pltpu.SemaphoreType.DMA]
    *own_tables, short_own = pl.pallas_call(
        functools.partial(own_kernel, unit=unit, cells=works[0]),
        out_shape=(*tables(cells), shorts(works[0])),
        in_specs=[VMEM] * 3,
        out_specs=(VMEM,) * 5,
        scratch_shapes=planned,
        compiler_params=limit(6),
        cost_estimate=cost(2),
        name="own_pairs",
    )(mine, par, plan)
    ghost_tables = pl.pallas_call(
        functools.partial(ghost_kernel, n_x=n_x, ghosts=ghosts // CELL, unit=unit),
        out_shape=tables(2 * ghosts // CELL),
        in_specs=[VMEM] * 2,
        out_specs=(VMEM,) * 4,
        compiler_params=limit(6),
        cost_estimate=cost(1),
        name="ghosts",
    )(near_low, near_high)

    place = dict(thick=thick, bit=bit, block=block)
    total, short_more = pl.pallas_call(
        functools.partial(early_kernel, **place, unit=unit, work=works[3]),
        out_shape=(jax.ShapeDtypeStruct((planes, half, depth), F32), shorts(works[3])),
        in_specs=[VMEM] * (len(groups) + 6),
        out_specs=(VMEM, VMEM),
        scratch_shapes=[pltpu.VMEM((planes * half, count), BF16)] * 2
        + [pltpu.VMEM((depth, count), BF16)] * 2
        + planned,
        compiler_params=limit(12),
        cost_estimate=cost(2),
        name="early",
    )(*groups, par, plan, *own_tables)
    held = late.shape[0]
    rim = jax.ShapeDtypeStruct((RIM, half, depth), F32)
    packet = jax.ShapeDtypeStruct((RIM, half, depth), BF16)
    sent_y, packet_y, x_late, y_late, z_late = pl.pallas_call(
        functools.partial(across_kernel, **place),
        out_shape=(
            rim,
            packet,
            jax.ShapeDtypeStruct((held, 16, count), F32),
            jax.ShapeDtypeStruct((held, half, count), F32),
            jax.ShapeDtypeStruct((held, depth, count), BF16),
        ),
        in_specs=[VMEM] * 3,
        out_specs=(VMEM,) * 5,
        scratch_shapes=[pltpu.VMEM((RIM * half, count), BF16)] * 2,
        compiler_params=limit(12),
        cost_estimate=cost(1),
        name="across",
    )(late, par, total)
    route = [(i, (i + 1 if i % 2 else i - 1) % slabs) for i in range(slabs)]
    got_y = lax.ppermute(packet_y, "brick", route)
    sent_c, packet_c = pl.pallas_call(
        functools.partial(beside_kernel, thick=thick),
        out_shape=(rim, packet),
        in_specs=[VMEM] * 5,
        out_specs=(VMEM, VMEM),
        scratch_shapes=[pltpu.VMEM((RIM * half, count), BF16)] * 2,
        compiler_params=limit(12),
        cost_estimate=cost(1),
        name="beside",
    )(late, par, total, y_late, z_late)
    got_c = lax.ppermute(packet_c, "brick", [(i, i ^ 1) for i in range(slabs)])
    force = jax.ShapeDtypeStruct((3, count), F32)
    inner = thick - RIM
    dev_middle, grad_middle, partner_middle, short_a = pl.pallas_call(
        functools.partial(middle_kernel, **place, members=members, unit=unit, work=works[1]),
        out_shape=(
            jax.ShapeDtypeStruct((inner, half, depth), F32),
            jax.ShapeDtypeStruct((inner * half, depth), BF16),
            force,
            shorts(works[1]),
        ),
        in_specs=[VMEM] * 14,
        out_specs=(VMEM,) * 4,
        scratch_shapes=[pltpu.VMEM((inner * half, count), BF16)] * 2 + planned,
        compiler_params=limit(12),
        cost_estimate=cost(2),
        name="middle",
    )(late, x_late, y_late, z_late, total, mine, par, plan, own_obs, own_weight, *ghost_tables)
    deviation, grad, partner = pl.pallas_call(
        functools.partial(grad_kernel, **place, share=share, members=members),
        out_shape=(
            jax.ShapeDtypeStruct((thick, share, depth), F32),
            jax.ShapeDtypeStruct((planes * half, depth), BF16),
            force,
        ),
        in_specs=[VMEM] * 13,
        out_specs=(VMEM, VMEM, VMEM),
        scratch_shapes=[
            pltpu.VMEM((2 * RIM * half, depth), BF16),
            pltpu.VMEM((thick, half, depth), F32),
        ],
        compiler_params=limit(12),
        cost_estimate=cost(1),
        name="grad",
    )(
        late, par, sent_y, got_y, sent_c, got_c, dev_middle, grad_middle, partner_middle,
        near_low, near_high, own_obs, own_weight,
    )

    swap = [(i, i ^ (1 << bit)) for i in range(members)]
    other = lax.ppermute(partner, "replica", swap)
    deviation, own, short_b = pl.pallas_call(
        functools.partial(force_kernel, **place, unit=unit, work=works[2]),
        out_shape=(
            jax.ShapeDtypeStruct(deviation.shape, F32),
            force,
            shorts(works[2]),
        ),
        in_specs=[VMEM] * 13,
        out_specs=(HBM, VMEM, VMEM),
        scratch_shapes=planned + [pltpu.SemaphoreType.DMA],
        compiler_params=limit(8),
        cost_estimate=cost(2),
        name="force",
    )(grad, deviation, mine, par, plan, *own_tables, *ghost_tables)
    v_half, part = pl.pallas_call(
        functools.partial(kick_kernel, works=works),
        out_shape=(force, jax.ShapeDtypeStruct((8, CELL), F32)),
        in_specs=[VMEM] * 8,
        out_specs=(VMEM, VMEM),
        compiler_params=limit(2),
        name="kick",
    )(own, other, short_own, short_a, short_b, short_more, par, speed)
    if slabs == 4:
        parts = [part]
        for mask in (2, 3, 1):
            parts.append(lax.ppermute(part, "brick", [(i, i ^ mask) for i in range(slabs)]))
    else:
        parts = [lax.psum(part, "brick")]
    moved = jax.ShapeDtypeStruct((3, 1, count), F32)
    new_positions, new_velocities = pl.pallas_call(
        functools.partial(drift_kernel, freedom=3 * count * slabs),
        out_shape=(moved, moved),
        in_specs=[VMEM] * (len(parts) + 2) + [SMEM],
        out_specs=(VMEM, VMEM),
        compiler_params=limit(2),
        name="drift",
    )(*parts, v_half, mine, target_warmth_levels)
    return (
        jnp.transpose(new_positions, (1, 0, 2)),
        jnp.transpose(new_velocities, (1, 0, 2)),
        deviation,
    )


def solution(mesh):
    return jax.shard_map(
        local,
        mesh=mesh,
        in_specs=(
            P("replica", None, "brick"),
            P("replica", None, "brick"),
            P("brick"),
            P("brick"),
            P("brick"),
            P("brick"),
            P("brick"),
            P("brick", None, None),
            P("brick", None, None),
            P("brick", None),
            P("brick"),
            P(None, "brick"),
            P("replica"),
        ),
        out_specs=(
            P("replica", None, "brick"),
            P("replica", None, "brick"),
            P("brick", "replica", None),
        ),
        check_vma=False,
    )
```
